32 devices in a mesh: tok: 16 (over z, x, core), head: 2 (over y).
Axes of the slice: x: 2, y: 2, z: 4, core: 2. Of those that a mesh axis runs over, the one named last changes fastest.
Arguments:
- queries: bfloat16 [1024, 4096], P('tok', 'head'), may hold values from -6 to 6
- keys: bfloat16 [8192, 1024], P('tok', 'head'), may hold values from -256 to 256
- values: bfloat16 [8192, 1024], P('tok', 'head'), may hold values from -6 to 6
- out_weight: bfloat16 [4096, 4096], P('head'), may hold values from -0.59765625 to 0.59765625
- task_slot: int32 [8, 8, 16], P('head'), may hold values from -1 to 7, as said below
- task_count: int32 [8, 16], P('head'), may hold values from 1 to 8, as said below
Outputs:
- projected: bfloat16 [1024, 4096], P('tok', 'head')
The draws below stay inside these ranges and needn't reach their ends.
Inputs may be any that keep to these rules, and one draw needn't show every extreme that they name: For each key head h and key block c, the entries task_slot[h, b, c] that are not -1 take each of the values 0 to task_count[h, c] - 1 exactly once. Key blocks 0 and 15 are attended by every query block under every key head. task_count[h, c] is the number of query blocks that attend key block c under key head h.
All inputs are finite; a program needn't handle non-finite values.
Results may differ from the reference program's by a relative error of at most 0.015.
Values may be sent and summed in bfloat16 or wider, within the bound.
No kernel may reach another device: no remote copies, remote signals or barrier semaphores. Data moves between devices by JAX's collectives and lax.ppermute only.
A program may use at most 64 MiB of HBM per device.

```python
import functools
import jax
import jax.numpy as jnp
from jax import lax

D = 4096
HEADS = 32
KVH = 8
HEAD_SIZE = 128
QBLK = 128
KBLK = 512
QTOK = 1024
QB = 8
KB = 16
KEYS = 8192


def query_values(key):
    base_key = jax.random.fold_in(key, 11)
    return jnp.clip(jax.random.normal(jax.random.fold_in(base_key, 3), (QTOK, HEADS * HEAD_SIZE), jnp.float32), -6.0, 6.0)


def draw_queries(key, part):
    return query_values(key).astype(jnp.bfloat16)


def draw_keys(key, part):
    base_key = jax.random.fold_in(key, 23)
    key_field = 2.0 * jnp.clip(jax.random.normal(jax.random.fold_in(base_key, 1), (KEYS, KVH * HEAD_SIZE), jnp.float32), -6.0, 6.0)
    return key_field.astype(jnp.bfloat16)


def task_tables(key):
    base_key = jax.random.fold_in(key, 37)
    count_limit = 3 * QB // 4 + 1
    counts = jax.random.randint(jax.random.fold_in(base_key, 1), (KVH, KB), 1, count_limit, dtype=jnp.int32)
    counts = counts.at[:, 0].set(QB).at[:, KB - 1].set(QB)
    order_keys = jax.random.split(jax.random.fold_in(base_key, 2), KVH * KB)
    orders = jax.vmap(lambda order_key: jax.random.permutation(order_key, QB))(order_keys).astype(jnp.int32)
    orders = jnp.transpose(orders.reshape(KVH, KB, QB), (0, 2, 1))
    slots = jnp.where(orders < counts[:, None, :], orders, -1).astype(jnp.int32)
    return (slots, counts.astype(jnp.int32))


def draw_task_slot(key, part):
    return task_tables(key)[0]


def draw_task_count(key, part):
    return task_tables(key)[1]


def block_scale(own_key, dims, cuts, least, top_value):
    level = 1.0
    for axis_at, blocks in cuts:
        steps = jax.random.uniform(jax.random.fold_in(jax.random.fold_in(own_key, 6), axis_at), (blocks,), jnp.float32, least / len(cuts), top_value / len(cuts))
        level = level * jnp.repeat(jnp.exp(steps), dims[axis_at] // blocks).reshape((-1,) + (1,) * (len(dims) - 1 - axis_at))
    return level


def gaussian(rng, shape, scale, reach, shards=(), kind=jnp.bfloat16):
    drawn = scale * jax.random.normal(rng, shape, jnp.float32)
    if shards:
        drawn = drawn * block_scale(rng, shape, shards, -0.22, 0.18)
    return jnp.clip(drawn, -reach, reach).astype(kind)


def setup_inputs(seed: int = 0) -> dict:
    streams_of = jax.random.split(jax.random.key(seed), 7)
    return {
        "queries": draw_queries(jax.random.fold_in(streams_of[6], 71), 0),
        "keys": draw_keys(jax.random.fold_in(streams_of[6], 71), 0),
        "values": gaussian(streams_of[2], (KEYS, KVH * HEAD_SIZE), 1.0, 6.0, ((0, 16), (1, 2))),
        "out_weight": gaussian(streams_of[3], (HEADS * HEAD_SIZE, D), 0.1, 0.59765625, ((0, 2),)),
        "task_slot": draw_task_slot(jax.random.fold_in(streams_of[6], 71), 0),
        "task_count": draw_task_count(jax.random.fold_in(streams_of[6], 71), 0),
    }


theta_base = 500000.0
neg_fill = -1.0e30


def rotate(block_rows, first_row):
    head_width = block_rows.shape[-1]
    half_width = head_width // 2
    frequency = theta_base ** (-(jnp.arange(half_width, dtype=jnp.float32) * (2.0 / head_width)))
    places = (first_row + jnp.arange(block_rows.shape[0], dtype=jnp.int32)).astype(jnp.float32)
    angles = places[:, None] * frequency[None, :]
    cosine = jnp.cos(angles)[:, None, :]
    sine_table = jnp.sin(angles)[:, None, :]
    first_half = block_rows[..., :half_width]
    second_half = block_rows[..., half_width:]
    return jnp.concatenate([first_half * cosine - second_half * sine_table, second_half * cosine + first_half * sine_table], axis=-1)


def attend_block(block_id, rotated, head_keys_matrix, head_values_matrix, slots, limits, head_kv):
    group_size = HEADS // KVH
    block_id = block_id.astype(jnp.int32)
    row_start = (block_id * QBLK).astype(jnp.int32)
    head_start = jnp.asarray(head_kv * group_size).astype(jnp.int32)
    zero_start = jnp.asarray(0).astype(jnp.int32)
    query_row_block = lax.dynamic_slice(rotated, (row_start, head_start, zero_start), (QBLK, group_size, HEAD_SIZE)).astype(jnp.float32)
    row_slots = lax.dynamic_index_in_dim(slots, block_id, 0, keepdims=False)
    active = (row_slots >= 0) & (row_slots < limits)
    attention_logits = jnp.einsum("zxv,lsv->xzls", query_row_block, head_keys_matrix) * (HEAD_SIZE ** -0.5)
    maxima = jnp.max(attention_logits, axis=-1)
    probabilities = jnp.exp(attention_logits - maxima[..., None])
    totals = jnp.sum(probabilities, axis=-1)
    rounded_scores = lax.optimization_barrier(probabilities.astype(jnp.bfloat16)).astype(jnp.float32)
    weighted_value_sum = jnp.einsum("hlpf,pfu->lhpu", rounded_scores, head_values_matrix)
    normed = (weighted_value_sum / jnp.transpose(totals, (1, 0, 2))[..., None]).astype(jnp.bfloat16)
    normed = lax.optimization_barrier(normed).astype(jnp.float32)
    logsum = jnp.transpose(maxima + jnp.log(totals), (1, 0, 2))
    logsum = jnp.where(active[None, None, :], logsum, neg_fill)
    largest = jnp.max(logsum, axis=-1, keepdims=True)
    weights = jnp.exp(logsum - largest)
    numerator = jnp.einsum("qgb,qgbd->qgd", weights, normed)
    return (numerator / jnp.sum(weights, axis=-1)[..., None]).astype(jnp.bfloat16)


def reference(queries, keys, values, out_weight, task_slot, task_count):
    group_size = HEADS // KVH
    shaped = queries.astype(jnp.float32).reshape(QTOK, HEADS, HEAD_SIZE)
    rotated = rotate(shaped, 0).astype(jnp.bfloat16)
    pieces = []
    for head_kv in range(KVH):
        head_keys_matrix = keys[:, head_kv * HEAD_SIZE:(head_kv + 1) * HEAD_SIZE].astype(jnp.float32).reshape(KB, KBLK, HEAD_SIZE)
        head_values_matrix = values[:, head_kv * HEAD_SIZE:(head_kv + 1) * HEAD_SIZE].astype(jnp.float32).reshape(KB, KBLK, HEAD_SIZE)
        worker = functools.partial(attend_block, rotated=rotated, head_keys_matrix=head_keys_matrix, head_values_matrix=head_values_matrix, slots=task_slot[head_kv], limits=task_count[head_kv], head_kv=head_kv)
        results = lax.map(worker, jnp.arange(QB, dtype=jnp.int32))
        pieces.append(results.reshape(QTOK, group_size * HEAD_SIZE))
    attention = jnp.concatenate(pieces, axis=1)
    return jnp.dot(attention, out_weight, preferred_element_type=jnp.float32).astype(jnp.bfloat16)
```

```python
import functools
import math

import jax
import jax.numpy as jnp
from jax import lax
from jax.experimental import pallas as pl
from jax.experimental.pallas import tpu as pltpu
from jax.sharding import PartitionSpec as P

HEADS = 32
KVH = 8
HEAD_SIZE = 128
QBLK = 128

theta_base = 500000.0
neg_fill = -1e30
LOG2E = math.log2(math.e)
STAT_ROWS = 8


def rotary_tables(rows, first_row):
    half = HEAD_SIZE // 2
    frequency = theta_base ** (-(jnp.arange(half, dtype=jnp.float32) * (2.0 / HEAD_SIZE)))
    places = (first_row + jnp.arange(rows, dtype=jnp.int32)).astype(jnp.float32)
    angles = places[:, None] * frequency[None, :]
    cosine = jnp.cos(angles)
    sine = jnp.sin(angles)
    return (
        jnp.concatenate([cosine, cosine], axis=1),
        jnp.concatenate([-sine, sine], axis=1),
    )


def pack_queries_kernel(group, q_per_kv, cos_ref, sin_ref, q_ref, *out_refs):
    own = lax.rem(lax.axis_index("tok"), group)
    rows = q_ref.shape[0]
    cosine = cos_ref[...]
    sine = sin_ref[...]
    for offset in range(group):
        head = own ^ offset
        for j in range(q_per_kv):
            start = pl.multiple_of((head * q_per_kv + j) * HEAD_SIZE, HEAD_SIZE)
            x = q_ref[:, pl.ds(start, HEAD_SIZE)].astype(jnp.float32)
            turned = pltpu.roll(x, HEAD_SIZE // 2, 1)
            out_refs[offset][j * rows : (j + 1) * rows, :] = (
                x * cosine + turned * sine
            ).astype(jnp.bfloat16)


def pack_queries(queries, group, q_per_kv, first_row):
    rows = queries.shape[0]
    cosine, sine = rotary_tables(rows, first_row)
    piece = jax.ShapeDtypeStruct((q_per_kv * rows, HEAD_SIZE), jnp.bfloat16)
    return pl.pallas_call(
        functools.partial(pack_queries_kernel, group, q_per_kv),
        out_shape=[piece] * group,
        name="pack_queries",
        cost_estimate=pl.CostEstimate(
            flops=6 * queries.size, bytes_accessed=4 * queries.size, transcendentals=0
        ),
        compiler_params=pltpu.CompilerParams(vmem_limit_bytes=8 << 20),
    )(cosine, sine, queries)


def pack_cache_kernel(group, k_ref, v_ref, *out_refs):
    own = lax.rem(lax.axis_index("tok"), group)
    keys = k_ref.shape[0]
    for offset in range(group):
        start = pl.multiple_of((own ^ offset) * HEAD_SIZE, HEAD_SIZE)
        out_refs[offset][:keys, :] = k_ref[:, pl.ds(start, HEAD_SIZE)]
        out_refs[offset][keys:, :] = v_ref[:, pl.ds(start, HEAD_SIZE)]


def pack_cache(keys, values, group):
    piece = jax.ShapeDtypeStruct((2 * keys.shape[0], HEAD_SIZE), jnp.bfloat16)
    return pl.pallas_call(
        functools.partial(pack_cache_kernel, group),
        out_shape=[piece] * group,
        name="pack_cache",
        cost_estimate=pl.CostEstimate(
            flops=0, bytes_accessed=8 * keys.size, transcendentals=0
        ),
        compiler_params=pltpu.CompilerParams(vmem_limit_bytes=16 << 20),
    )(keys, values)


def split_stat(stat, width):
    high = stat.astype(jnp.bfloat16).astype(jnp.float32)
    rest = stat - high
    middle = rest.astype(jnp.bfloat16).astype(jnp.float32)
    low = rest - middle
    row = lax.broadcasted_iota(jnp.int32, (STAT_ROWS, width), 0)
    spread = jnp.where(row == 0, high, jnp.where(row == 1, middle, jnp.where(row == 2, low, 0.0)))
    return spread.astype(jnp.bfloat16)


def join_stat(ref):
    stat = ref[HEAD_SIZE : HEAD_SIZE + STAT_ROWS, :].astype(jnp.float32)
    return stat[0:1] + stat[1:2] + stat[2:3]


def attention_kernel(plan, slot_ref, count_ref, *refs):
    group, displacements, rows_dev, slab = plan
    n_chunks = len(displacements)
    q_refs = refs[:n_chunks]
    kv_refs = refs[n_chunks : n_chunks + group]
    out_refs = refs[n_chunks + group : 2 * n_chunks + group]
    m_ref, l_ref, acc_ref = refs[2 * n_chunks + group :]
    server = lax.axis_index("tok")
    head = lax.rem(server, group)
    keys = kv_refs[0].shape[0] // 2
    scale = HEAD_SIZE ** (-0.5) * LOG2E
    for i in range(n_chunks):
        width = q_refs[i].shape[0]
        block = ((server ^ displacements[i]) * rows_dev) // QBLK
        m_ref[...] = jnp.full_like(m_ref, neg_fill)
        l_ref[...] = jnp.zeros_like(l_ref)
        acc_ref[...] = jnp.zeros_like(acc_ref)
        for k in range(group):
            key_block = server ^ k
            slot = slot_ref[head, block, key_block]
            active = (slot >= 0) & (slot < count_ref[head, key_block])

            @pl.when(active)
            def _(i=i, k=k, width=width):
                for c in range(0, width, slab):
                    scores = lax.dot_general(
                        kv_refs[k][:keys, :],
                        q_refs[i][c : c + slab, :],
                        (((1,), (1,)), ((), ())),
                        preferred_element_type=jnp.float32,
                    )
                    m_old = m_ref[0:1, c : c + slab]
                    m_new = jnp.maximum(m_old, jnp.max(scores, axis=0, keepdims=True))
                    p = jnp.exp2((scores - m_new) * scale)
                    fade = jnp.exp2((m_old - m_new) * scale)
                    l_ref[0:1, c : c + slab] = fade * l_ref[0:1, c : c + slab] + jnp.sum(
                        p, axis=0, keepdims=True
                    )
                    m_ref[0:1, c : c + slab] = m_new
                    acc_ref[:, c : c + slab] = fade * acc_ref[:, c : c + slab] + lax.dot_general(
                        kv_refs[k][keys:, :],
                        p.astype(jnp.bfloat16),
                        (((0,), (0,)), ((), ())),
                        preferred_element_type=jnp.float32,
                    )

        total = l_ref[0:1, :]
        seen = total > 0.0
        inverse = 1.0 / jnp.where(seen, total, 1.0)
        stat = jnp.where(seen, m_ref[0:1, :] * scale + jnp.log2(jnp.where(seen, total, 1.0)), neg_fill)
        out_refs[i][:HEAD_SIZE, :] = (acc_ref[...] * inverse).astype(jnp.bfloat16)
        out_refs[i][HEAD_SIZE:, :] = split_stat(stat, width)


def attention(chunks, displacements, caches, task_slot, task_count, rows_dev):
    group = len(caches)
    width = chunks[0].shape[0]
    n = len(chunks)
    keys = caches[0].shape[0] // 2
    vmem = pl.BlockSpec(memory_space=pltpu.VMEM)
    smem = pl.BlockSpec(memory_space=pltpu.SMEM)
    out = jax.ShapeDtypeStruct((HEAD_SIZE + STAT_ROWS, width), jnp.bfloat16)
    return pl.pallas_call(
        functools.partial(attention_kernel, (group, tuple(displacements), rows_dev, min(256, width))),
        out_shape=[out] * n,
        in_specs=[smem, smem] + [vmem] * (n + group),
        out_specs=[vmem] * n,
        scratch_shapes=[
            pltpu.VMEM((8, width), jnp.float32),
            pltpu.VMEM((8, width), jnp.float32),
            pltpu.VMEM((HEAD_SIZE, width), jnp.float32),
        ],
        name="attention",
        cost_estimate=pl.CostEstimate(
            flops=4 * n * group * keys * width * HEAD_SIZE,
            bytes_accessed=4 * n * width * HEAD_SIZE + 4 * group * keys * HEAD_SIZE,
            transcendentals=n * group * keys * width,
        ),
        compiler_params=pltpu.CompilerParams(vmem_limit_bytes=24 << 20),
    )(task_slot, task_count, *chunks, *caches)


def merged(refs):
    stats = [join_stat(ref) for ref in refs]
    largest = functools.reduce(jnp.maximum, stats)
    weights = [jnp.exp2(stat - largest) for stat in stats]
    total = functools.reduce(jnp.add, weights)
    inverse = 1.0 / total
    value = functools.reduce(
        jnp.add,
        [
            (weight * inverse) * ref[:HEAD_SIZE, :].astype(jnp.float32)
            for weight, ref in zip(weights, refs)
        ],
    )
    return value, largest + jnp.log2(total)


def merge_kernel(*refs):
    *in_refs, out_ref = refs
    value, stat = merged(in_refs)
    out_ref[:HEAD_SIZE, :] = value.astype(jnp.bfloat16)
    out_ref[HEAD_SIZE:, :] = split_stat(stat, out_ref.shape[1])


def finish_kernel(n_in, *refs):
    in_refs, out_refs = refs[:n_in], refs[n_in:]
    value, _ = merged(in_refs)
    value = value.astype(jnp.bfloat16)
    part = out_refs[0].shape[1]
    for i, out_ref in enumerate(out_refs):
        out_ref[...] = value[:, i * part : (i + 1) * part]


def merge(messages):
    return pl.pallas_call(
        merge_kernel,
        out_shape=jax.ShapeDtypeStruct(messages[0].shape, jnp.bfloat16),
        name="merge",
        cost_estimate=pl.CostEstimate(
            flops=4 * len(messages) * messages[0].size,
            bytes_accessed=2 * (len(messages) + 1) * messages[0].size,
            transcendentals=0,
        ),
        compiler_params=pltpu.CompilerParams(vmem_limit_bytes=8 << 20),
    )(*messages)


def finish(messages, parts):
    width = messages[0].shape[1]
    return pl.pallas_call(
        functools.partial(finish_kernel, len(messages)),
        out_shape=[jax.ShapeDtypeStruct((HEAD_SIZE, width // parts), jnp.bfloat16)] * parts,
        name="finish",
        cost_estimate=pl.CostEstimate(
            flops=4 * len(messages) * messages[0].size,
            bytes_accessed=2 * (len(messages) + 1) * messages[0].size,
            transcendentals=0,
        ),
        compiler_params=pltpu.CompilerParams(vmem_limit_bytes=8 << 20),
    )(*messages)


def project_kernel(plan, *refs):
    group, rows, far = plan
    piece_refs, w_ref = refs[:group], refs[group]
    rest = refs[group + 1 :]
    add_ref = None if far else rest[0]
    out_ref, left_ref = rest[-2:]

    @pl.when(pl.program_id(0) == 0)
    def _():
        own = lax.rem(lax.axis_index("tok"), group)
        per = piece_refs[0].shape[1] // rows
        for offset in range(group):
            for j in range(per):
                block = jnp.transpose(
                    piece_refs[offset][:, j * rows : (j + 1) * rows].astype(jnp.float32)
                )
                start = pl.multiple_of(((own ^ offset) * per + j) * HEAD_SIZE, HEAD_SIZE)
                left_ref[:, pl.ds(start, HEAD_SIZE)] = block.astype(jnp.bfloat16)

    total = jnp.dot(left_ref[...], w_ref[...], preferred_element_type=jnp.float32)
    if add_ref is not None:
        total = total + add_ref[...].astype(jnp.float32)
    out_ref[...] = total.astype(jnp.bfloat16)


def project(pieces, out_weight, columns, half, rows, added):
    group = len(pieces)
    depth, width = out_weight.shape
    tile = min(512, columns)
    steps = columns // tile
    far = added is None

    def column(i):
        if columns == width:
            return i
        return (lax.axis_index("head") ^ half) * steps + i

    whole = pl.BlockSpec(pieces[0].shape, lambda i: (0, 0))
    in_specs = [whole] * group + [pl.BlockSpec((depth, tile), lambda i: (0, column(i)))]
    operands = list(pieces) + [out_weight]
    if not far:
        in_specs.append(pl.BlockSpec((rows, tile), lambda i: (0, i)))
        operands.append(added)
    return pl.pallas_call(
        functools.partial(project_kernel, (group, rows, far)),
        out_shape=jax.ShapeDtypeStruct((rows, columns), jnp.bfloat16),
        grid=(steps,),
        in_specs=in_specs,
        out_specs=pl.BlockSpec((rows, tile), lambda i: (0, i)),
        scratch_shapes=[pltpu.VMEM((rows, depth), jnp.bfloat16)],
        name="project",
        cost_estimate=pl.CostEstimate(
            flops=2 * rows * depth * columns,
            bytes_accessed=2 * depth * columns,
            transcendentals=0,
        ),
        compiler_params=pltpu.CompilerParams(vmem_limit_bytes=16 << 20),
    )(*operands)


def swap(x, bits, servers):
    return lax.ppermute(x, "tok", [(i, i ^ bits) for i in range(servers)])


def on_device(queries, keys, values, out_weight, task_slot, task_count):
    servers = lax.axis_size("tok")
    heads = lax.axis_size("head")
    server = lax.axis_index("tok")
    rows = queries.shape[0]
    group = task_slot.shape[0]
    q_per_kv = HEADS // KVH
    planes = servers // group
    move = functools.partial(swap, servers=servers)

    caches = pack_cache(keys, values, group)
    pieces = pack_queries(queries, group, q_per_kv, server * rows)
    if group == 4:
        mine = jnp.concatenate([pieces[0], move(pieces[1], 1)], axis=0)
        across = jnp.concatenate([pieces[2], move(pieces[3], 1)], axis=0)
        own_chunks = [(0, mine), (2, move(across, 2))]
        cache_x = move(caches[3], 1)
        caches = [caches[0], move(caches[1], 1), move(caches[2], 2), move(cache_x, 2)]
    else:
        own_chunks = [(0, pieces[0])]

    held = list(own_chunks)
    bit = servers // 2
    while bit >= group:
        held = held + [(d ^ bit, move(chunk, bit)) for d, chunk in held]
        bit //= 2

    partial = {}
    call = functools.partial(
        attention, caches=caches, task_slot=task_slot, task_count=task_count, rows_dev=rows
    )
    near = [(d, chunk) for d, chunk in held if d // group <= 1]
    rest = [(d, chunk) for d, chunk in held if d // group > 1]
    waves = [near] + [rest[i : i + 2] for i in range(0, len(rest), 2)]
    for wave in waves:
        if wave:
            results = call([chunk for _, chunk in wave], [d for d, _ in wave])
            for (d, _), result in zip(wave, results):
                partial[d] = [result]

    bit = group
    while bit < servers:
        for d in sorted(partial, reverse=True):
            if d & bit:
                messages = partial.pop(d)
                message = messages[0] if len(messages) == 1 else merge(messages)
                partial[d ^ bit].append(move(message, bit))
        bit *= 2

    if group == 4:
        far_own, far_other = finish(partial[2], 2)
        far_other = move(move(far_other, 2), 1)
        far_own = move(far_own, 2)
        near_own, near_other = finish(partial[0], 2)
        near_other = move(near_other, 1)
        attended = [near_own, near_other, far_own, far_other]
    else:
        attended = finish(partial[0], 1)

    if heads == 2:
        columns = out_weight.shape[1] // 2
        away = project(attended, out_weight, columns, 1, rows, None)
        arrived = lax.ppermute(away, "head", [(0, 1), (1, 0)])
        return project(attended, out_weight, columns, 0, rows, arrived)
    share = project(attended, out_weight, out_weight.shape[1], 0, rows, None)
    return lax.psum_scatter(share, "head", scatter_dimension=1, tiled=True)


def solution(mesh):
    placed = (
        P("tok", "head"),
        P("tok", "head"),
        P("tok", "head"),
        P("head", None),
        P("head", None, None),
        P("head", None),
    )
    return jax.shard_map(
        on_device, mesh=mesh, in_specs=placed, out_specs=P("tok", "head"), check_vma=False
    )
```

```python
import functools
import math

import jax
import jax.numpy as jnp
from jax import lax
from jax.experimental import pallas as pl
from jax.experimental.pallas import tpu as pltpu
from jax.sharding import PartitionSpec as P

HEADS = 32
KVH = 8
HEAD_SIZE = 128
QBLK = 128

theta_base = 500000.0
neg_fill = -1e30
LOG2E = math.log2(math.e)
STAT_ROWS = 8
SUM_ROWS = 16


def rotary_tables(rows, first_row):
    half = HEAD_SIZE // 2
    frequency = theta_base ** (-(jnp.arange(half, dtype=jnp.float32) * (2.0 / HEAD_SIZE)))
    places = (first_row + jnp.arange(rows, dtype=jnp.int32)).astype(jnp.float32)
    angles = places[:, None] * frequency[None, :]
    cosine = jnp.cos(angles)
    sine = jnp.sin(angles)
    return (
        jnp.concatenate([cosine, cosine], axis=1),
        jnp.concatenate([-sine, sine], axis=1),
    )


def pack_queries_kernel(order, q_per_kv, cos_ref, sin_ref, q_ref, *out_refs):
    own = lax.rem(lax.axis_index("tok"), sum(len(offsets) for offsets in order))
    rows = q_ref.shape[0]
    cosine = cos_ref[...]
    sine = sin_ref[...]
    for offsets, out_ref in zip(order, out_refs):
        for at, offset in enumerate(offsets):
            head = own ^ offset
            for j in range(q_per_kv):
                start = pl.multiple_of((head * q_per_kv + j) * HEAD_SIZE, HEAD_SIZE)
                x = q_ref[:, pl.ds(start, HEAD_SIZE)].astype(jnp.float32)
                turned = pltpu.roll(x, HEAD_SIZE // 2, 1)
                row = (at * q_per_kv + j) * rows
                out_ref[row : row + rows, :] = (x * cosine + turned * sine).astype(jnp.bfloat16)


def pack_queries(queries, order, q_per_kv, first_row):
    rows = queries.shape[0]
    cosine, sine = rotary_tables(rows, first_row)
    return pl.pallas_call(
        functools.partial(pack_queries_kernel, order, q_per_kv),
        out_shape=[
            jax.ShapeDtypeStruct((len(offsets) * q_per_kv * rows, HEAD_SIZE), jnp.bfloat16)
            for offsets in order
        ],
        name="pack_queries",
        cost_estimate=pl.CostEstimate(
            flops=6 * queries.size, bytes_accessed=4 * queries.size, transcendentals=0
        ),
        compiler_params=pltpu.CompilerParams(vmem_limit_bytes=8 << 20),
    )(cosine, sine, queries)


def pack_cache_kernel(order, k_ref, v_ref, *out_refs):
    own = lax.rem(lax.axis_index("tok"), sum(len(offsets) for offsets in order))
    keys = k_ref.shape[0]
    for offsets, out_ref in zip(order, out_refs):
        for at, offset in enumerate(offsets):
            start = pl.multiple_of((own ^ offset) * HEAD_SIZE, HEAD_SIZE)
            row = 2 * at * keys
            out_ref[row : row + keys, :] = k_ref[:, pl.ds(start, HEAD_SIZE)]
            out_ref[row + keys : row + 2 * keys, :] = v_ref[:, pl.ds(start, HEAD_SIZE)]


def pack_cache(keys, values, order):
    return pl.pallas_call(
        functools.partial(pack_cache_kernel, order),
        out_shape=[
            jax.ShapeDtypeStruct((len(offsets) * 2 * keys.shape[0], HEAD_SIZE), jnp.bfloat16)
            for offsets in order
        ],
        name="pack_cache",
        cost_estimate=pl.CostEstimate(
            flops=0, bytes_accessed=8 * keys.size, transcendentals=0
        ),
        compiler_params=pltpu.CompilerParams(vmem_limit_bytes=16 << 20),
    )(keys, values)


def lay_cache_kernel(keys, *refs):
    *in_refs, k_ref, v_ref = refs
    for at, ref in enumerate(in_refs):
        k_ref[at] = ref[:keys, :]
        v_ref[at, :HEAD_SIZE, :] = jnp.transpose(
            ref[keys : 2 * keys, :].astype(jnp.float32)
        ).astype(jnp.bfloat16)
        v_ref[at, HEAD_SIZE:, :] = jnp.ones((SUM_ROWS, keys), jnp.bfloat16)


def lay_cache(pieces, keys):
    group = len(pieces)
    return pl.pallas_call(
        functools.partial(lay_cache_kernel, keys),
        out_shape=[
            jax.ShapeDtypeStruct((group, keys, HEAD_SIZE), jnp.bfloat16),
            jax.ShapeDtypeStruct((group, HEAD_SIZE + SUM_ROWS, keys), jnp.bfloat16),
        ],
        name="lay_cache",
        cost_estimate=pl.CostEstimate(
            flops=0, bytes_accessed=8 * group * keys * HEAD_SIZE, transcendentals=0
        ),
        compiler_params=pltpu.CompilerParams(vmem_limit_bytes=16 << 20),
    )(*pieces)


def split_stat(stat, width):
    high = stat.astype(jnp.bfloat16).astype(jnp.float32)
    rest = stat - high
    middle = rest.astype(jnp.bfloat16).astype(jnp.float32)
    low = rest - middle
    row = lax.broadcasted_iota(jnp.int32, (STAT_ROWS, width), 0)
    spread = jnp.where(row == 0, high, jnp.where(row == 1, middle, jnp.where(row == 2, low, 0.0)))
    return spread.astype(jnp.bfloat16)


def join_stat(ref):
    stat = ref[HEAD_SIZE : HEAD_SIZE + STAT_ROWS, :].astype(jnp.float32)
    return stat[0:1] + stat[1:2] + stat[2:3]


def attention_kernel(plan, slot_ref, count_ref, *refs):
    displacements, widths, rows_dev, slab = plan
    n_chunks = len(displacements)
    n_in = len(widths)
    q_in_refs = refs[:n_in]
    k_ref, v_ref, out_ref = refs[n_in : n_in + 3]
    list_ref, q_ref, m_ref, acc_ref, *slots = refs[n_in + 3 :]
    group, keys = k_ref.shape[:2]
    width = q_ref.shape[1]
    server = lax.axis_index("tok")
    head = lax.rem(server, group)
    scale = HEAD_SIZE ** (-0.5) * LOG2E

    found = jnp.int32(0)
    for i in range(n_chunks):
        block = ((server ^ displacements[i]) * rows_dev) // QBLK
        for k in range(group):
            key_block = server ^ k
            slot = slot_ref[head, block, key_block]
            active = (slot >= 0) & (slot < count_ref[head, key_block])
            list_ref[found] = i * group + k
            found = found + active.astype(jnp.int32)

    at = 0
    for q_in_ref, n in zip(q_in_refs, widths):
        for i in range(n):
            q_ref[at + i] = q_in_ref[i * width : (i + 1) * width, :]
        at += n
    m_ref[...] = jnp.full_like(m_ref, neg_fill)
    acc_ref[...] = jnp.zeros_like(acc_ref)

    def pair(i):
        entry = list_ref[i]
        return entry // group, lax.rem(entry, group)

    def score(i, slot):
        chunk, k = pair(i)
        s_ref, top_ref, fade_ref = slot
        for c in range(0, width, slab):
            scores = lax.dot_general(
                k_ref[k],
                q_ref[chunk, c : c + slab, :],
                (((1,), (1,)), ((), ())),
                preferred_element_type=jnp.float32,
            )
            s_ref[:, c : c + slab] = scores
            old = m_ref[chunk, :, c : c + slab]
            new = jnp.maximum(old, jnp.max(scores, axis=0, keepdims=True))
            m_ref[chunk, :, c : c + slab] = new
            top_ref[:, c : c + slab] = new
            fade_ref[:, c : c + slab] = jnp.exp2((old - new) * scale)

    def weigh(i, slot):
        chunk, k = pair(i)
        s_ref, top_ref, fade_ref = slot
        for c in range(0, width, slab):
            p = jnp.exp2((s_ref[:, c : c + slab] - top_ref[0:1, c : c + slab]) * scale)
            product = jnp.dot(
                v_ref[k], p.astype(jnp.bfloat16), preferred_element_type=jnp.float32
            )
            acc_ref[chunk, :, c : c + slab] = (
                acc_ref[chunk, :, c : c + slab] * fade_ref[0:1, c : c + slab] + product
            )

    even, odd = slots[:3], slots[3:]

    @pl.when(found > 0)
    def _():
        score(0, even)

    def step(i, here, there):
        @pl.when(i + 1 < found)
        def _():
            score(i + 1, there)
            weigh(i, here)

        @pl.when(i + 1 == found)
        def _():
            weigh(i, here)

    def two(j, carry):
        step(2 * j, even, odd)
        step(2 * j + 1, odd, even)
        return carry

    lax.fori_loop(0, (found + 1) // 2, two, 0)

    for i in range(n_chunks):
        total = acc_ref[i, HEAD_SIZE : HEAD_SIZE + 1, :]
        seen = total > 0.0
        safe = jnp.where(seen, total, 1.0)
        stat = jnp.where(seen, m_ref[i, 0:1, :] * scale + jnp.log2(safe), neg_fill)
        lanes = slice(i * width, (i + 1) * width)
        out_ref[:HEAD_SIZE, lanes] = (acc_ref[i, :HEAD_SIZE, :] * (1.0 / safe)).astype(jnp.bfloat16)
        out_ref[HEAD_SIZE:, lanes] = split_stat(stat, width)


def attention(chunks, displacements, cache, task_slot, task_count, rows_dev, width):
    k, v = cache
    group, keys = k.shape[:2]
    widths = tuple(chunk.shape[0] // width for chunk in chunks)
    n = len(displacements)
    vmem = pl.BlockSpec(memory_space=pltpu.VMEM)
    smem = pl.BlockSpec(memory_space=pltpu.SMEM)
    slot = [
        pltpu.VMEM((keys, width), jnp.float32),
        pltpu.VMEM((8, width), jnp.float32),
        pltpu.VMEM((8, width), jnp.float32),
    ]
    return pl.pallas_call(
        functools.partial(
            attention_kernel, (tuple(displacements), widths, rows_dev, min(256, width))
        ),
        out_shape=jax.ShapeDtypeStruct((HEAD_SIZE + STAT_ROWS, n * width), jnp.bfloat16),
        in_specs=[smem, smem] + [vmem] * (len(chunks) + 2),
        out_specs=vmem,
        scratch_shapes=[
            pltpu.SMEM((n * group + 1,), jnp.int32),
            pltpu.VMEM((n, width, HEAD_SIZE), jnp.bfloat16),
            pltpu.VMEM((n, 8, width), jnp.float32),
            pltpu.VMEM((n, HEAD_SIZE + SUM_ROWS, width), jnp.float32),
        ]
        + slot
        + slot,
        name="attention",
        cost_estimate=pl.CostEstimate(
            flops=4 * n * group * keys * width * HEAD_SIZE,
            bytes_accessed=4 * n * width * HEAD_SIZE + 4 * group * keys * HEAD_SIZE,
            transcendentals=n * group * keys * width,
        ),
        compiler_params=pltpu.CompilerParams(vmem_limit_bytes=24 << 20),
    )(task_slot, task_count, *chunks, k, v)


def merged(refs):
    stats = [join_stat(ref) for ref in refs]
    largest = functools.reduce(jnp.maximum, stats)
    weights = [jnp.exp2(stat - largest) for stat in stats]
    total = functools.reduce(jnp.add, weights)
    inverse = 1.0 / total
    value = functools.reduce(
        jnp.add,
        [
            (weight * inverse) * ref[:HEAD_SIZE, :].astype(jnp.float32)
            for weight, ref in zip(weights, refs)
        ],
    )
    return value, largest + jnp.log2(total)


def merge_kernel(n_in, keep_stat, *refs):
    in_refs, out_refs = refs[:n_in], refs[n_in:]
    value, stat = merged(in_refs)
    value = value.astype(jnp.bfloat16)
    part = out_refs[0].shape[1]
    for i, out_ref in enumerate(out_refs):
        lanes = slice(i * part, (i + 1) * part)
        out_ref[:HEAD_SIZE, :] = value[:, lanes]
        if keep_stat:
            out_ref[HEAD_SIZE:, :] = split_stat(stat[:, lanes], part)


def merge(messages, parts, keep_stat=True):
    height, width = messages[0].shape
    height = height if keep_stat else HEAD_SIZE
    return pl.pallas_call(
        functools.partial(merge_kernel, len(messages), keep_stat),
        out_shape=[jax.ShapeDtypeStruct((height, width // parts), jnp.bfloat16)] * parts,
        name="merge" if keep_stat else "finish",
        cost_estimate=pl.CostEstimate(
            flops=4 * len(messages) * messages[0].size,
            bytes_accessed=2 * (len(messages) + 1) * messages[0].size,
            transcendentals=0,
        ),
        compiler_params=pltpu.CompilerParams(vmem_limit_bytes=8 << 20),
    )(*messages)


def project_kernel(plan, *refs):
    group, rows, far = plan
    piece_refs, w_ref = refs[:group], refs[group]
    rest = refs[group + 1 :]
    add_ref = None if far else rest[0]
    out_ref, left_ref = rest[-2:]

    @pl.when(pl.program_id(0) == 0)
    def _():
        own = lax.rem(lax.axis_index("tok"), group)
        per = piece_refs[0].shape[1] // rows
        for offset in range(group):
            for j in range(per):
                block = jnp.transpose(
                    piece_refs[offset][:, j * rows : (j + 1) * rows].astype(jnp.float32)
                )
                start = pl.multiple_of(((own ^ offset) * per + j) * HEAD_SIZE, HEAD_SIZE)
                left_ref[:, pl.ds(start, HEAD_SIZE)] = block.astype(jnp.bfloat16)

    total = jnp.dot(left_ref[...], w_ref[...], preferred_element_type=jnp.float32)
    if add_ref is not None:
        total = total + add_ref[...].astype(jnp.float32)
    out_ref[...] = total.astype(jnp.bfloat16)


def project(pieces, out_weight, columns, half, rows, added):
    group = len(pieces)
    depth, width = out_weight.shape
    tile = min(512, columns)
    steps = columns // tile
    far = added is None

    def column(i):
        if columns == width:
            return i
        return (lax.axis_index("head") ^ half) * steps + i

    whole = pl.BlockSpec(pieces[0].shape, lambda i: (0, 0))
    in_specs = [whole] * group + [pl.BlockSpec((depth, tile), lambda i: (0, column(i)))]
    operands = list(pieces) + [out_weight]
    if not far:
        in_specs.append(pl.BlockSpec((rows, tile), lambda i: (0, i)))
        operands.append(added)
    return pl.pallas_call(
        functools.partial(project_kernel, (group, rows, far)),
        out_shape=jax.ShapeDtypeStruct((rows, columns), jnp.bfloat16),
        grid=(steps,),
        in_specs=in_specs,
        out_specs=pl.BlockSpec((rows, tile), lambda i: (0, i)),
        scratch_shapes=[pltpu.VMEM((rows, depth), jnp.bfloat16)],
        name="project",
        cost_estimate=pl.CostEstimate(
            flops=2 * rows * depth * columns,
            bytes_accessed=2 * depth * columns,
            transcendentals=0,
        ),
        compiler_params=pltpu.CompilerParams(vmem_limit_bytes=16 << 20),
    )(*operands)


def swap(x, bits, servers):
    return lax.ppermute(x, "tok", [(i, i ^ bits) for i in range(servers)])


def attend_grouped(queries, keys, values, task_slot, task_count, move):
    core, column, near, far = 1, 2, 4, 8
    rows, n_keys = queries.shape[0], keys.shape[0]
    q_per_kv = HEADS // KVH
    part = q_per_kv * rows
    width = 2 * part

    keep, send = pack_queries(queries, ((0, 2), (1, 3)), q_per_kv, lax.axis_index("tok") * rows)
    mine, theirs, away = pack_cache(keys, values, ((0,), (1,), (2, 3)))
    got = move(send, core)
    own = jnp.concatenate([keep[:part], got[:part]], axis=0)
    other = jnp.concatenate([keep[part:], got[part:]], axis=0)
    own_far = move(own, far)
    other_far = move(other, far | column)
    other_own = move(other, column)
    beside = move(away, column)
    both_near = move(jnp.concatenate([own, other_own], axis=0), near)
    own_last = move(own_far, near)
    other_last = move(other_far, near)

    pieces = [mine, move(theirs, core), beside[: 2 * n_keys], move(beside[2 * n_keys :], core)]
    call = functools.partial(
        attention,
        cache=lay_cache(pieces, n_keys),
        task_slot=task_slot,
        task_count=task_count,
        rows_dev=rows,
        width=width,
    )
    part_own = call([own, other_own], [0, column])
    part_near = call([both_near], [near, near | column])
    part_far = call([own_far, other_far], [far, far | column])
    part_last = call([own_last, other_last], [far | near, far | near | column])

    last = move(part_last, near)
    own_back, other_back = merge([part_far, last], 2)
    own_back = move(own_back, far)
    other_back = move(other_back, far | column)
    own_here, other_here = merge([part_own, move(part_near, near)], 2)
    other_here = move(other_here, column)
    a_own, a_other = merge([own_here, own_back], 2, False)
    b_own, b_other = merge([other_here, other_back], 2, False)
    return [a_own, move(a_other, core), b_own, move(b_other, core)]


def attend_general(queries, keys, values, task_slot, task_count, move, servers):
    assert task_slot.shape[0] == 1
    rows = queries.shape[0]
    q_per_kv = HEADS // KVH
    (own,) = pack_queries(queries, ((0,),), q_per_kv, lax.axis_index("tok") * rows)
    cache = lay_cache(pack_cache(keys, values, ((0,),)), keys.shape[0])
    held = {0: own}
    bit = servers // 2
    while bit:
        held.update({d ^ bit: move(chunk, bit) for d, chunk in held.items()})
        bit //= 2
    order = sorted(held)
    width = q_per_kv * rows
    partial = {}
    step = min(4, servers)
    for i in range(0, servers, step):
        result = attention(
            [held[d] for d in order[i : i + step]],
            order[i : i + step],
            cache,
            task_slot,
            task_count,
            rows,
            width,
        )
        for j, d in enumerate(order[i : i + step]):
            partial[d] = [result[:, j * width : (j + 1) * width]]
    bit = 1
    while bit < servers:
        for d in sorted(partial, reverse=True):
            if d & bit:
                messages = partial.pop(d)
                message = messages[0] if len(messages) == 1 else merge(messages, 1)[0]
                partial[d ^ bit].append(move(message, bit))
        bit *= 2
    return merge(partial[0], 1, False)


def on_device(queries, keys, values, out_weight, task_slot, task_count):
    servers = lax.axis_size("tok")
    heads = lax.axis_size("head")
    rows = queries.shape[0]
    group = task_slot.shape[0]
    move = functools.partial(swap, servers=servers)
    if group == 4 and servers == 16:
        attended = attend_grouped(queries, keys, values, task_slot, task_count, move)
    else:
        attended = attend_general(queries, keys, values, task_slot, task_count, move, servers)

    if heads == 2:
        columns = out_weight.shape[1] // 2
        away = project(attended, out_weight, columns, 1, rows, None)
        arrived = lax.ppermute(away, "head", [(0, 1), (1, 0)])
        return project(attended, out_weight, columns, 0, rows, arrived)
    share = project(attended, out_weight, out_weight.shape[1], 0, rows, None)
    return lax.psum_scatter(share, "head", scatter_dimension=1, tiled=True)


def solution(mesh):
    placed = (
        P("tok", "head"),
        P("tok", "head"),
        P("tok", "head"),
        P("head", None),
        P("head", None, None),
        P("head", None),
    )
    return jax.shard_map(
        on_device, mesh=mesh, in_specs=placed, out_specs=P("tok", "head"), check_vma=False
    )
```

```python
import functools
import math

import jax
import jax.numpy as jnp
from jax import lax
from jax.experimental import pallas as pl
from jax.experimental.pallas import tpu as pltpu
from jax.sharding import PartitionSpec as P


HEADS = 32
KVH = 8
HEAD_SIZE = 128
QBLK = 128

theta_base = 500000.0
neg_fill = -1e30
LOG2E = math.log2(math.e)
STAT_ROWS = 8
SUM_ROWS = 16
PACK_VMEM = 56 << 20
LAY_VMEM = 8 << 20


def rotary_tables(rows, first_row):
    half = HEAD_SIZE // 2
    frequency = theta_base ** (-(jnp.arange(half, dtype=jnp.float32) * (2.0 / HEAD_SIZE)))
    places = (first_row + jnp.arange(rows, dtype=jnp.int32)).astype(jnp.float32)
    angles = places[:, None] * frequency[None, :]
    cosine = jnp.cos(angles)
    sine = jnp.sin(angles)
    return (
        jnp.concatenate([cosine, cosine], axis=1),
        jnp.concatenate([-sine, sine], axis=1),
    )


def pack_kernel(plan, *refs):
    q_order, kv_order, q_per_kv, group = plan
    n_q, n_kv = len(q_order), len(kv_order)
    cos_ref, sin_ref, q_hbm, k_hbm, v_hbm = refs[:5]
    q_out_refs = refs[5 : 5 + n_q]
    kv_out_refs = refs[5 + n_q : 5 + n_q + n_kv]
    q_ref, sems = refs[5 + n_q + n_kv :]
    rows, keys = q_ref.shape[0], k_hbm.shape[0]
    own = lax.rem(lax.axis_index("tok"), group)

    q_copy = pltpu.make_async_copy(q_hbm, q_ref, sems.at[0])
    q_copy.start()
    copies = []
    for offsets, out_ref in zip(kv_order, kv_out_refs):
        for at, offset in enumerate(offsets):
            start = pl.multiple_of((own ^ offset) * HEAD_SIZE, HEAD_SIZE)
            for part, ref in enumerate((k_hbm, v_hbm)):
                row = (2 * at + part) * keys
                copy = pltpu.make_async_copy(
                    ref.at[:, pl.ds(start, HEAD_SIZE)],
                    out_ref.at[row : row + keys, :],
                    sems.at[1 + len(copies)],
                )
                copy.start()
                copies.append(copy)

    q_copy.wait()
    cosine = cos_ref[...]
    sine = sin_ref[...]
    for offsets, out_ref in zip(q_order, q_out_refs):
        for at, offset in enumerate(offsets):
            head = own ^ offset
            for j in range(q_per_kv):
                start = pl.multiple_of((head * q_per_kv + j) * HEAD_SIZE, HEAD_SIZE)
                x = q_ref[:, pl.ds(start, HEAD_SIZE)].astype(jnp.float32)
                turned = pltpu.roll(x, HEAD_SIZE // 2, 1)
                row = (at * q_per_kv + j) * rows
                out_ref[row : row + rows, :] = (x * cosine + turned * sine).astype(jnp.bfloat16)
    for copy in copies:
        copy.wait()


def pack(queries, keys, values, group, q_order, kv_order):
    rows = queries.shape[0]
    q_per_kv = HEADS // KVH
    cosine, sine = rotary_tables(rows, lax.axis_index("tok") * rows)
    hbm = pl.BlockSpec(memory_space=pltpu.HBM)
    vmem = pl.BlockSpec(memory_space=pltpu.VMEM)
    q_out = [
        jax.ShapeDtypeStruct((len(offsets) * q_per_kv * rows, HEAD_SIZE), jnp.bfloat16)
        for offsets in q_order
    ]
    kv_out = [
        jax.ShapeDtypeStruct((len(offsets) * 2 * keys.shape[0], HEAD_SIZE), jnp.bfloat16)
        for offsets in kv_order
    ]
    results = pl.pallas_call(
        functools.partial(pack_kernel, (q_order, kv_order, q_per_kv, group)),
        out_shape=q_out + kv_out,
        in_specs=[vmem, vmem] + [hbm] * 3,
        out_specs=[vmem] * (len(q_out) + len(kv_out)),
        scratch_shapes=[
            pltpu.VMEM(queries.shape, queries.dtype),
            pltpu.SemaphoreType.DMA((1 + 2 * group,)),
        ],
        name="pack",
        cost_estimate=pl.CostEstimate(
            flops=6 * queries.size,
            bytes_accessed=4 * queries.size + 8 * keys.size,
            transcendentals=0,
        ),
        compiler_params=pltpu.CompilerParams(vmem_limit_bytes=PACK_VMEM),
    )(cosine, sine, queries, keys, values)
    return results[: len(q_out)], results[len(q_out) :]


def lay(keys, values):
    turned = jnp.transpose(values.astype(jnp.float32)).astype(jnp.bfloat16)
    ones = jnp.ones((SUM_ROWS, keys.shape[0]), jnp.bfloat16)
    return keys, turned, ones


def lay_own_kernel(plan, k_hbm, v_hbm, slot_hbm, count_hbm, k_out, v_out, mask_ref, *scratch):
    calls, rows = plan
    k_ref, v_ref, slot_ref, count_ref, sems = scratch
    server = lax.axis_index("tok")
    group = slot_ref.shape[0]
    own = lax.rem(server, group)
    start = pl.multiple_of(own * HEAD_SIZE, HEAD_SIZE)
    copies = [
        pltpu.make_async_copy(slot_hbm, slot_ref, sems.at[0]),
        pltpu.make_async_copy(count_hbm, count_ref, sems.at[1]),
        pltpu.make_async_copy(k_hbm.at[:, pl.ds(start, HEAD_SIZE)], k_ref, sems.at[2]),
        pltpu.make_async_copy(v_hbm.at[:, pl.ds(start, HEAD_SIZE)], v_ref, sems.at[3]),
    ]
    for copy in copies:
        copy.start()
    for copy in copies:
        copy.wait()
    for call, displacements in enumerate(calls):
        mask = jnp.int32(0)
        for i, displacement in enumerate(displacements):
            block = ((server ^ displacement) * rows) // QBLK
            for k in range(group):
                key_block = server ^ k
                slot = slot_ref[own, block, key_block]
                active = (slot >= 0) & (slot < count_ref[own, key_block])
                mask = mask | (active.astype(jnp.int32) << (i * group + k))
        mask_ref[call] = jnp.full(mask_ref.shape[1:], mask, jnp.int32)
    k_out[...], v_out[:HEAD_SIZE, :], v_out[HEAD_SIZE:, :] = lay(k_ref[...], v_ref[...])


def lay_own(keys, values, task_slot, task_count, calls, rows):
    n = keys.shape[0]
    hbm = pl.BlockSpec(memory_space=pltpu.HBM)
    return pl.pallas_call(
        functools.partial(lay_own_kernel, (calls, rows)),
        out_shape=[
            jax.ShapeDtypeStruct((n, HEAD_SIZE), jnp.bfloat16),
            jax.ShapeDtypeStruct((HEAD_SIZE + SUM_ROWS, n), jnp.bfloat16),
            jax.ShapeDtypeStruct((len(calls), 8, HEAD_SIZE), jnp.int32),
        ],
        in_specs=[hbm] * 4,
        scratch_shapes=[
            pltpu.VMEM((n, HEAD_SIZE), keys.dtype),
            pltpu.VMEM((n, HEAD_SIZE), values.dtype),
            pltpu.SMEM(task_slot.shape, task_slot.dtype),
            pltpu.SMEM(task_count.shape, task_count.dtype),
            pltpu.SemaphoreType.DMA((4,)),
        ],
        name="lay_own",
        cost_estimate=pl.CostEstimate(
            flops=0, bytes_accessed=8 * n * HEAD_SIZE, transcendentals=0
        ),
        compiler_params=pltpu.CompilerParams(vmem_limit_bytes=LAY_VMEM),
    )(keys, values, task_slot, task_count)


def lay_cache_kernel(keys, counts, k_own, v_own, *refs):
    *in_refs, k_ref, v_ref = refs
    k_ref[0] = k_own[...]
    v_ref[0] = v_own[...]
    at = 1
    for ref, count in zip(in_refs, counts):
        for i in range(count):
            row = 2 * i * keys
            k_ref[at], v_ref[at, :HEAD_SIZE, :], v_ref[at, HEAD_SIZE:, :] = lay(
                ref[row : row + keys, :], ref[row + keys : row + 2 * keys, :]
            )
            at += 1


def lay_cache(k_own, v_own, pieces, counts):
    group = 1 + sum(counts)
    keys = k_own.shape[0]
    return pl.pallas_call(
        functools.partial(lay_cache_kernel, keys, counts),
        out_shape=[
            jax.ShapeDtypeStruct((group,) + k_own.shape, jnp.bfloat16),
            jax.ShapeDtypeStruct((group,) + v_own.shape, jnp.bfloat16),
        ],
        name="lay_cache",
        cost_estimate=pl.CostEstimate(
            flops=0, bytes_accessed=8 * group * keys * HEAD_SIZE, transcendentals=0
        ),
        compiler_params=pltpu.CompilerParams(vmem_limit_bytes=8 << 20),
    )(k_own, v_own, *pieces)


def split_stat(stat, width):
    high = stat.astype(jnp.bfloat16).astype(jnp.float32)
    rest = stat - high
    middle = rest.astype(jnp.bfloat16).astype(jnp.float32)
    low = rest - middle
    row = lax.broadcasted_iota(jnp.int32, (STAT_ROWS, width), 0)
    spread = jnp.where(row == 0, high, jnp.where(row == 1, middle, jnp.where(row == 2, low, 0.0)))
    return spread.astype(jnp.bfloat16)


def join_stat(ref):
    stat = ref[HEAD_SIZE : HEAD_SIZE + STAT_ROWS, :].astype(jnp.float32)
    return stat[0:1] + stat[1:2] + stat[2:3]


def attention_kernel(plan, mask_ref, *refs):
    which, widths, slab = plan
    n_chunks = sum(widths)
    n_in = len(widths)
    q_in_refs = refs[:n_in]
    k_ref, v_ref, _, out_ref = refs[n_in : n_in + 4]
    list_ref, q_ref, m_ref, acc_ref, *slots = refs[n_in + 4 :]
    group, _ = k_ref.shape[:2]
    width = q_ref.shape[1]
    scale = HEAD_SIZE ** (-0.5) * LOG2E

    mask = mask_ref[which, 0, 0]
    found = jnp.int32(0)
    for i in range(n_chunks * group):
        list_ref[found] = i
        found = found + ((mask >> i) & 1)

    at = 0
    for q_in_ref, n in zip(q_in_refs, widths):
        for i in range(n):
            q_ref[at + i] = q_in_ref[i * width : (i + 1) * width, :]
        at += n
    m_ref[...] = jnp.full_like(m_ref, neg_fill)
    acc_ref[...] = jnp.zeros_like(acc_ref)

    def pair(i):
        entry = list_ref[i]
        return entry // group, lax.rem(entry, group)

    def score(i, slot):
        chunk, k = pair(i)
        s_ref, top_ref, fade_ref = slot
        for c in range(0, width, slab):
            scores = lax.dot_general(
                k_ref[k],
                q_ref[chunk, c : c + slab, :],
                (((1,), (1,)), ((), ())),
                preferred_element_type=jnp.float32,
            )
            s_ref[:, c : c + slab] = scores
            old = m_ref[chunk, :, c : c + slab]
            new = jnp.maximum(old, jnp.max(scores, axis=0, keepdims=True))
            m_ref[chunk, :, c : c + slab] = new
            top_ref[:, c : c + slab] = new
            fade_ref[:, c : c + slab] = jnp.exp2((old - new) * scale)

    def weigh(i, slot):
        chunk, k = pair(i)
        s_ref, top_ref, fade_ref = slot
        for c in range(0, width, slab):
            p = jnp.exp2((s_ref[:, c : c + slab] - top_ref[0:1, c : c + slab]) * scale)
            product = jnp.dot(
                v_ref[k], p.astype(jnp.bfloat16), preferred_element_type=jnp.float32
            )
            acc_ref[chunk, :, c : c + slab] = (
                acc_ref[chunk, :, c : c + slab] * fade_ref[0:1, c : c + slab] + product
            )

    even, odd = slots[:3], slots[3:]

    @pl.when(found > 0)
    def _():
        score(0, even)

    def step(i, here, there):
        @pl.when(i + 1 < found)
        def _():
            score(i + 1, there)
            weigh(i, here)

        @pl.when(i + 1 == found)
        def _():
            weigh(i, here)

    def two(j, carry):
        step(2 * j, even, odd)
        step(2 * j + 1, odd, even)
        return carry

    lax.fori_loop(0, (found + 1) // 2, two, 0)

    for i in range(n_chunks):
        total = acc_ref[i, HEAD_SIZE : HEAD_SIZE + 1, :]
        seen = total > 0.0
        safe = jnp.where(seen, total, 1.0)
        stat = jnp.where(seen, m_ref[i, 0:1, :] * scale + jnp.log2(safe), neg_fill)
        lanes = slice(i * width, (i + 1) * width)
        out_ref[:HEAD_SIZE, lanes] = (acc_ref[i, :HEAD_SIZE, :] * (1.0 / safe)).astype(jnp.bfloat16)
        out_ref[HEAD_SIZE:, lanes] = split_stat(stat, width)


def attention(chunks, which, cache, masks, width, after):
    k, v = cache
    group, keys = k.shape[:2]
    widths = tuple(chunk.shape[0] // width for chunk in chunks)
    n = sum(widths)
    vmem = pl.BlockSpec(memory_space=pltpu.VMEM)
    slot = [
        pltpu.VMEM((keys, width), jnp.float32),
        pltpu.VMEM((8, width), jnp.float32),
        pltpu.VMEM((8, width), jnp.float32),
    ]
    return pl.pallas_call(
        functools.partial(attention_kernel, (which, widths, min(256, width))),
        out_shape=jax.ShapeDtypeStruct((HEAD_SIZE + STAT_ROWS, n * width), jnp.bfloat16),
        in_specs=[vmem] * (len(chunks) + 3)
        + [pl.BlockSpec(memory_space=pl.ANY)],
        out_specs=vmem,
        scratch_shapes=[
            pltpu.SMEM((n * group + 1,), jnp.int32),
            pltpu.VMEM((n, width, HEAD_SIZE), jnp.bfloat16),
            pltpu.VMEM((n, 8, width), jnp.float32),
            pltpu.VMEM((n, HEAD_SIZE + SUM_ROWS, width), jnp.float32),
        ]
        + slot
        + slot,
        name="attention",
        cost_estimate=pl.CostEstimate(
            flops=4 * n * group * keys * width * HEAD_SIZE,
            bytes_accessed=4 * n * width * HEAD_SIZE + 4 * group * keys * HEAD_SIZE,
            transcendentals=n * group * keys * width,
        ),
        compiler_params=pltpu.CompilerParams(vmem_limit_bytes=16 << 20),
    )(masks, *chunks, k, v, after)


def merged(refs):
    stats = [join_stat(ref) for ref in refs]
    largest = functools.reduce(jnp.maximum, stats)
    weights = [jnp.exp2(stat - largest) for stat in stats]
    total = functools.reduce(jnp.add, weights)
    inverse = 1.0 / total
    value = functools.reduce(
        jnp.add,
        [
            (weight * inverse) * ref[:HEAD_SIZE, :].astype(jnp.float32)
            for weight, ref in zip(weights, refs)
        ],
    )
    return value, largest + jnp.log2(total)


def merge_kernel(n_in, keep_stat, *refs):
    in_refs, out_refs = refs[:n_in], refs[n_in:]
    value, stat = merged(in_refs)
    value = value.astype(jnp.bfloat16)
    part = out_refs[0].shape[1]
    for i, out_ref in enumerate(out_refs):
        lanes = slice(i * part, (i + 1) * part)
        out_ref[:HEAD_SIZE, :] = value[:, lanes]
        if keep_stat:
            out_ref[HEAD_SIZE:, :] = split_stat(stat[:, lanes], part)


def merge(messages, parts, keep_stat=True):
    height, width = messages[0].shape
    height = height if keep_stat else HEAD_SIZE
    return pl.pallas_call(
        functools.partial(merge_kernel, len(messages), keep_stat),
        out_shape=[jax.ShapeDtypeStruct((height, width // parts), jnp.bfloat16)] * parts,
        name="merge" if keep_stat else "finish",
        cost_estimate=pl.CostEstimate(
            flops=4 * len(messages) * messages[0].size,
            bytes_accessed=2 * (len(messages) + 1) * messages[0].size,
            transcendentals=0,
        ),
        compiler_params=pltpu.CompilerParams(vmem_limit_bytes=8 << 20),
    )(*messages)


def gather_kernel(rows, *refs):
    *piece_refs, out_ref = refs
    group = len(piece_refs)
    own = lax.rem(lax.axis_index("tok"), group)
    per = piece_refs[0].shape[1] // rows
    for offset in range(group):
        for j in range(per):
            block = jnp.transpose(
                piece_refs[offset][:, j * rows : (j + 1) * rows].astype(jnp.float32)
            )
            start = pl.multiple_of(((own ^ offset) * per + j) * HEAD_SIZE, HEAD_SIZE)
            out_ref[:, pl.ds(start, HEAD_SIZE)] = block.astype(jnp.bfloat16)


def gather(pieces, rows):
    width = sum(piece.shape[1] for piece in pieces) // rows * HEAD_SIZE
    return pl.pallas_call(
        functools.partial(gather_kernel, rows),
        out_shape=jax.ShapeDtypeStruct((rows, width), jnp.bfloat16),
        name="gather",
        cost_estimate=pl.CostEstimate(
            flops=0, bytes_accessed=4 * rows * width, transcendentals=0
        ),
        compiler_params=pltpu.CompilerParams(vmem_limit_bytes=4 << 20),
    )(*pieces)


def project_kernel(half, start, left_ref, w_ref, out_ref):
    columns = out_ref.shape[1]
    if half is not None:
        start = (lax.axis_index("head") ^ half) * (w_ref.shape[1] // 2) + start
    start = pl.multiple_of(start, HEAD_SIZE)
    out_ref[...] = jnp.dot(
        left_ref[...], w_ref[:, pl.ds(start, columns)], preferred_element_type=jnp.float32
    ).astype(out_ref.dtype)


def project(left, out_weight, half, start, columns, kind):
    rows, depth = left.shape
    return pl.pallas_call(
        functools.partial(project_kernel, half, start),
        out_shape=jax.ShapeDtypeStruct((rows, columns), kind),
        in_specs=[pl.BlockSpec(memory_space=pltpu.VMEM)] * 2,
        out_specs=pl.BlockSpec(memory_space=pltpu.VMEM),
        name="project",
        cost_estimate=pl.CostEstimate(
            flops=2 * rows * depth * columns,
            bytes_accessed=2 * depth * columns,
            transcendentals=0,
        ),
        compiler_params=pltpu.CompilerParams(vmem_limit_bytes=24 << 20),
    )(left, out_weight)


def swap(x, bits, servers):
    return lax.ppermute(x, "tok", [(i, i ^ bits) for i in range(servers)])


def attend_grouped(queries, keys, values, task_slot, task_count, move):
    core, column, near, far = 1, 2, 4, 8
    rows, n_keys = queries.shape[0], keys.shape[0]
    q_per_kv = HEADS // KVH
    part = q_per_kv * rows
    width = 2 * part

    calls = tuple((plane, plane | column) for plane in (0, near, far, near | far))
    (keep, send), (away, theirs) = pack(
        queries, keys, values, 4, ((0, 2), (1, 3)), ((2,), (1, 3))
    )
    got = move(send, core)
    own = jnp.concatenate([keep[:part], got[:part]], axis=0)
    other = jnp.concatenate([keep[part:], got[part:]], axis=0)
    own_far = move(own, far)
    other_far = move(other, far | column)
    other_own = move(other, column)
    beside = move(theirs, core)
    across = move(jnp.concatenate([away, beside[2 * n_keys :]], axis=0), column)
    both_near = move(jnp.concatenate([own, other_own], axis=0), near)
    own_last = move(own_far, near)
    other_last = move(other_far, near)

    k_own, v_own, masks = lay_own(keys, values, task_slot, task_count, calls, rows)
    cache = lay_cache(k_own, v_own, [beside, across], (1, 2))
    call = functools.partial(attention, cache=cache, masks=masks, width=width)
    part_own = call([own, other_own], 0, after=masks)
    part_near = call([both_near], 1, after=part_own)
    part_far = call([own_far, other_far], 2, after=part_near)
    part_last = call([own_last, other_last], 3, after=part_far)

    last = move(part_last, near)
    own_back, other_back = merge([part_far, last], 2)
    own_back = move(own_back, far)
    other_back = move(other_back, far | column)
    own_here, other_here = merge([part_own, move(part_near, near)], 2)
    other_here = move(other_here, column)
    a_own, a_other = merge([own_here, own_back], 2, False)
    b_own, b_other = merge([other_here, other_back], 2, False)
    return [a_own, move(a_other, core), b_own, move(b_other, core)]


def attend_general(queries, keys, values, task_slot, task_count, move, servers):
    assert task_slot.shape[0] == 1
    rows = queries.shape[0]
    width = HEADS // KVH * rows
    step = min(4, servers)
    calls = tuple(tuple(range(i, i + step)) for i in range(0, servers, step))
    (own,), _ = pack(queries, keys, values, 1, ((0,),), ())
    k_own, v_own, masks = lay_own(keys, values, task_slot, task_count, calls, rows)
    cache = lay_cache(k_own, v_own, [], ())
    held = {0: own}
    bit = servers // 2
    while bit:
        held.update({d ^ bit: move(chunk, bit) for d, chunk in held.items()})
        bit //= 2
    partial = {}
    for which, call in enumerate(calls):
        result = attention([held[d] for d in call], which, cache, masks, width, masks)
        for j, d in enumerate(call):
            partial[d] = [result[:, j * width : (j + 1) * width]]
    bit = 1
    while bit < servers:
        for d in sorted(partial, reverse=True):
            if d & bit:
                messages = partial.pop(d)
                message = messages[0] if len(messages) == 1 else merge(messages, 1)[0]
                partial[d ^ bit].append(move(message, bit))
        bit *= 2
    return merge(partial[0], 1, False)


def on_device(queries, keys, values, out_weight, task_slot, task_count):
    servers = lax.axis_size("tok")
    heads = lax.axis_size("head")
    rows = queries.shape[0]
    group = task_slot.shape[0]
    move = functools.partial(swap, servers=servers)
    if group == 4 and servers == 16:
        attended = attend_grouped(queries, keys, values, task_slot, task_count, move)
    else:
        attended = attend_general(queries, keys, values, task_slot, task_count, move, servers)
    left = gather(attended, rows)

    columns = out_weight.shape[1] // heads
    if heads == 2:
        piece = columns // 2
        arrived = [
            lax.ppermute(
                project(left, out_weight, 1, start, piece, jnp.bfloat16), "head", [(0, 1), (1, 0)]
            )
            for start in (0, piece)
        ]
        here = project(left, out_weight, 0, 0, columns, jnp.float32)
        return (here + jnp.concatenate(arrived, axis=1).astype(jnp.float32)).astype(jnp.bfloat16)
    share = project(left, out_weight, None, 0, out_weight.shape[1], jnp.bfloat16)
    return lax.psum_scatter(share, "head", scatter_dimension=1, tiled=True)


def solution(mesh):
    placed = (
        P("tok", "head"),
        P("tok", "head"),
        P("tok", "head"),
        P("head", None),
        P("head", None, None),
        P("head", None),
    )
    return jax.shard_map(
        on_device, mesh=mesh, in_specs=placed, out_specs=P("tok", "head"), check_vma=False
    )
```

```python
import functools
import math

import jax
import jax.numpy as jnp
from jax import lax
from jax.experimental import pallas as pl
from jax.experimental.pallas import tpu as pltpu
from jax.sharding import PartitionSpec as P


HEADS = 32
KVH = 8
HEAD_SIZE = 128
QBLK = 128

theta_base = 500000.0
neg_fill = -1e30
LOG2E = math.log2(math.e)
STAT_ROWS = 8
SUM_ROWS = 16
PACK_VMEM = 47 << 20
LAY_VMEM = 8 << 20


def rotary_tables(rows, first_row):
    half = HEAD_SIZE // 2
    frequency = theta_base ** (-(jnp.arange(half, dtype=jnp.float32) * (2.0 / HEAD_SIZE)))
    places = (first_row + jnp.arange(rows, dtype=jnp.int32)).astype(jnp.float32)
    angles = places[:, None] * frequency[None, :]
    cosine = jnp.cos(angles)
    sine = jnp.sin(angles)
    return (
        jnp.concatenate([cosine, cosine], axis=1),
        jnp.concatenate([-sine, sine], axis=1),
    )


def pack_queries_kernel(order, q_per_kv, group, cos_ref, sin_ref, q_ref, *out_refs):
    own = lax.rem(lax.axis_index("tok"), group)
    rows = q_ref.shape[0]
    cosine = cos_ref[...]
    sine = sin_ref[...]
    for offsets, out_ref in zip(order, out_refs):
        for at, offset in enumerate(offsets):
            head = own ^ offset
            for j in range(q_per_kv):
                start = pl.multiple_of((head * q_per_kv + j) * HEAD_SIZE, HEAD_SIZE)
                x = q_ref[:, pl.ds(start, HEAD_SIZE)].astype(jnp.float32)
                turned = pltpu.roll(x, HEAD_SIZE // 2, 1)
                row = (at * q_per_kv + j) * rows
                out_ref[row : row + rows, :] = (x * cosine + turned * sine).astype(jnp.bfloat16)


def pack_queries(queries, group, order):
    rows = queries.shape[0]
    q_per_kv = HEADS // KVH
    cosine, sine = rotary_tables(rows, lax.axis_index("tok") * rows)
    return pl.pallas_call(
        functools.partial(pack_queries_kernel, order, q_per_kv, group),
        out_shape=[
            jax.ShapeDtypeStruct((len(offsets) * q_per_kv * rows, HEAD_SIZE), jnp.bfloat16)
            for offsets in order
        ],
        name="pack_queries",
        cost_estimate=pl.CostEstimate(
            flops=6 * queries.size, bytes_accessed=4 * queries.size, transcendentals=0
        ),
        compiler_params=pltpu.CompilerParams(vmem_limit_bytes=PACK_VMEM),
    )(cosine, sine, queries)


def pack_cache_kernel(order, group, k_ref, v_ref, *out_refs):
    own = lax.rem(lax.axis_index("tok"), group)
    keys = k_ref.shape[0]
    for offsets, out_ref in zip(order, out_refs):
        for at, offset in enumerate(offsets):
            start = pl.multiple_of((own ^ offset) * HEAD_SIZE, HEAD_SIZE)
            row = 2 * at * keys
            out_ref[row : row + keys, :] = k_ref[:, pl.ds(start, HEAD_SIZE)]
            out_ref[row + keys : row + 2 * keys, :] = v_ref[:, pl.ds(start, HEAD_SIZE)]


def pack_cache(keys, values, group, order):
    return pl.pallas_call(
        functools.partial(pack_cache_kernel, order, group),
        out_shape=[
            jax.ShapeDtypeStruct((len(offsets) * 2 * keys.shape[0], HEAD_SIZE), jnp.bfloat16)
            for offsets in order
        ],
        name="pack_cache",
        cost_estimate=pl.CostEstimate(
            flops=0, bytes_accessed=8 * keys.size, transcendentals=0
        ),
        compiler_params=pltpu.CompilerParams(vmem_limit_bytes=PACK_VMEM),
    )(keys, values)


def lay(keys, values):
    turned = jnp.transpose(values.astype(jnp.float32)).astype(jnp.bfloat16)
    ones = jnp.ones((SUM_ROWS, keys.shape[0]), jnp.bfloat16)
    return keys, turned, ones


def lay_own_kernel(plan, k_hbm, v_hbm, slot_hbm, count_hbm, k_out, v_out, mask_ref, *scratch):
    calls, rows = plan
    k_ref, v_ref, slot_ref, count_ref, sems = scratch
    server = lax.axis_index("tok")
    group = slot_ref.shape[0]
    own = lax.rem(server, group)
    start = pl.multiple_of(own * HEAD_SIZE, HEAD_SIZE)
    copies = [
        pltpu.make_async_copy(slot_hbm, slot_ref, sems.at[0]),
        pltpu.make_async_copy(count_hbm, count_ref, sems.at[1]),
        pltpu.make_async_copy(k_hbm.at[:, pl.ds(start, HEAD_SIZE)], k_ref, sems.at[2]),
        pltpu.make_async_copy(v_hbm.at[:, pl.ds(start, HEAD_SIZE)], v_ref, sems.at[3]),
    ]
    for copy in copies:
        copy.start()
    for copy in copies:
        copy.wait()
    for call, displacements in enumerate(calls):
        mask = jnp.int32(0)
        for i, displacement in enumerate(displacements):
            block = ((server ^ displacement) * rows) // QBLK
            for k in range(group):
                key_block = server ^ k
                slot = slot_ref[own, block, key_block]
                active = (slot >= 0) & (slot < count_ref[own, key_block])
                mask = mask | (active.astype(jnp.int32) << (i * group + k))
        mask_ref[call] = jnp.full(mask_ref.shape[1:], mask, jnp.int32)
    k_out[...], v_out[:HEAD_SIZE, :], v_out[HEAD_SIZE:, :] = lay(k_ref[...], v_ref[...])


def lay_own(keys, values, task_slot, task_count, calls, rows):
    n = keys.shape[0]
    hbm = pl.BlockSpec(memory_space=pltpu.HBM)
    return pl.pallas_call(
        functools.partial(lay_own_kernel, (calls, rows)),
        out_shape=[
            jax.ShapeDtypeStruct((n, HEAD_SIZE), jnp.bfloat16),
            jax.ShapeDtypeStruct((HEAD_SIZE + SUM_ROWS, n), jnp.bfloat16),
            jax.ShapeDtypeStruct((len(calls), 8, HEAD_SIZE), jnp.int32),
        ],
        in_specs=[hbm] * 4,
        scratch_shapes=[
            pltpu.VMEM((n, HEAD_SIZE), keys.dtype),
            pltpu.VMEM((n, HEAD_SIZE), values.dtype),
            pltpu.SMEM(task_slot.shape, task_slot.dtype),
            pltpu.SMEM(task_count.shape, task_count.dtype),
            pltpu.SemaphoreType.DMA((4,)),
        ],
        name="lay_own",
        cost_estimate=pl.CostEstimate(
            flops=0, bytes_accessed=8 * n * HEAD_SIZE, transcendentals=0
        ),
        compiler_params=pltpu.CompilerParams(vmem_limit_bytes=LAY_VMEM),
    )(keys, values, task_slot, task_count)


def lay_cache_kernel(keys, counts, k_own, v_own, *refs):
    *in_refs, k_ref, v_ref = refs
    k_ref[0] = k_own[...]
    v_ref[0] = v_own[...]
    at = 1
    for ref, count in zip(in_refs, counts):
        for i in range(count):
            row = 2 * i * keys
            k_ref[at], v_ref[at, :HEAD_SIZE, :], v_ref[at, HEAD_SIZE:, :] = lay(
                ref[row : row + keys, :], ref[row + keys : row + 2 * keys, :]
            )
            at += 1


def lay_cache(k_own, v_own, pieces, counts):
    group = 1 + sum(counts)
    keys = k_own.shape[0]
    return pl.pallas_call(
        functools.partial(lay_cache_kernel, keys, counts),
        out_shape=[
            jax.ShapeDtypeStruct((group,) + k_own.shape, jnp.bfloat16),
            jax.ShapeDtypeStruct((group,) + v_own.shape, jnp.bfloat16),
        ],
        name="lay_cache",
        cost_estimate=pl.CostEstimate(
            flops=0, bytes_accessed=8 * group * keys * HEAD_SIZE, transcendentals=0
        ),
        compiler_params=pltpu.CompilerParams(vmem_limit_bytes=8 << 20),
    )(k_own, v_own, *pieces)


def split_stat(stat, width):
    high = stat.astype(jnp.bfloat16).astype(jnp.float32)
    rest = stat - high
    middle = rest.astype(jnp.bfloat16).astype(jnp.float32)
    low = rest - middle
    row = lax.broadcasted_iota(jnp.int32, (STAT_ROWS, width), 0)
    spread = jnp.where(row == 0, high, jnp.where(row == 1, middle, jnp.where(row == 2, low, 0.0)))
    return spread.astype(jnp.bfloat16)


def join_stat(ref):
    stat = ref[HEAD_SIZE : HEAD_SIZE + STAT_ROWS, :].astype(jnp.float32)
    return stat[0:1] + stat[1:2] + stat[2:3]


def attention_kernel(plan, mask_ref, *refs):
    which, widths, slab = plan
    n_chunks = sum(widths)
    n_in = len(widths)
    q_in_refs = refs[:n_in]
    k_ref, v_ref, _, out_ref = refs[n_in : n_in + 4]
    list_ref, q_ref, m_ref, acc_ref, *slots = refs[n_in + 4 :]
    group, _ = k_ref.shape[:2]
    width = q_ref.shape[1]
    scale = HEAD_SIZE ** (-0.5) * LOG2E

    mask = mask_ref[which, 0, 0]
    found = jnp.int32(0)
    for i in range(n_chunks * group):
        list_ref[found] = i
        found = found + ((mask >> i) & 1)

    at = 0
    for q_in_ref, n in zip(q_in_refs, widths):
        for i in range(n):
            q_ref[at + i] = q_in_ref[i * width : (i + 1) * width, :]
        at += n
    m_ref[...] = jnp.full_like(m_ref, neg_fill)
    acc_ref[...] = jnp.zeros_like(acc_ref)

    def pair(i):
        entry = list_ref[i]
        return entry // group, lax.rem(entry, group)

    def score(i, slot):
        chunk, k = pair(i)
        s_ref, top_ref, fade_ref = slot
        for c in range(0, width, slab):
            scores = lax.dot_general(
                k_ref[k],
                q_ref[chunk, c : c + slab, :],
                (((1,), (1,)), ((), ())),
                preferred_element_type=jnp.float32,
            )
            s_ref[:, c : c + slab] = scores
            old = m_ref[chunk, :, c : c + slab]
            new = jnp.maximum(old, jnp.max(scores, axis=0, keepdims=True))
            m_ref[chunk, :, c : c + slab] = new
            top_ref[:, c : c + slab] = new
            fade_ref[:, c : c + slab] = jnp.exp2((old - new) * scale)

    def weigh(i, slot):
        chunk, k = pair(i)
        s_ref, top_ref, fade_ref = slot
        for c in range(0, width, slab):
            p = jnp.exp2((s_ref[:, c : c + slab] - top_ref[0:1, c : c + slab]) * scale)
            product = jnp.dot(
                v_ref[k], p.astype(jnp.bfloat16), preferred_element_type=jnp.float32
            )
            acc_ref[chunk, :, c : c + slab] = (
                acc_ref[chunk, :, c : c + slab] * fade_ref[0:1, c : c + slab] + product
            )

    even, odd = slots[:3], slots[3:]

    @pl.when(found > 0)
    def _():
        score(0, even)

    def step(i, here, there):
        @pl.when(i + 1 < found)
        def _():
            score(i + 1, there)
            weigh(i, here)

        @pl.when(i + 1 == found)
        def _():
            weigh(i, here)

    def two(j, carry):
        step(2 * j, even, odd)
        step(2 * j + 1, odd, even)
        return carry

    lax.fori_loop(0, (found + 1) // 2, two, 0)

    for i in range(n_chunks):
        total = acc_ref[i, HEAD_SIZE : HEAD_SIZE + 1, :]
        seen = total > 0.0
        safe = jnp.where(seen, total, 1.0)
        stat = jnp.where(seen, m_ref[i, 0:1, :] * scale + jnp.log2(safe), neg_fill)
        lanes = slice(i * width, (i + 1) * width)
        out_ref[:HEAD_SIZE, lanes] = (acc_ref[i, :HEAD_SIZE, :] * (1.0 / safe)).astype(jnp.bfloat16)
        out_ref[HEAD_SIZE:, lanes] = split_stat(stat, width)


def attention(chunks, which, cache, masks, width, after):
    k, v = cache
    group, keys = k.shape[:2]
    widths = tuple(chunk.shape[0] // width for chunk in chunks)
    n = sum(widths)
    vmem = pl.BlockSpec(memory_space=pltpu.VMEM)
    slot = [
        pltpu.VMEM((keys, width), jnp.float32),
        pltpu.VMEM((8, width), jnp.float32),
        pltpu.VMEM((8, width), jnp.float32),
    ]
    return pl.pallas_call(
        functools.partial(attention_kernel, (which, widths, min(256, width))),
        out_shape=jax.ShapeDtypeStruct((HEAD_SIZE + STAT_ROWS, n * width), jnp.bfloat16),
        in_specs=[vmem] * (len(chunks) + 3)
        + [pl.BlockSpec(memory_space=pl.ANY)],
        out_specs=vmem,
        scratch_shapes=[
            pltpu.SMEM((n * group + 1,), jnp.int32),
            pltpu.VMEM((n, width, HEAD_SIZE), jnp.bfloat16),
            pltpu.VMEM((n, 8, width), jnp.float32),
            pltpu.VMEM((n, HEAD_SIZE + SUM_ROWS, width), jnp.float32),
        ]
        + slot
        + slot,
        name="attention",
        cost_estimate=pl.CostEstimate(
            flops=4 * n * group * keys * width * HEAD_SIZE,
            bytes_accessed=4 * n * width * HEAD_SIZE + 4 * group * keys * HEAD_SIZE,
            transcendentals=n * group * keys * width,
        ),
        compiler_params=pltpu.CompilerParams(vmem_limit_bytes=16 << 20),
    )(masks, *chunks, k, v, after)


def merge_kernel(spans, keep_stat, *refs):
    in_refs, out_refs = refs[: len(spans)], refs[len(spans) :]
    views = [ref.at[:, lanes] for ref, lanes in zip(in_refs, spans)]
    stats = [join_stat(ref) for ref in views]
    largest = functools.reduce(jnp.maximum, stats)
    weights = [jnp.exp2(stat - largest) for stat in stats]
    total = functools.reduce(jnp.add, weights)
    inverse = 1.0 / total
    value = functools.reduce(
        jnp.add,
        [
            (weight * inverse) * ref[:HEAD_SIZE, :].astype(jnp.float32)
            for weight, ref in zip(weights, views)
        ],
    ).astype(jnp.bfloat16)
    stat = largest + jnp.log2(total)
    part = out_refs[0].shape[1]
    for i, out_ref in enumerate(out_refs):
        lanes = slice(i * part, (i + 1) * part)
        out_ref[:HEAD_SIZE, :] = value[:, lanes]
        if keep_stat:
            out_ref[HEAD_SIZE:, :] = split_stat(stat[:, lanes], part)


def merge(messages, parts, keep_stat=True):
    arrays = [array for array, _, _ in messages]
    height = arrays[0].shape[0] if keep_stat else HEAD_SIZE
    width = arrays[0].shape[1] // messages[0][2]
    spans = tuple(slice(i * width, (i + 1) * width) for _, i, _ in messages)
    size = len(messages) * height * width
    return pl.pallas_call(
        functools.partial(merge_kernel, spans, keep_stat),
        out_shape=[jax.ShapeDtypeStruct((height, width // parts), jnp.bfloat16)] * parts,
        name="merge" if keep_stat else "finish",
        cost_estimate=pl.CostEstimate(flops=4 * size, bytes_accessed=4 * size, transcendentals=0),
        compiler_params=pltpu.CompilerParams(vmem_limit_bytes=8 << 20),
    )(*arrays)


def gather_kernel(rows, *refs):
    *piece_refs, out_ref = refs
    group = len(piece_refs)
    own = lax.rem(lax.axis_index("tok"), group)
    per = piece_refs[0].shape[1] // rows
    for offset in range(group):
        for j in range(per):
            block = jnp.transpose(
                piece_refs[offset][:, j * rows : (j + 1) * rows].astype(jnp.float32)
            )
            start = pl.multiple_of(((own ^ offset) * per + j) * HEAD_SIZE, HEAD_SIZE)
            out_ref[:, pl.ds(start, HEAD_SIZE)] = block.astype(jnp.bfloat16)


def gather(pieces, rows):
    width = sum(piece.shape[1] for piece in pieces) // rows * HEAD_SIZE
    return pl.pallas_call(
        functools.partial(gather_kernel, rows),
        out_shape=jax.ShapeDtypeStruct((rows, width), jnp.bfloat16),
        name="gather",
        cost_estimate=pl.CostEstimate(
            flops=0, bytes_accessed=4 * rows * width, transcendentals=0
        ),
        compiler_params=pltpu.CompilerParams(vmem_limit_bytes=4 << 20),
    )(*pieces)


def project_kernel(half, start, left_ref, w_ref, out_ref):
    columns = out_ref.shape[1]
    if half is not None:
        start = (lax.axis_index("head") ^ half) * (w_ref.shape[1] // 2) + start
    start = pl.multiple_of(start, HEAD_SIZE)
    out_ref[...] = jnp.dot(
        left_ref[...], w_ref[:, pl.ds(start, columns)], preferred_element_type=jnp.float32
    ).astype(out_ref.dtype)


def project(left, out_weight, half, start, columns, kind):
    rows, depth = left.shape
    return pl.pallas_call(
        functools.partial(project_kernel, half, start),
        out_shape=jax.ShapeDtypeStruct((rows, columns), kind),
        in_specs=[pl.BlockSpec(memory_space=pltpu.VMEM)] * 2,
        out_specs=pl.BlockSpec(memory_space=pltpu.VMEM),
        name="project",
        cost_estimate=pl.CostEstimate(
            flops=2 * rows * depth * columns,
            bytes_accessed=2 * depth * columns,
            transcendentals=0,
        ),
        compiler_params=pltpu.CompilerParams(vmem_limit_bytes=24 << 20),
    )(left, out_weight)


def swap(x, bits, servers):
    return lax.ppermute(x, "tok", [(i, i ^ bits) for i in range(servers)])


def attend_grouped(queries, keys, values, task_slot, task_count, move):
    core, column, near, far = 1, 2, 4, 8
    rows, n_keys = queries.shape[0], keys.shape[0]
    q_per_kv = HEADS // KVH
    part = q_per_kv * rows
    width = 2 * part

    keep, give = pack_queries(queries, 4, ((0, 2), (1, 3)))
    theirs, away = pack_cache(keys, values, 4, ((1,), (2, 3)))
    got = move(give, core)
    own = jnp.concatenate([keep[:part], got[:part]], axis=0)
    other = jnp.concatenate([keep[part:], got[part:]], axis=0)
    own_far = move(own, far)
    other_far = move(other, far | column)
    other_own = move(other, column)
    across = move(away, column)
    beside = move(theirs, core)
    beyond = move(across[2 * n_keys :], core)
    both_near = move(jnp.concatenate([own, other_own], axis=0), near)
    own_last = move(own_far, near)
    other_last = move(other_far, near)

    calls = ((0, column), (near, near | column), (far, far | column), (far | near | column,), (far | near,))
    k_own, v_own, masks = lay_own(keys, values, task_slot, task_count, calls, rows)
    cache = lay_cache(k_own, v_own, [beside, across, beyond], (1, 1, 1))

    def call(chunks, which, after):
        return attention(chunks, which, cache, masks, width, after)

    part_own = call([own, other_own], 0, masks)
    part_near = call([both_near], 1, part_own)
    part_far = call([own_far, other_far], 2, part_near)
    part_last_b = call([other_last], 3, part_far)
    part_last_a = call([own_last], 4, part_last_b)

    last_b = move(part_last_b, near)
    last_a = move(part_last_a, near)
    near_back = move(part_near, near)
    (far_b,) = merge([(part_far, 1, 2), (last_b, 0, 1)], 1)
    far_b = move(far_b, far | column)
    (far_a,) = merge([(part_far, 0, 2), (last_a, 0, 1)], 1)
    far_a = move(far_a, far)
    (here_b,) = merge([(part_own, 1, 2), (near_back, 1, 2)], 1)
    here_b = move(here_b, column)
    b_own, b_other = merge([(here_b, 0, 1), (far_b, 0, 1)], 2, False)
    b_other = move(b_other, core)
    a_own, a_other = merge([(part_own, 0, 2), (near_back, 0, 2), (far_a, 0, 1)], 2, False)
    a_other = move(a_other, core)
    return [a_own, a_other, b_own, b_other]


def attend_general(queries, keys, values, task_slot, task_count, move, servers):
    assert task_slot.shape[0] == 1
    rows = queries.shape[0]
    width = HEADS // KVH * rows
    step = min(4, servers)
    calls = tuple(tuple(range(i, i + step)) for i in range(0, servers, step))
    (own,) = pack_queries(queries, 1, ((0,),))
    k_own, v_own, masks = lay_own(keys, values, task_slot, task_count, calls, rows)
    cache = lay_cache(k_own, v_own, [], ())
    held = {0: own}
    bit = servers // 2
    while bit:
        held.update({d ^ bit: move(chunk, bit) for d, chunk in held.items()})
        bit //= 2
    partial = {}
    for which, call in enumerate(calls):
        result = attention([held[d] for d in call], which, cache, masks, width, masks)
        for j, d in enumerate(call):
            partial[d] = [result[:, j * width : (j + 1) * width]]
    bit = 1
    while bit < servers:
        for d in sorted(partial, reverse=True):
            if d & bit:
                messages = partial.pop(d)
                message = messages[0] if len(messages) == 1 else merge([(m, 0, 1) for m in messages], 1)[0]
                partial[d ^ bit].append(move(message, bit))
        bit *= 2
    return merge([(m, 0, 1) for m in partial[0]], 1, False)


def on_device(queries, keys, values, out_weight, task_slot, task_count):
    servers = lax.axis_size("tok")
    heads = lax.axis_size("head")
    rows = queries.shape[0]
    group = task_slot.shape[0]
    move = functools.partial(swap, servers=servers)
    if group == 4 and servers == 16:
        attended = attend_grouped(queries, keys, values, task_slot, task_count, move)
    else:
        attended = attend_general(queries, keys, values, task_slot, task_count, move, servers)
    left = gather(attended, rows)

    columns = out_weight.shape[1] // heads
    if heads == 2:
        return exchange_halves(left, out_weight, columns)
    share = project(left, out_weight, None, 0, out_weight.shape[1], jnp.bfloat16)
    return lax.psum_scatter(share, "head", scatter_dimension=1, tiled=True)


def exchange_halves(left, out_weight, columns):
    piece = columns // 2
    arrived = []
    for i in range(2):
        part = project(left, out_weight, 1, i * piece, piece, jnp.bfloat16)
        arrived.append(lax.ppermute(part, "head", [(0, 1), (1, 0)]))
    here = project(left, out_weight, 0, 0, columns, jnp.float32)
    return (here + jnp.concatenate(arrived, axis=1).astype(jnp.float32)).astype(jnp.bfloat16)


def solution(mesh):
    placed = (
        P("tok", "head"),
        P("tok", "head"),
        P("tok", "head"),
        P("head", None),
        P("head", None, None),
        P("head", None),
    )
    return jax.shard_map(
        on_device, mesh=mesh, in_specs=placed, out_specs=P("tok", "head"), check_vma=False
    )
```

```python
import functools
import math

import jax
import jax.numpy as jnp
from jax import lax
from jax.experimental import pallas as pl
from jax.experimental.pallas import tpu as pltpu
from jax.sharding import PartitionSpec as P


HEADS = 32
KVH = 8
HEAD_SIZE = 128
QBLK = 128

theta_base = 500000.0
neg_fill = -1e30
LOG2E = math.log2(math.e)
STAT_ROWS = 8
SUM_ROWS = 16
PACK_VMEM = 47 << 20
LAY_VMEM = 8 << 20


def rotary_tables(rows, first_row):
    half = HEAD_SIZE // 2
    frequency = theta_base ** (-(jnp.arange(half, dtype=jnp.float32) * (2.0 / HEAD_SIZE)))
    places = (first_row + jnp.arange(rows, dtype=jnp.int32)).astype(jnp.float32)
    angles = places[:, None] * frequency[None, :]
    cosine = jnp.cos(angles)
    sine = jnp.sin(angles)
    return (
        jnp.concatenate([cosine, cosine], axis=1),
        jnp.concatenate([-sine, sine], axis=1),
    )


def pack_queries_kernel(order, q_per_kv, group, cos_ref, sin_ref, q_ref, *out_refs):
    own = lax.rem(lax.axis_index("tok"), group)
    rows = q_ref.shape[0]
    cosine = cos_ref[...]
    sine = sin_ref[...]
    for offsets, out_ref in zip(order, out_refs):
        for at, offset in enumerate(offsets):
            head = own ^ offset
            for j in range(q_per_kv):
                start = pl.multiple_of((head * q_per_kv + j) * HEAD_SIZE, HEAD_SIZE)
                x = q_ref[:, pl.ds(start, HEAD_SIZE)].astype(jnp.float32)
                turned = pltpu.roll(x, HEAD_SIZE // 2, 1)
                row = (at * q_per_kv + j) * rows
                out_ref[row : row + rows, :] = (x * cosine + turned * sine).astype(jnp.bfloat16)


def pack_queries(queries, group, order):
    rows = queries.shape[0]
    q_per_kv = HEADS // KVH
    cosine, sine = rotary_tables(rows, lax.axis_index("tok") * rows)
    return pl.pallas_call(
        functools.partial(pack_queries_kernel, order, q_per_kv, group),
        out_shape=[
            jax.ShapeDtypeStruct((len(offsets) * q_per_kv * rows, HEAD_SIZE), jnp.bfloat16)
            for offsets in order
        ],
        name="pack_queries",
        cost_estimate=pl.CostEstimate(
            flops=6 * queries.size, bytes_accessed=4 * queries.size, transcendentals=0
        ),
        compiler_params=pltpu.CompilerParams(vmem_limit_bytes=PACK_VMEM),
    )(cosine, sine, queries)


def pack_cache_kernel(order, group, k_ref, v_ref, *out_refs):
    own = lax.rem(lax.axis_index("tok"), group)
    keys = k_ref.shape[0]
    for offsets, out_ref in zip(order, out_refs):
        for at, offset in enumerate(offsets):
            start = pl.multiple_of((own ^ offset) * HEAD_SIZE, HEAD_SIZE)
            row = 2 * at * keys
            out_ref[row : row + keys, :] = k_ref[:, pl.ds(start, HEAD_SIZE)]
            out_ref[row + keys : row + 2 * keys, :] = v_ref[:, pl.ds(start, HEAD_SIZE)]


def pack_cache(keys, values, group, order):
    return pl.pallas_call(
        functools.partial(pack_cache_kernel, order, group),
        out_shape=[
            jax.ShapeDtypeStruct((len(offsets) * 2 * keys.shape[0], HEAD_SIZE), jnp.bfloat16)
            for offsets in order
        ],
        name="pack_cache",
        cost_estimate=pl.CostEstimate(
            flops=0, bytes_accessed=8 * keys.size, transcendentals=0
        ),
        compiler_params=pltpu.CompilerParams(vmem_limit_bytes=PACK_VMEM),
    )(keys, values)


def lay(keys, values):
    turned = jnp.transpose(values.astype(jnp.float32)).astype(jnp.bfloat16)
    ones = jnp.ones((SUM_ROWS, keys.shape[0]), jnp.bfloat16)
    return keys, turned, ones


def lay_own_kernel(plan, k_hbm, v_hbm, slot_hbm, count_hbm, k_out, v_out, mask_ref, *scratch):
    calls, rows = plan
    k_ref, v_ref, slot_ref, count_ref, sems = scratch
    server = lax.axis_index("tok")
    group = slot_ref.shape[0]
    own = lax.rem(server, group)
    start = pl.multiple_of(own * HEAD_SIZE, HEAD_SIZE)
    copies = [
        pltpu.make_async_copy(slot_hbm, slot_ref, sems.at[0]),
        pltpu.make_async_copy(count_hbm, count_ref, sems.at[1]),
        pltpu.make_async_copy(k_hbm.at[:, pl.ds(start, HEAD_SIZE)], k_ref, sems.at[2]),
        pltpu.make_async_copy(v_hbm.at[:, pl.ds(start, HEAD_SIZE)], v_ref, sems.at[3]),
    ]
    for copy in copies:
        copy.start()
    for copy in copies:
        copy.wait()
    for call, displacements in enumerate(calls):
        mask = jnp.int32(0)
        for i, displacement in enumerate(displacements):
            block = ((server ^ displacement) * rows) // QBLK
            for k in range(group):
                key_block = server ^ k
                slot = slot_ref[own, block, key_block]
                active = (slot >= 0) & (slot < count_ref[own, key_block])
                mask = mask | (active.astype(jnp.int32) << (i * group + k))
        mask_ref[call] = jnp.full(mask_ref.shape[1:], mask, jnp.int32)
    k_out[...], v_out[:HEAD_SIZE, :], v_out[HEAD_SIZE:, :] = lay(k_ref[...], v_ref[...])


def lay_own(keys, values, task_slot, task_count, calls, rows):
    n = keys.shape[0]
    hbm = pl.BlockSpec(memory_space=pltpu.HBM)
    return pl.pallas_call(
        functools.partial(lay_own_kernel, (calls, rows)),
        out_shape=[
            jax.ShapeDtypeStruct((n, HEAD_SIZE), jnp.bfloat16),
            jax.ShapeDtypeStruct((HEAD_SIZE + SUM_ROWS, n), jnp.bfloat16),
            jax.ShapeDtypeStruct((len(calls), 8, HEAD_SIZE), jnp.int32),
        ],
        in_specs=[hbm] * 4,
        scratch_shapes=[
            pltpu.VMEM((n, HEAD_SIZE), keys.dtype),
            pltpu.VMEM((n, HEAD_SIZE), values.dtype),
            pltpu.SMEM(task_slot.shape, task_slot.dtype),
            pltpu.SMEM(task_count.shape, task_count.dtype),
            pltpu.SemaphoreType.DMA((4,)),
        ],
        name="lay_own",
        cost_estimate=pl.CostEstimate(
            flops=0, bytes_accessed=8 * n * HEAD_SIZE, transcendentals=0
        ),
        compiler_params=pltpu.CompilerParams(vmem_limit_bytes=LAY_VMEM),
    )(keys, values, task_slot, task_count)


def lay_cache_kernel(keys, counts, k_own, v_own, *refs):
    *in_refs, k_ref, v_ref = refs
    k_ref[0] = k_own[...]
    v_ref[0] = v_own[...]
    at = 1
    for ref, count in zip(in_refs, counts):
        for i in range(count):
            row = 2 * i * keys
            k_ref[at], v_ref[at, :HEAD_SIZE, :], v_ref[at, HEAD_SIZE:, :] = lay(
                ref[row : row + keys, :], ref[row + keys : row + 2 * keys, :]
            )
            at += 1


def lay_cache(k_own, v_own, pieces, counts):
    group = 1 + sum(counts)
    keys = k_own.shape[0]
    return pl.pallas_call(
        functools.partial(lay_cache_kernel, keys, counts),
        out_shape=[
            jax.ShapeDtypeStruct((group,) + k_own.shape, jnp.bfloat16),
            jax.ShapeDtypeStruct((group,) + v_own.shape, jnp.bfloat16),
        ],
        name="lay_cache",
        cost_estimate=pl.CostEstimate(
            flops=0, bytes_accessed=8 * group * keys * HEAD_SIZE, transcendentals=0
        ),
        compiler_params=pltpu.CompilerParams(vmem_limit_bytes=8 << 20),
    )(k_own, v_own, *pieces)


def split_stat(stat, width):
    high = stat.astype(jnp.bfloat16).astype(jnp.float32)
    rest = stat - high
    middle = rest.astype(jnp.bfloat16).astype(jnp.float32)
    low = rest - middle
    row = lax.broadcasted_iota(jnp.int32, (STAT_ROWS, width), 0)
    spread = jnp.where(row == 0, high, jnp.where(row == 1, middle, jnp.where(row == 2, low, 0.0)))
    return spread.astype(jnp.bfloat16)


def join_stat(ref):
    stat = ref[HEAD_SIZE : HEAD_SIZE + STAT_ROWS, :].astype(jnp.float32)
    return stat[0:1] + stat[1:2] + stat[2:3]


def attention_kernel(plan, mask_ref, *refs):
    which, widths, slab = plan
    n_chunks = sum(widths)
    n_in = len(widths)
    q_in_refs = refs[:n_in]
    k_ref, v_ref, _ = refs[n_in : n_in + 3]
    out_refs = refs[n_in + 3 : n_in + 3 + n_chunks]
    list_ref, q_ref, m_ref, acc_ref, *slots = refs[n_in + 3 + n_chunks :]
    group, _ = k_ref.shape[:2]
    width = q_ref.shape[1]
    scale = HEAD_SIZE ** (-0.5) * LOG2E

    mask = mask_ref[which, 0, 0]
    found = jnp.int32(0)
    for i in range(n_chunks * group):
        list_ref[found] = i
        found = found + ((mask >> i) & 1)

    at = 0
    for q_in_ref, n in zip(q_in_refs, widths):
        for i in range(n):
            q_ref[at + i] = q_in_ref[i * width : (i + 1) * width, :]
        at += n
    m_ref[...] = jnp.full_like(m_ref, neg_fill)
    acc_ref[...] = jnp.zeros_like(acc_ref)

    def pair(i):
        entry = list_ref[i]
        return entry // group, lax.rem(entry, group)

    def score(i, slot):
        chunk, k = pair(i)
        s_ref, top_ref, fade_ref = slot
        for c in range(0, width, slab):
            scores = lax.dot_general(
                k_ref[k],
                q_ref[chunk, c : c + slab, :],
                (((1,), (1,)), ((), ())),
                preferred_element_type=jnp.float32,
            )
            s_ref[:, c : c + slab] = scores
            old = m_ref[chunk, :, c : c + slab]
            new = jnp.maximum(old, jnp.max(scores, axis=0, keepdims=True))
            m_ref[chunk, :, c : c + slab] = new
            top_ref[:, c : c + slab] = new
            fade_ref[:, c : c + slab] = jnp.exp2((old - new) * scale)

    def weigh(i, slot):
        chunk, k = pair(i)
        s_ref, top_ref, fade_ref = slot
        for c in range(0, width, slab):
            p = jnp.exp2((s_ref[:, c : c + slab] - top_ref[0:1, c : c + slab]) * scale)
            product = jnp.dot(
                v_ref[k], p.astype(jnp.bfloat16), preferred_element_type=jnp.float32
            )
            acc_ref[chunk, :, c : c + slab] = (
                acc_ref[chunk, :, c : c + slab] * fade_ref[0:1, c : c + slab] + product
            )

    even, odd = slots[:3], slots[3:]

    @pl.when(found > 0)
    def _():
        score(0, even)

    def step(i, here, there):
        @pl.when(i + 1 < found)
        def _():
            score(i + 1, there)
            weigh(i, here)

        @pl.when(i + 1 == found)
        def _():
            weigh(i, here)

    def two(j, carry):
        step(2 * j, even, odd)
        step(2 * j + 1, odd, even)
        return carry

    lax.fori_loop(0, (found + 1) // 2, two, 0)

    for i in range(n_chunks):
        total = acc_ref[i, HEAD_SIZE : HEAD_SIZE + 1, :]
        seen = total > 0.0
        safe = jnp.where(seen, total, 1.0)
        stat = jnp.where(seen, m_ref[i, 0:1, :] * scale + jnp.log2(safe), neg_fill)
        out_refs[i][:HEAD_SIZE, :] = (acc_ref[i, :HEAD_SIZE, :] * (1.0 / safe)).astype(jnp.bfloat16)
        out_refs[i][HEAD_SIZE:, :] = split_stat(stat, width)


def attention(chunks, which, cache, masks, width, after):
    k, v = cache
    group, keys = k.shape[:2]
    widths = tuple(chunk.shape[0] // width for chunk in chunks)
    n = sum(widths)
    vmem = pl.BlockSpec(memory_space=pltpu.VMEM)
    slot = [
        pltpu.VMEM((keys, width), jnp.float32),
        pltpu.VMEM((8, width), jnp.float32),
        pltpu.VMEM((8, width), jnp.float32),
    ]
    return pl.pallas_call(
        functools.partial(attention_kernel, (which, widths, min(256, width))),
        out_shape=[jax.ShapeDtypeStruct((HEAD_SIZE + STAT_ROWS, width), jnp.bfloat16)] * n,
        in_specs=[vmem] * (len(chunks) + 3)
        + [pl.BlockSpec(memory_space=pl.ANY)],
        out_specs=[vmem] * n,
        scratch_shapes=[
            pltpu.SMEM((n * group + 1,), jnp.int32),
            pltpu.VMEM((n, width, HEAD_SIZE), jnp.bfloat16),
            pltpu.VMEM((n, 8, width), jnp.float32),
            pltpu.VMEM((n, HEAD_SIZE + SUM_ROWS, width), jnp.float32),
        ]
        + slot
        + slot,
        name="attention",
        cost_estimate=pl.CostEstimate(
            flops=4 * n * group * keys * width * HEAD_SIZE,
            bytes_accessed=4 * n * width * HEAD_SIZE + 4 * group * keys * HEAD_SIZE,
            transcendentals=n * group * keys * width,
        ),
        compiler_params=pltpu.CompilerParams(vmem_limit_bytes=16 << 20),
    )(masks, *chunks, k, v, after)


def merge_kernel(n_in, keep_stat, *refs):
    in_refs, out_refs = refs[:n_in], refs[n_in:]
    stats = [join_stat(ref) for ref in in_refs]
    largest = functools.reduce(jnp.maximum, stats)
    weights = [jnp.exp2(stat - largest) for stat in stats]
    total = functools.reduce(jnp.add, weights)
    inverse = 1.0 / total
    value = functools.reduce(
        jnp.add,
        [
            (weight * inverse) * ref[:HEAD_SIZE, :].astype(jnp.float32)
            for weight, ref in zip(weights, in_refs)
        ],
    ).astype(jnp.bfloat16)
    stat = largest + jnp.log2(total)
    part = out_refs[0].shape[1]
    for i, out_ref in enumerate(out_refs):
        lanes = slice(i * part, (i + 1) * part)
        out_ref[:HEAD_SIZE, :] = value[:, lanes]
        if keep_stat:
            out_ref[HEAD_SIZE:, :] = split_stat(stat[:, lanes], part)


def merge(messages, parts, keep_stat=True):
    height, width = messages[0].shape
    height = height if keep_stat else HEAD_SIZE
    size = len(messages) * height * width
    return pl.pallas_call(
        functools.partial(merge_kernel, len(messages), keep_stat),
        out_shape=[jax.ShapeDtypeStruct((height, width // parts), jnp.bfloat16)] * parts,
        name="merge" if keep_stat else "finish",
        cost_estimate=pl.CostEstimate(flops=4 * size, bytes_accessed=4 * size, transcendentals=0),
        compiler_params=pltpu.CompilerParams(vmem_limit_bytes=8 << 20),
    )(*messages)


def gather_kernel(rows, *refs):
    *piece_refs, out_ref = refs
    group = len(piece_refs)
    own = lax.rem(lax.axis_index("tok"), group)
    per = piece_refs[0].shape[1] // rows
    for offset in range(group):
        for j in range(per):
            block = jnp.transpose(
                piece_refs[offset][:, j * rows : (j + 1) * rows].astype(jnp.float32)
            )
            start = pl.multiple_of(((own ^ offset) * per + j) * HEAD_SIZE, HEAD_SIZE)
            out_ref[:, pl.ds(start, HEAD_SIZE)] = block.astype(jnp.bfloat16)


def gather(pieces, rows):
    width = sum(piece.shape[1] for piece in pieces) // rows * HEAD_SIZE
    return pl.pallas_call(
        functools.partial(gather_kernel, rows),
        out_shape=jax.ShapeDtypeStruct((rows, width), jnp.bfloat16),
        name="gather",
        cost_estimate=pl.CostEstimate(
            flops=0, bytes_accessed=4 * rows * width, transcendentals=0
        ),
        compiler_params=pltpu.CompilerParams(vmem_limit_bytes=4 << 20),
    )(*pieces)


def project_kernel(half, start, left_ref, w_ref, out_ref):
    columns = out_ref.shape[1]
    if half is not None:
        start = (lax.axis_index("head") ^ half) * (w_ref.shape[1] // 2) + start
    start = pl.multiple_of(start, HEAD_SIZE)
    out_ref[...] = jnp.dot(
        left_ref[...], w_ref[:, pl.ds(start, columns)], preferred_element_type=jnp.float32
    ).astype(out_ref.dtype)


def project(left, out_weight, half, start, columns, kind):
    rows, depth = left.shape
    return pl.pallas_call(
        functools.partial(project_kernel, half, start),
        out_shape=jax.ShapeDtypeStruct((rows, columns), kind),
        in_specs=[pl.BlockSpec(memory_space=pltpu.VMEM)] * 2,
        out_specs=pl.BlockSpec(memory_space=pltpu.VMEM),
        name="project",
        cost_estimate=pl.CostEstimate(
            flops=2 * rows * depth * columns,
            bytes_accessed=2 * depth * columns,
            transcendentals=0,
        ),
        compiler_params=pltpu.CompilerParams(vmem_limit_bytes=24 << 20),
    )(left, out_weight)


def swap(x, bits, servers):
    return lax.ppermute(x, "tok", [(i, i ^ bits) for i in range(servers)])


def attend_grouped(queries, keys, values, task_slot, task_count, move):
    core, column, near, far = 1, 2, 4, 8
    rows, n_keys = queries.shape[0], keys.shape[0]
    q_per_kv = HEADS // KVH
    part = q_per_kv * rows
    width = 2 * part

    keep, give = pack_queries(queries, 4, ((0, 2), (1, 3)))
    theirs, away = pack_cache(keys, values, 4, ((1,), (2, 3)))
    got = move(give, core)
    own = jnp.concatenate([keep[:part], got[:part]], axis=0)
    other = jnp.concatenate([keep[part:], got[part:]], axis=0)
    own_far = move(own, far)
    other_far = move(other, far | column)
    other_own = move(other, column)
    across = move(away, column)
    beside = move(theirs, core)
    beyond = move(across[2 * n_keys :], core)
    both_near = move(jnp.concatenate([own, other_own], axis=0), near)
    own_last = move(own_far, near)
    other_last = move(other_far, near)

    calls = ((0, column), (near, near | column), (far, far | column), (far | near | column,), (far | near,))
    k_own, v_own, masks = lay_own(keys, values, task_slot, task_count, calls, rows)
    cache = lay_cache(k_own, v_own, [beside, across, beyond], (1, 1, 1))

    def call(chunks, which, after):
        return attention(chunks, which, cache, masks, width, after)

    own_a, own_b = call([own, other_own], 0, masks)
    near_a, near_b = call([both_near], 1, own_a)
    far_a, far_b = call([own_far, other_far], 2, near_a)
    (last_b,) = call([other_last], 3, far_a)
    (last_a,) = call([own_last], 4, last_b)

    near_b = move(near_b, near | column)
    near_a = move(near_a, near)
    own_b = move(own_b, column)
    last_b = move(last_b, near)
    last_a = move(last_a, near)
    (far_b,) = merge([far_b, last_b], 1)
    far_b = move(far_b, far | column)
    (far_a,) = merge([far_a, last_a], 1)
    far_a = move(far_a, far)
    b_own, b_other = merge([own_b, near_b, far_b], 2, False)
    b_other = move(b_other, core)
    a_own, a_other = merge([own_a, near_a, far_a], 2, False)
    a_other = move(a_other, core)
    return [a_own, a_other, b_own, b_other]


def attend_general(queries, keys, values, task_slot, task_count, move, servers):
    assert task_slot.shape[0] == 1
    rows = queries.shape[0]
    width = HEADS // KVH * rows
    step = min(4, servers)
    calls = tuple(tuple(range(i, i + step)) for i in range(0, servers, step))
    (own,) = pack_queries(queries, 1, ((0,),))
    k_own, v_own, masks = lay_own(keys, values, task_slot, task_count, calls, rows)
    cache = lay_cache(k_own, v_own, [], ())
    held = {0: own}
    bit = servers // 2
    while bit:
        held.update({d ^ bit: move(chunk, bit) for d, chunk in held.items()})
        bit //= 2
    partial = {}
    for which, call in enumerate(calls):
        result = attention([held[d] for d in call], which, cache, masks, width, masks)
        for j, d in enumerate(call):
            partial[d] = [result[j]]
    bit = 1
    while bit < servers:
        for d in sorted(partial, reverse=True):
            if d & bit:
                messages = partial.pop(d)
                message = messages[0] if len(messages) == 1 else merge(messages, 1)[0]
                partial[d ^ bit].append(move(message, bit))
        bit *= 2
    return merge(partial[0], 1, False)


def on_device(queries, keys, values, out_weight, task_slot, task_count):
    servers = lax.axis_size("tok")
    heads = lax.axis_size("head")
    rows = queries.shape[0]
    group = task_slot.shape[0]
    move = functools.partial(swap, servers=servers)
    if group == 4 and servers == 16:
        attended = attend_grouped(queries, keys, values, task_slot, task_count, move)
    else:
        attended = attend_general(queries, keys, values, task_slot, task_count, move, servers)
    left = gather(attended, rows)

    columns = out_weight.shape[1] // heads
    if heads == 2:
        return exchange_halves(left, out_weight, columns)
    share = project(left, out_weight, None, 0, out_weight.shape[1], jnp.bfloat16)
    return lax.psum_scatter(share, "head", scatter_dimension=1, tiled=True)


def exchange_halves(left, out_weight, columns):
    piece = columns // 2
    arrived = []
    for i in range(2):
        part = project(left, out_weight, 1, i * piece, piece, jnp.bfloat16)
        arrived.append(lax.ppermute(part, "head", [(0, 1), (1, 0)]))
    here = project(left, out_weight, 0, 0, columns, jnp.float32)
    return (here + jnp.concatenate(arrived, axis=1).astype(jnp.float32)).astype(jnp.bfloat16)


def solution(mesh):
    placed = (
        P("tok", "head"),
        P("tok", "head"),
        P("tok", "head"),
        P("head", None),
        P("head", None, None),
        P("head", None),
    )
    return jax.shard_map(
        on_device, mesh=mesh, in_specs=placed, out_specs=P("tok", "head"), check_vma=False
    )
```

```python
import functools
import math

import jax
import jax.numpy as jnp
from jax import lax
from jax.experimental import pallas as pl
from jax.experimental.pallas import tpu as pltpu
from jax.sharding import PartitionSpec as P


HEADS = 32
KVH = 8
HEAD_SIZE = 128
QBLK = 128

theta_base = 500000.0
neg_fill = -1e30
LOG2E = math.log2(math.e)
STAT_ROWS = 8
SUM_ROWS = 16
PACK_VMEM = 47 << 20
LAY_VMEM = 8 << 20


def rotary_tables(rows, first_row):
    half = HEAD_SIZE // 2
    frequency = theta_base ** (-(jnp.arange(half, dtype=jnp.float32) * (2.0 / HEAD_SIZE)))
    places = (first_row + jnp.arange(rows, dtype=jnp.int32)).astype(jnp.float32)
    angles = places[:, None] * frequency[None, :]
    cosine = jnp.cos(angles)
    sine = jnp.sin(angles)
    return (
        jnp.concatenate([cosine, cosine], axis=1),
        jnp.concatenate([-sine, sine], axis=1),
    )


def pack_queries_kernel(order, q_per_kv, group, cos_ref, sin_ref, q_ref, *out_refs):
    own = lax.rem(lax.axis_index("tok"), group)
    rows = q_ref.shape[0]
    cosine = cos_ref[...]
    sine = sin_ref[...]
    for offsets, out_ref in zip(order, out_refs):
        for at, offset in enumerate(offsets):
            head = own ^ offset
            for j in range(q_per_kv):
                start = pl.multiple_of((head * q_per_kv + j) * HEAD_SIZE, HEAD_SIZE)
                x = q_ref[:, pl.ds(start, HEAD_SIZE)].astype(jnp.float32)
                turned = pltpu.roll(x, HEAD_SIZE // 2, 1)
                row = (at * q_per_kv + j) * rows
                out_ref[row : row + rows, :] = (x * cosine + turned * sine).astype(jnp.bfloat16)


def pack_queries(queries, group, order):
    rows = queries.shape[0]
    q_per_kv = HEADS // KVH
    cosine, sine = rotary_tables(rows, lax.axis_index("tok") * rows)
    return pl.pallas_call(
        functools.partial(pack_queries_kernel, order, q_per_kv, group),
        out_shape=[
            jax.ShapeDtypeStruct((len(offsets) * q_per_kv * rows, HEAD_SIZE), jnp.bfloat16)
            for offsets in order
        ],
        name="pack_queries",
        cost_estimate=pl.CostEstimate(
            flops=6 * queries.size, bytes_accessed=4 * queries.size, transcendentals=0
        ),
        compiler_params=pltpu.CompilerParams(vmem_limit_bytes=PACK_VMEM),
    )(cosine, sine, queries)


def pack_cache_kernel(order, group, k_ref, v_ref, *out_refs):
    own = lax.rem(lax.axis_index("tok"), group)
    keys = k_ref.shape[0]
    for offsets, out_ref in zip(order, out_refs):
        for at, offset in enumerate(offsets):
            start = pl.multiple_of((own ^ offset) * HEAD_SIZE, HEAD_SIZE)
            row = 2 * at * keys
            out_ref[row : row + keys, :] = k_ref[:, pl.ds(start, HEAD_SIZE)]
            out_ref[row + keys : row + 2 * keys, :] = v_ref[:, pl.ds(start, HEAD_SIZE)]


def pack_cache(keys, values, group, order):
    return pl.pallas_call(
        functools.partial(pack_cache_kernel, order, group),
        out_shape=[
            jax.ShapeDtypeStruct((len(offsets) * 2 * keys.shape[0], HEAD_SIZE), jnp.bfloat16)
            for offsets in order
        ],
        name="pack_cache",
        cost_estimate=pl.CostEstimate(
            flops=0, bytes_accessed=8 * keys.size, transcendentals=0
        ),
        compiler_params=pltpu.CompilerParams(vmem_limit_bytes=PACK_VMEM),
    )(keys, values)


def lay(keys, values):
    turned = jnp.transpose(values.astype(jnp.float32)).astype(jnp.bfloat16)
    ones = jnp.ones((SUM_ROWS, keys.shape[0]), jnp.bfloat16)
    return keys, turned, ones


def lay_own_kernel(plan, k_hbm, v_hbm, slot_hbm, count_hbm, k_out, v_out, mask_ref, *scratch):
    calls, rows = plan
    k_ref, v_ref, slot_ref, count_ref, sems = scratch
    server = lax.axis_index("tok")
    group = slot_ref.shape[0]
    own = lax.rem(server, group)
    start = pl.multiple_of(own * HEAD_SIZE, HEAD_SIZE)
    copies = [
        pltpu.make_async_copy(slot_hbm, slot_ref, sems.at[0]),
        pltpu.make_async_copy(count_hbm, count_ref, sems.at[1]),
        pltpu.make_async_copy(k_hbm.at[:, pl.ds(start, HEAD_SIZE)], k_ref, sems.at[2]),
        pltpu.make_async_copy(v_hbm.at[:, pl.ds(start, HEAD_SIZE)], v_ref, sems.at[3]),
    ]
    for copy in copies:
        copy.start()
    for copy in copies:
        copy.wait()
    for call, displacements in enumerate(calls):
        mask = jnp.int32(0)
        for i, displacement in enumerate(displacements):
            block = ((server ^ displacement) * rows) // QBLK
            for k in range(group):
                key_block = server ^ k
                slot = slot_ref[own, block, key_block]
                active = (slot >= 0) & (slot < count_ref[own, key_block])
                mask = mask | (active.astype(jnp.int32) << (i * group + k))
        mask_ref[call] = jnp.full(mask_ref.shape[1:], mask, jnp.int32)
    k_out[...], v_out[:HEAD_SIZE, :], v_out[HEAD_SIZE:, :] = lay(k_ref[...], v_ref[...])


def lay_own(keys, values, task_slot, task_count, calls, rows):
    n = keys.shape[0]
    hbm = pl.BlockSpec(memory_space=pltpu.HBM)
    return pl.pallas_call(
        functools.partial(lay_own_kernel, (calls, rows)),
        out_shape=[
            jax.ShapeDtypeStruct((n, HEAD_SIZE), jnp.bfloat16),
            jax.ShapeDtypeStruct((HEAD_SIZE + SUM_ROWS, n), jnp.bfloat16),
            jax.ShapeDtypeStruct((len(calls), 8, HEAD_SIZE), jnp.int32),
        ],
        in_specs=[hbm] * 4,
        scratch_shapes=[
            pltpu.VMEM((n, HEAD_SIZE), keys.dtype),
            pltpu.VMEM((n, HEAD_SIZE), values.dtype),
            pltpu.SMEM(task_slot.shape, task_slot.dtype),
            pltpu.SMEM(task_count.shape, task_count.dtype),
            pltpu.SemaphoreType.DMA((4,)),
        ],
        name="lay_own",
        cost_estimate=pl.CostEstimate(
            flops=0, bytes_accessed=8 * n * HEAD_SIZE, transcendentals=0
        ),
        compiler_params=pltpu.CompilerParams(vmem_limit_bytes=LAY_VMEM),
    )(keys, values, task_slot, task_count)


def lay_cache_kernel(k_own, v_own, *refs):
    *in_refs, k_ref, v_ref = refs
    keys = k_own.shape[0]
    k_ref[0] = k_own[...]
    v_ref[0] = v_own[...]
    for at, ref in enumerate(in_refs, 1):
        k_ref[at], v_ref[at, :HEAD_SIZE, :], v_ref[at, HEAD_SIZE:, :] = lay(
            ref[:keys, :], ref[keys:, :]
        )


def lay_cache(k_own, v_own, pieces):
    group = 1 + len(pieces)
    return pl.pallas_call(
        lay_cache_kernel,
        out_shape=[
            jax.ShapeDtypeStruct((group,) + k_own.shape, jnp.bfloat16),
            jax.ShapeDtypeStruct((group,) + v_own.shape, jnp.bfloat16),
        ],
        name="lay_cache",
        cost_estimate=pl.CostEstimate(
            flops=0, bytes_accessed=8 * group * k_own.size, transcendentals=0
        ),
        compiler_params=pltpu.CompilerParams(vmem_limit_bytes=8 << 20),
    )(k_own, v_own, *pieces)


def split_stat(stat, width):
    high = stat.astype(jnp.bfloat16).astype(jnp.float32)
    rest = stat - high
    middle = rest.astype(jnp.bfloat16).astype(jnp.float32)
    low = rest - middle
    row = lax.broadcasted_iota(jnp.int32, (STAT_ROWS, width), 0)
    spread = jnp.where(row == 0, high, jnp.where(row == 1, middle, jnp.where(row == 2, low, 0.0)))
    return spread.astype(jnp.bfloat16)


def join_stat(ref):
    stat = ref[HEAD_SIZE : HEAD_SIZE + STAT_ROWS, :].astype(jnp.float32)
    return stat[0:1] + stat[1:2] + stat[2:3]


def attention_kernel(plan, mask_ref, *refs):
    which, widths, slab = plan
    n_chunks = sum(widths)
    n_in = len(widths)
    q_in_refs = refs[:n_in]
    k_ref, v_ref, _ = refs[n_in : n_in + 3]
    out_refs = refs[n_in + 3 : n_in + 3 + n_chunks]
    list_ref, q_ref, m_ref, acc_ref, *slots = refs[n_in + 3 + n_chunks :]
    group, _ = k_ref.shape[:2]
    width = q_ref.shape[1]
    scale = HEAD_SIZE ** (-0.5) * LOG2E

    mask = mask_ref[which, 0, 0]
    found = jnp.int32(0)
    for i in range(n_chunks * group):
        list_ref[found] = i
        found = found + ((mask >> i) & 1)

    at = 0
    for q_in_ref, n in zip(q_in_refs, widths):
        for i in range(n):
            q_ref[at + i] = q_in_ref[i * width : (i + 1) * width, :]
        at += n
    m_ref[...] = jnp.full_like(m_ref, neg_fill)
    acc_ref[...] = jnp.zeros_like(acc_ref)

    def pair(i):
        entry = list_ref[i]
        return entry // group, lax.rem(entry, group)

    def score(i, slot):
        chunk, k = pair(i)
        s_ref, top_ref, fade_ref = slot
        for c in range(0, width, slab):
            scores = lax.dot_general(
                k_ref[k],
                q_ref[chunk, c : c + slab, :],
                (((1,), (1,)), ((), ())),
                preferred_element_type=jnp.float32,
            )
            s_ref[:, c : c + slab] = scores
            old = m_ref[chunk, :, c : c + slab]
            new = jnp.maximum(old, jnp.max(scores, axis=0, keepdims=True))
            m_ref[chunk, :, c : c + slab] = new
            top_ref[:, c : c + slab] = new
            fade_ref[:, c : c + slab] = jnp.exp2((old - new) * scale)

    def weigh(i, slot):
        chunk, k = pair(i)
        s_ref, top_ref, fade_ref = slot
        for c in range(0, width, slab):
            p = jnp.exp2((s_ref[:, c : c + slab] - top_ref[0:1, c : c + slab]) * scale)
            product = jnp.dot(
                v_ref[k], p.astype(jnp.bfloat16), preferred_element_type=jnp.float32
            )
            acc_ref[chunk, :, c : c + slab] = (
                acc_ref[chunk, :, c : c + slab] * fade_ref[0:1, c : c + slab] + product
            )

    even, odd = slots[:3], slots[3:]

    @pl.when(found > 0)
    def _():
        score(0, even)

    def step(i, here, there):
        @pl.when(i + 1 < found)
        def _():
            score(i + 1, there)
            weigh(i, here)

        @pl.when(i + 1 == found)
        def _():
            weigh(i, here)

    def two(j, carry):
        step(2 * j, even, odd)
        step(2 * j + 1, odd, even)
        return carry

    lax.fori_loop(0, (found + 1) // 2, two, 0)

    for i in range(n_chunks):
        total = acc_ref[i, HEAD_SIZE : HEAD_SIZE + 1, :]
        seen = total > 0.0
        safe = jnp.where(seen, total, 1.0)
        stat = jnp.where(seen, m_ref[i, 0:1, :] * scale + jnp.log2(safe), neg_fill)
        out_refs[i][:HEAD_SIZE, :] = (acc_ref[i, :HEAD_SIZE, :] * (1.0 / safe)).astype(jnp.bfloat16)
        out_refs[i][HEAD_SIZE:, :] = split_stat(stat, width)


def attention(chunks, which, cache, masks, width, after):
    k, v = cache
    group, keys = k.shape[:2]
    widths = tuple(chunk.shape[0] // width for chunk in chunks)
    n = sum(widths)
    vmem = pl.BlockSpec(memory_space=pltpu.VMEM)
    slot = [
        pltpu.VMEM((keys, width), jnp.float32),
        pltpu.VMEM((8, width), jnp.float32),
        pltpu.VMEM((8, width), jnp.float32),
    ]
    return pl.pallas_call(
        functools.partial(attention_kernel, (which, widths, min(256, width))),
        out_shape=[jax.ShapeDtypeStruct((HEAD_SIZE + STAT_ROWS, width), jnp.bfloat16)] * n,
        in_specs=[vmem] * (len(chunks) + 3)
        + [pl.BlockSpec(memory_space=pl.ANY)],
        out_specs=[vmem] * n,
        scratch_shapes=[
            pltpu.SMEM((n * group + 1,), jnp.int32),
            pltpu.VMEM((n, width, HEAD_SIZE), jnp.bfloat16),
            pltpu.VMEM((n, 8, width), jnp.float32),
            pltpu.VMEM((n, HEAD_SIZE + SUM_ROWS, width), jnp.float32),
        ]
        + slot
        + slot,
        name="attention",
        cost_estimate=pl.CostEstimate(
            flops=4 * n * group * keys * width * HEAD_SIZE,
            bytes_accessed=4 * n * width * HEAD_SIZE + 4 * group * keys * HEAD_SIZE,
            transcendentals=n * group * keys * width,
        ),
        compiler_params=pltpu.CompilerParams(vmem_limit_bytes=16 << 20),
    )(masks, *chunks, k, v, after)


def merge_kernel(n_in, keep_stat, *refs):
    in_refs, out_refs = refs[:n_in], refs[n_in:]
    stats = [join_stat(ref) for ref in in_refs]
    largest = functools.reduce(jnp.maximum, stats)
    weights = [jnp.exp2(stat - largest) for stat in stats]
    total = functools.reduce(jnp.add, weights)
    inverse = 1.0 / total
    value = functools.reduce(
        jnp.add,
        [
            (weight * inverse) * ref[:HEAD_SIZE, :].astype(jnp.float32)
            for weight, ref in zip(weights, in_refs)
        ],
    ).astype(jnp.bfloat16)
    stat = largest + jnp.log2(total)
    part = out_refs[0].shape[1]
    for i, out_ref in enumerate(out_refs):
        lanes = slice(i * part, (i + 1) * part)
        out_ref[:HEAD_SIZE, :] = value[:, lanes]
        if keep_stat:
            out_ref[HEAD_SIZE:, :] = split_stat(stat[:, lanes], part)


def merge(messages, parts, keep_stat=True):
    height, width = messages[0].shape
    height = height if keep_stat else HEAD_SIZE
    size = len(messages) * height * width
    return pl.pallas_call(
        functools.partial(merge_kernel, len(messages), keep_stat),
        out_shape=[jax.ShapeDtypeStruct((height, width // parts), jnp.bfloat16)] * parts,
        name="merge" if keep_stat else "finish",
        cost_estimate=pl.CostEstimate(flops=4 * size, bytes_accessed=4 * size, transcendentals=0),
        compiler_params=pltpu.CompilerParams(vmem_limit_bytes=8 << 20),
    )(*messages)


def gather_kernel(rows, *refs):
    *piece_refs, out_ref = refs
    group = len(piece_refs)
    own = lax.rem(lax.axis_index("tok"), group)
    per = piece_refs[0].shape[1] // rows
    for offset in range(group):
        for j in range(per):
            block = jnp.transpose(
                piece_refs[offset][:, j * rows : (j + 1) * rows].astype(jnp.float32)
            )
            start = pl.multiple_of(((own ^ offset) * per + j) * HEAD_SIZE, HEAD_SIZE)
            out_ref[:, pl.ds(start, HEAD_SIZE)] = block.astype(jnp.bfloat16)


def gather(pieces, rows):
    width = sum(piece.shape[1] for piece in pieces) // rows * HEAD_SIZE
    return pl.pallas_call(
        functools.partial(gather_kernel, rows),
        out_shape=jax.ShapeDtypeStruct((rows, width), jnp.bfloat16),
        name="gather",
        cost_estimate=pl.CostEstimate(
            flops=0, bytes_accessed=4 * rows * width, transcendentals=0
        ),
        compiler_params=pltpu.CompilerParams(vmem_limit_bytes=4 << 20),
    )(*pieces)


def project_kernel(half, start, left_ref, w_ref, out_ref):
    columns = out_ref.shape[1]
    if half is not None:
        start = (lax.axis_index("head") ^ half) * (w_ref.shape[1] // 2) + start
    start = pl.multiple_of(start, HEAD_SIZE)
    out_ref[...] = jnp.dot(
        left_ref[...], w_ref[:, pl.ds(start, columns)], preferred_element_type=jnp.float32
    ).astype(out_ref.dtype)


def project(left, out_weight, half, start, columns, kind):
    rows, depth = left.shape
    return pl.pallas_call(
        functools.partial(project_kernel, half, start),
        out_shape=jax.ShapeDtypeStruct((rows, columns), kind),
        in_specs=[pl.BlockSpec(memory_space=pltpu.VMEM)] * 2,
        out_specs=pl.BlockSpec(memory_space=pltpu.VMEM),
        name="project",
        cost_estimate=pl.CostEstimate(
            flops=2 * rows * depth * columns,
            bytes_accessed=2 * depth * columns,
            transcendentals=0,
        ),
        compiler_params=pltpu.CompilerParams(vmem_limit_bytes=24 << 20),
    )(left, out_weight)


def swap(x, bits, servers):
    return lax.ppermute(x, "tok", [(i, i ^ bits) for i in range(servers)])


def attend_grouped(queries, keys, values, task_slot, task_count, move):
    core, column, near, far = 1, 2, 4, 8
    rows = queries.shape[0]
    q_per_kv = HEADS // KVH
    part = q_per_kv * rows
    width = 2 * part

    keep, give = pack_queries(queries, 4, ((0, 2), (1, 3)))
    pieces = pack_cache(keys, values, 4, ((core,), (column,), (column | core,)))
    got = move(give, core)
    own = jnp.concatenate([keep[:part], got[:part]], axis=0)
    other = move(jnp.concatenate([keep[part:], got[part:]], axis=0), column)
    across = move(pieces[1], column)
    beyond = move(pieces[2], column | core)
    own_far = move(own, far)
    beside = move(pieces[0], core)
    other_far = move(other, far)
    both_near = move(jnp.concatenate([own, other], axis=0), near)
    own_last = move(own_far, near)
    other_last = move(other_far, near)

    calls = ((0, column), (near, near | column), (far, far | column), (far | near,), (far | near | column,))
    k_own, v_own, masks = lay_own(keys, values, task_slot, task_count, calls, rows)
    cache = lay_cache(k_own, v_own, [beside, across, beyond])

    def call(chunks, which, after):
        return attention(chunks, which, cache, masks, width, after)

    far_a, far_b = call([own_far, other_far], 2, masks)
    own_a, own_b = call([own, other], 0, far_a)
    near_a, near_b = call([both_near], 1, own_a)
    (last_a,) = call([own_last], 3, near_a)
    (last_b,) = call([other_last], 4, last_a)

    far_b = move(far_b, far | column)
    last_a = move(last_a, near)
    last_b = move(last_b, far | near | column)
    near_b = move(near_b, near | column)
    near_a = move(near_a, near)
    own_b = move(own_b, column)
    (far_a,) = merge([far_a, last_a], 1)
    far_a = move(far_a, far)
    b_own, b_other = merge([own_b, near_b, far_b, last_b], 2, False)
    b_other = move(b_other, core)
    a_own, a_other = merge([own_a, near_a, far_a], 2, False)
    a_other = move(a_other, core)
    return [a_own, a_other, b_own, b_other]


def attend_general(queries, keys, values, task_slot, task_count, move, servers):
    assert task_slot.shape[0] == 1
    rows = queries.shape[0]
    width = HEADS // KVH * rows
    step = min(4, servers)
    calls = tuple(tuple(range(i, i + step)) for i in range(0, servers, step))
    (own,) = pack_queries(queries, 1, ((0,),))
    k_own, v_own, masks = lay_own(keys, values, task_slot, task_count, calls, rows)
    cache = lay_cache(k_own, v_own, [])
    held = {0: own}
    bit = servers // 2
    while bit:
        held.update({d ^ bit: move(chunk, bit) for d, chunk in held.items()})
        bit //= 2
    partial = {}
    for which, call in enumerate(calls):
        result = attention([held[d] for d in call], which, cache, masks, width, masks)
        for j, d in enumerate(call):
            partial[d] = [result[j]]
    bit = 1
    while bit < servers:
        for d in sorted(partial, reverse=True):
            if d & bit:
                messages = partial.pop(d)
                message = messages[0] if len(messages) == 1 else merge(messages, 1)[0]
                partial[d ^ bit].append(move(message, bit))
        bit *= 2
    return merge(partial[0], 1, False)


def on_device(queries, keys, values, out_weight, task_slot, task_count):
    servers = lax.axis_size("tok")
    heads = lax.axis_size("head")
    rows = queries.shape[0]
    group = task_slot.shape[0]
    move = functools.partial(swap, servers=servers)
    if group == 4 and servers == 16:
        attended = attend_grouped(queries, keys, values, task_slot, task_count, move)
    else:
        attended = attend_general(queries, keys, values, task_slot, task_count, move, servers)
    left = gather(attended, rows)

    columns = out_weight.shape[1] // heads
    if heads == 2:
        return exchange_halves(left, out_weight, columns)
    share = project(left, out_weight, None, 0, out_weight.shape[1], jnp.bfloat16)
    return lax.psum_scatter(share, "head", scatter_dimension=1, tiled=True)


def exchange_halves(left, out_weight, columns):
    piece = columns // 2
    arrived = []
    for i in range(2):
        part = project(left, out_weight, 1, i * piece, piece, jnp.bfloat16)
        arrived.append(lax.ppermute(part, "head", [(0, 1), (1, 0)]))
    here = project(left, out_weight, 0, 0, columns, jnp.float32)
    return (here + jnp.concatenate(arrived, axis=1).astype(jnp.float32)).astype(jnp.bfloat16)


def solution(mesh):
    placed = (
        P("tok", "head"),
        P("tok", "head"),
        P("tok", "head"),
        P("head", None),
        P("head", None, None),
        P("head", None),
    )
    return jax.shard_map(
        on_device, mesh=mesh, in_specs=placed, out_specs=P("tok", "head"), check_vma=False
    )
```

```python
import functools
import math

import jax
import jax.numpy as jnp
from jax import lax
from jax.experimental import pallas as pl
from jax.experimental.pallas import tpu as pltpu
from jax.sharding import PartitionSpec as P


HEADS = 32
KVH = 8
HEAD_SIZE = 128
QBLK = 128

theta_base = 500000.0
neg_fill = -1e30
LOG2E = math.log2(math.e)
STAT_ROWS = 8
SUM_ROWS = 16
PACK_VMEM = 47 << 20


def rotary_tables(rows, first_row):
    half = HEAD_SIZE // 2
    frequency = theta_base ** (-(jnp.arange(half, dtype=jnp.float32) * (2.0 / HEAD_SIZE)))
    places = (first_row + jnp.arange(rows, dtype=jnp.int32)).astype(jnp.float32)
    angles = places[:, None] * frequency[None, :]
    cosine = jnp.cos(angles)
    sine = jnp.sin(angles)
    return (
        jnp.concatenate([cosine, cosine], axis=1),
        jnp.concatenate([-sine, sine], axis=1),
    )


def pack_queries_kernel(order, q_per_kv, group, cos_ref, sin_ref, q_ref, *out_refs):
    own = lax.rem(lax.axis_index("tok"), group)
    rows = q_ref.shape[0]
    cosine = cos_ref[...]
    sine = sin_ref[...]
    for offsets, out_ref in zip(order, out_refs):
        for at, offset in enumerate(offsets):
            head = own ^ offset
            for j in range(q_per_kv):
                start = pl.multiple_of((head * q_per_kv + j) * HEAD_SIZE, HEAD_SIZE)
                x = q_ref[:, pl.ds(start, HEAD_SIZE)].astype(jnp.float32)
                turned = pltpu.roll(x, HEAD_SIZE // 2, 1)
                row = (at * q_per_kv + j) * rows
                out_ref[row : row + rows, :] = (x * cosine + turned * sine).astype(jnp.bfloat16)


def pack_queries(queries, group, order):
    rows = queries.shape[0]
    q_per_kv = HEADS // KVH
    cosine, sine = rotary_tables(rows, lax.axis_index("tok") * rows)
    return pl.pallas_call(
        functools.partial(pack_queries_kernel, order, q_per_kv, group),
        out_shape=[
            jax.ShapeDtypeStruct((len(offsets) * q_per_kv * rows, HEAD_SIZE), jnp.bfloat16)
            for offsets in order
        ],
        name="pack_queries",
        cost_estimate=pl.CostEstimate(
            flops=6 * queries.size, bytes_accessed=4 * queries.size, transcendentals=0
        ),
        compiler_params=pltpu.CompilerParams(vmem_limit_bytes=PACK_VMEM),
    )(cosine, sine, queries)


def pack_cache_kernel(order, group, k_ref, v_ref, *out_refs):
    own = lax.rem(lax.axis_index("tok"), group)
    keys = k_ref.shape[0]
    for offsets, out_ref in zip(order, out_refs):
        for at, offset in enumerate(offsets):
            start = pl.multiple_of((own ^ offset) * HEAD_SIZE, HEAD_SIZE)
            row = 2 * at * keys
            out_ref[row : row + keys, :] = k_ref[:, pl.ds(start, HEAD_SIZE)]
            out_ref[row + keys : row + 2 * keys, :] = v_ref[:, pl.ds(start, HEAD_SIZE)]


def pack_cache(keys, values, group, order):
    return pl.pallas_call(
        functools.partial(pack_cache_kernel, order, group),
        out_shape=[
            jax.ShapeDtypeStruct((len(offsets) * 2 * keys.shape[0], HEAD_SIZE), jnp.bfloat16)
            for offsets in order
        ],
        name="pack_cache",
        cost_estimate=pl.CostEstimate(
            flops=0, bytes_accessed=8 * keys.size, transcendentals=0
        ),
        compiler_params=pltpu.CompilerParams(vmem_limit_bytes=PACK_VMEM),
    )(keys, values)


def mask_kernel(calls, rows, slot_hbm, count_hbm, mask_ref, slot_ref, count_ref, sems):
    server = lax.axis_index("tok")
    group = slot_ref.shape[0]
    own = lax.rem(server, group)
    copies = [
        pltpu.make_async_copy(slot_hbm, slot_ref, sems.at[0]),
        pltpu.make_async_copy(count_hbm, count_ref, sems.at[1]),
    ]
    for copy in copies:
        copy.start()
    for copy in copies:
        copy.wait()
    for call, displacements in enumerate(calls):
        mask = jnp.int32(0)
        for i, displacement in enumerate(displacements):
            block = ((server ^ displacement) * rows) // QBLK
            for k in range(group):
                key_block = server ^ k
                slot = slot_ref[own, block, key_block]
                active = (slot >= 0) & (slot < count_ref[own, key_block])
                mask = mask | (active.astype(jnp.int32) << (i * group + k))
        mask_ref[call] = jnp.full(mask_ref.shape[1:], mask, jnp.int32)


def active_masks(task_slot, task_count, calls, rows):
    hbm = pl.BlockSpec(memory_space=pltpu.HBM)
    return pl.pallas_call(
        functools.partial(mask_kernel, calls, rows),
        out_shape=jax.ShapeDtypeStruct((len(calls), 8, HEAD_SIZE), jnp.int32),
        in_specs=[hbm] * 2,
        scratch_shapes=[
            pltpu.SMEM(task_slot.shape, task_slot.dtype),
            pltpu.SMEM(task_count.shape, task_count.dtype),
            pltpu.SemaphoreType.DMA((2,)),
        ],
        name="masks",
        cost_estimate=pl.CostEstimate(
            flops=0, bytes_accessed=4 * task_slot.size, transcendentals=0
        ),
        compiler_params=pltpu.CompilerParams(vmem_limit_bytes=4 << 20),
    )(task_slot, task_count)


def lay_cache_kernel(*refs):
    *in_refs, k_ref, v_ref = refs
    keys = k_ref.shape[1]
    for at, ref in enumerate(in_refs):
        k_ref[at] = ref[:keys, :]
        v_ref[at, :HEAD_SIZE, :] = jnp.transpose(ref[keys:, :].astype(jnp.float32)).astype(
            jnp.bfloat16
        )
        v_ref[at, HEAD_SIZE:, :] = jnp.ones((SUM_ROWS, keys), jnp.bfloat16)


def lay_cache(pieces):
    group = len(pieces)
    keys = pieces[0].shape[0] // 2
    return pl.pallas_call(
        lay_cache_kernel,
        out_shape=[
            jax.ShapeDtypeStruct((group, keys, HEAD_SIZE), jnp.bfloat16),
            jax.ShapeDtypeStruct((group, HEAD_SIZE + SUM_ROWS, keys), jnp.bfloat16),
        ],
        name="lay_cache",
        cost_estimate=pl.CostEstimate(
            flops=0, bytes_accessed=8 * group * keys * HEAD_SIZE, transcendentals=0
        ),
        compiler_params=pltpu.CompilerParams(vmem_limit_bytes=8 << 20),
    )(*pieces)


def split_stat(stat, width):
    high = stat.astype(jnp.bfloat16).astype(jnp.float32)
    rest = stat - high
    middle = rest.astype(jnp.bfloat16).astype(jnp.float32)
    low = rest - middle
    row = lax.broadcasted_iota(jnp.int32, (STAT_ROWS, width), 0)
    spread = jnp.where(row == 0, high, jnp.where(row == 1, middle, jnp.where(row == 2, low, 0.0)))
    return spread.astype(jnp.bfloat16)


def join_stat(ref):
    stat = ref[HEAD_SIZE : HEAD_SIZE + STAT_ROWS, :].astype(jnp.float32)
    return stat[0:1] + stat[1:2] + stat[2:3]


def attention_kernel(plan, mask_ref, *refs):
    which, widths, slab = plan
    n_chunks = sum(widths)
    n_in = len(widths)
    q_in_refs = refs[:n_in]
    k_ref, v_ref, _ = refs[n_in : n_in + 3]
    out_refs = refs[n_in + 3 : n_in + 3 + n_chunks]
    list_ref, q_ref, m_ref, acc_ref, *slots = refs[n_in + 3 + n_chunks :]
    group, _ = k_ref.shape[:2]
    width = q_ref.shape[1]
    scale = HEAD_SIZE ** (-0.5) * LOG2E

    mask = mask_ref[which, 0, 0]
    found = jnp.int32(0)
    for i in range(n_chunks * group):
        list_ref[found] = i
        found = found + ((mask >> i) & 1)

    at = 0
    for q_in_ref, n in zip(q_in_refs, widths):
        for i in range(n):
            q_ref[at + i] = q_in_ref[i * width : (i + 1) * width, :]
        at += n
    m_ref[...] = jnp.full_like(m_ref, neg_fill)
    acc_ref[...] = jnp.zeros_like(acc_ref)

    def pair(i):
        entry = list_ref[i]
        return entry // group, lax.rem(entry, group)

    def score(i, slot):
        chunk, k = pair(i)
        s_ref, top_ref, fade_ref = slot
        for c in range(0, width, slab):
            scores = lax.dot_general(
                k_ref[k],
                q_ref[chunk, c : c + slab, :],
                (((1,), (1,)), ((), ())),
                preferred_element_type=jnp.float32,
            )
            s_ref[:, c : c + slab] = scores
            old = m_ref[chunk, :, c : c + slab]
            new = jnp.maximum(old, jnp.max(scores, axis=0, keepdims=True))
            m_ref[chunk, :, c : c + slab] = new
            top_ref[:, c : c + slab] = new
            fade_ref[:, c : c + slab] = jnp.exp2((old - new) * scale)

    def weigh(i, slot):
        chunk, k = pair(i)
        s_ref, top_ref, fade_ref = slot
        for c in range(0, width, slab):
            p = jnp.exp2((s_ref[:, c : c + slab] - top_ref[0:1, c : c + slab]) * scale)
            product = jnp.dot(
                v_ref[k], p.astype(jnp.bfloat16), preferred_element_type=jnp.float32
            )
            acc_ref[chunk, :, c : c + slab] = (
                acc_ref[chunk, :, c : c + slab] * fade_ref[0:1, c : c + slab] + product
            )

    even, odd = slots[:3], slots[3:]

    @pl.when(found > 0)
    def _():
        score(0, even)

    def step(i, here, there):
        @pl.when(i + 1 < found)
        def _():
            score(i + 1, there)
            weigh(i, here)

        @pl.when(i + 1 == found)
        def _():
            weigh(i, here)

    def two(j, carry):
        step(2 * j, even, odd)
        step(2 * j + 1, odd, even)
        return carry

    lax.fori_loop(0, (found + 1) // 2, two, 0)

    for i in range(n_chunks):
        total = acc_ref[i, HEAD_SIZE : HEAD_SIZE + 1, :]
        seen = total > 0.0
        safe = jnp.where(seen, total, 1.0)
        stat = jnp.where(seen, m_ref[i, 0:1, :] * scale + jnp.log2(safe), neg_fill)
        out_refs[i][:HEAD_SIZE, :] = (acc_ref[i, :HEAD_SIZE, :] * (1.0 / safe)).astype(jnp.bfloat16)
        out_refs[i][HEAD_SIZE:, :] = split_stat(stat, width)


def attention(chunks, which, cache, masks, width, after):
    k, v = cache
    group, keys = k.shape[:2]
    widths = tuple(chunk.shape[0] // width for chunk in chunks)
    n = sum(widths)
    vmem = pl.BlockSpec(memory_space=pltpu.VMEM)
    slot = [
        pltpu.VMEM((keys, width), jnp.float32),
        pltpu.VMEM((8, width), jnp.float32),
        pltpu.VMEM((8, width), jnp.float32),
    ]
    return pl.pallas_call(
        functools.partial(attention_kernel, (which, widths, min(256, width))),
        out_shape=[jax.ShapeDtypeStruct((HEAD_SIZE + STAT_ROWS, width), jnp.bfloat16)] * n,
        in_specs=[vmem] * (len(chunks) + 3)
        + [pl.BlockSpec(memory_space=pl.ANY)],
        out_specs=[vmem] * n,
        scratch_shapes=[
            pltpu.SMEM((n * group + 1,), jnp.int32),
            pltpu.VMEM((n, width, HEAD_SIZE), jnp.bfloat16),
            pltpu.VMEM((n, 8, width), jnp.float32),
            pltpu.VMEM((n, HEAD_SIZE + SUM_ROWS, width), jnp.float32),
        ]
        + slot
        + slot,
        name="attention",
        cost_estimate=pl.CostEstimate(
            flops=4 * n * group * keys * width * HEAD_SIZE,
            bytes_accessed=4 * n * width * HEAD_SIZE + 4 * group * keys * HEAD_SIZE,
            transcendentals=n * group * keys * width,
        ),
        compiler_params=pltpu.CompilerParams(vmem_limit_bytes=16 << 20),
    )(masks, *chunks, k, v, after)


def merge_kernel(n_in, keep_stat, *refs):
    in_refs, out_refs = refs[:n_in], refs[n_in:]
    stats = [join_stat(ref) for ref in in_refs]
    largest = functools.reduce(jnp.maximum, stats)
    weights = [jnp.exp2(stat - largest) for stat in stats]
    total = functools.reduce(jnp.add, weights)
    inverse = 1.0 / total
    value = functools.reduce(
        jnp.add,
        [
            (weight * inverse) * ref[:HEAD_SIZE, :].astype(jnp.float32)
            for weight, ref in zip(weights, in_refs)
        ],
    ).astype(jnp.bfloat16)
    stat = largest + jnp.log2(total)
    part = out_refs[0].shape[1]
    for i, out_ref in enumerate(out_refs):
        lanes = slice(i * part, (i + 1) * part)
        out_ref[:HEAD_SIZE, :] = value[:, lanes]
        if keep_stat:
            out_ref[HEAD_SIZE:, :] = split_stat(stat[:, lanes], part)


def merge(messages, parts, keep_stat=True):
    height, width = messages[0].shape
    height = height if keep_stat else HEAD_SIZE
    size = len(messages) * height * width
    return pl.pallas_call(
        functools.partial(merge_kernel, len(messages), keep_stat),
        out_shape=[jax.ShapeDtypeStruct((height, width // parts), jnp.bfloat16)] * parts,
        name="merge" if keep_stat else "finish",
        cost_estimate=pl.CostEstimate(flops=4 * size, bytes_accessed=4 * size, transcendentals=0),
        compiler_params=pltpu.CompilerParams(vmem_limit_bytes=8 << 20),
    )(*messages)


def gather_kernel(rows, *refs):
    *piece_refs, out_ref = refs
    group = len(piece_refs)
    own = lax.rem(lax.axis_index("tok"), group)
    per = piece_refs[0].shape[1] // rows
    for offset in range(group):
        for j in range(per):
            block = jnp.transpose(
                piece_refs[offset][:, j * rows : (j + 1) * rows].astype(jnp.float32)
            )
            start = pl.multiple_of(((own ^ offset) * per + j) * HEAD_SIZE, HEAD_SIZE)
            out_ref[:, pl.ds(start, HEAD_SIZE)] = block.astype(jnp.bfloat16)


def gather(pieces, rows):
    width = sum(piece.shape[1] for piece in pieces) // rows * HEAD_SIZE
    return pl.pallas_call(
        functools.partial(gather_kernel, rows),
        out_shape=jax.ShapeDtypeStruct((rows, width), jnp.bfloat16),
        name="gather",
        cost_estimate=pl.CostEstimate(
            flops=0, bytes_accessed=4 * rows * width, transcendentals=0
        ),
        compiler_params=pltpu.CompilerParams(vmem_limit_bytes=4 << 20),
    )(*pieces)


def project_kernel(half, start, left_ref, w_ref, out_ref):
    columns = out_ref.shape[1]
    if half is not None:
        start = (lax.axis_index("head") ^ half) * (w_ref.shape[1] // 2) + start
    start = pl.multiple_of(start, HEAD_SIZE)
    out_ref[...] = jnp.dot(
        left_ref[...], w_ref[:, pl.ds(start, columns)], preferred_element_type=jnp.float32
    ).astype(out_ref.dtype)


def project(left, out_weight, half, start, columns, kind):
    rows, depth = left.shape
    return pl.pallas_call(
        functools.partial(project_kernel, half, start),
        out_shape=jax.ShapeDtypeStruct((rows, columns), kind),
        in_specs=[pl.BlockSpec(memory_space=pltpu.VMEM)] * 2,
        out_specs=pl.BlockSpec(memory_space=pltpu.VMEM),
        name="project",
        cost_estimate=pl.CostEstimate(
            flops=2 * rows * depth * columns,
            bytes_accessed=2 * depth * columns,
            transcendentals=0,
        ),
        compiler_params=pltpu.CompilerParams(vmem_limit_bytes=24 << 20),
    )(left, out_weight)


def swap(x, bits, servers):
    return lax.ppermute(x, "tok", [(i, i ^ bits) for i in range(servers)])


def attend_grouped(queries, keys, values, task_slot, task_count, move):
    core, column, near, far = 1, 2, 4, 8
    rows = queries.shape[0]
    q_per_kv = HEADS // KVH
    part = q_per_kv * rows
    width = 2 * part

    keep, give = pack_queries(queries, 4, ((0, 2), (1, 3)))
    pieces = pack_cache(keys, values, 4, ((0,), (core,), (column,), (column | core,)))
    got = move(give, core)
    own = jnp.concatenate([keep[:part], got[:part]], axis=0)
    other = move(jnp.concatenate([keep[part:], got[part:]], axis=0), column)
    across = move(pieces[2], column)
    beyond = move(pieces[3], column | core)
    own_far = move(own, far)
    beside = move(pieces[1], core)
    other_far = move(other, far)
    both_near = move(jnp.concatenate([own, other], axis=0), near)
    own_last = move(own_far, near)
    other_last = move(other_far, near)

    calls = ((0, column), (near, near | column), (far, far | column), (far | near,), (far | near | column,))
    masks = active_masks(task_slot, task_count, calls, rows)
    cache = lay_cache([pieces[0], beside, across, beyond])

    def call(chunks, which, after):
        return attention(chunks, which, cache, masks, width, after)

    own_a, own_b = call([own, other], 0, masks)
    far_a, far_b = call([own_far, other_far], 2, own_a)
    near_a, near_b = call([both_near], 1, far_a)
    (last_a,) = call([own_last], 3, near_a)
    (last_b,) = call([other_last], 4, last_a)

    far_b = move(far_b, far | column)
    last_a = move(last_a, near)
    last_b = move(last_b, far | near | column)
    near_b = move(near_b, near | column)
    near_a = move(near_a, near)
    own_b = move(own_b, column)
    (far_a,) = merge([far_a, last_a], 1)
    far_a = move(far_a, far)
    b_own, b_other = merge([own_b, near_b, far_b, last_b], 2, False)
    b_other = move(b_other, core)
    a_own, a_other = merge([own_a, near_a, far_a], 2, False)
    a_other = move(a_other, core)
    return [a_own, a_other, b_own, b_other]


def attend_general(queries, keys, values, task_slot, task_count, move, servers):
    assert task_slot.shape[0] == 1
    rows = queries.shape[0]
    width = HEADS // KVH * rows
    step = min(4, servers)
    calls = tuple(tuple(range(i, i + step)) for i in range(0, servers, step))
    (own,) = pack_queries(queries, 1, ((0,),))
    masks = active_masks(task_slot, task_count, calls, rows)
    cache = lay_cache(pack_cache(keys, values, 1, ((0,),)))
    held = {0: own}
    bit = servers // 2
    while bit:
        held.update({d ^ bit: move(chunk, bit) for d, chunk in held.items()})
        bit //= 2
    partial = {}
    for which, call in enumerate(calls):
        result = attention([held[d] for d in call], which, cache, masks, width, masks)
        for j, d in enumerate(call):
            partial[d] = [result[j]]
    bit = 1
    while bit < servers:
        for d in sorted(partial, reverse=True):
            if d & bit:
                messages = partial.pop(d)
                message = messages[0] if len(messages) == 1 else merge(messages, 1)[0]
                partial[d ^ bit].append(move(message, bit))
        bit *= 2
    return merge(partial[0], 1, False)


def on_device(queries, keys, values, out_weight, task_slot, task_count):
    servers = lax.axis_size("tok")
    heads = lax.axis_size("head")
    rows = queries.shape[0]
    group = task_slot.shape[0]
    move = functools.partial(swap, servers=servers)
    if group == 4 and servers == 16:
        attended = attend_grouped(queries, keys, values, task_slot, task_count, move)
    else:
        attended = attend_general(queries, keys, values, task_slot, task_count, move, servers)
    left = gather(attended, rows)

    columns = out_weight.shape[1] // heads
    if heads == 2:
        return exchange_halves(left, out_weight, columns)
    share = project(left, out_weight, None, 0, out_weight.shape[1], jnp.bfloat16)
    return lax.psum_scatter(share, "head", scatter_dimension=1, tiled=True)


def exchange_halves(left, out_weight, columns):
    piece = columns // 2
    arrived = []
    for i in range(2):
        part = project(left, out_weight, 1, i * piece, piece, jnp.bfloat16)
        arrived.append(lax.ppermute(part, "head", [(0, 1), (1, 0)]))
    here = project(left, out_weight, 0, 0, columns, jnp.float32)
    return (here + jnp.concatenate(arrived, axis=1).astype(jnp.float32)).astype(jnp.bfloat16)


def solution(mesh):
    placed = (
        P("tok", "head"),
        P("tok", "head"),
        P("tok", "head"),
        P("head", None),
        P("head", None, None),
        P("head", None),
    )
    return jax.shard_map(
        on_device, mesh=mesh, in_specs=placed, out_specs=P("tok", "head"), check_vma=False
    )
```

```python
import functools
import math

import jax
import jax.numpy as jnp
from jax import lax
from jax.experimental import pallas as pl
from jax.experimental.pallas import tpu as pltpu
from jax.sharding import PartitionSpec as P


HEADS = 32
KVH = 8
HEAD_SIZE = 128
QBLK = 128

theta_base = 500000.0
neg_fill = -1e30
LOG2E = math.log2(math.e)
STAT_ROWS = 8
SUM_ROWS = 16
PACK_VMEM = 47 << 20


def rotary_tables(rows, first_row):
    half = HEAD_SIZE // 2
    frequency = theta_base ** (-(jnp.arange(half, dtype=jnp.float32) * (2.0 / HEAD_SIZE)))
    places = (first_row + jnp.arange(rows, dtype=jnp.int32)).astype(jnp.float32)
    angles = places[:, None] * frequency[None, :]
    cosine = jnp.cos(angles)
    sine = jnp.sin(angles)
    return (
        jnp.concatenate([cosine, cosine], axis=1),
        jnp.concatenate([-sine, sine], axis=1),
    )


def pack_queries_kernel(order, q_per_kv, group, cos_ref, sin_ref, q_ref, *out_refs):
    own = lax.rem(lax.axis_index("tok"), group)
    rows = q_ref.shape[0]
    cosine = cos_ref[...]
    sine = sin_ref[...]
    for offsets, out_ref in zip(order, out_refs):
        for at, offset in enumerate(offsets):
            head = own ^ offset
            for j in range(q_per_kv):
                start = pl.multiple_of((head * q_per_kv + j) * HEAD_SIZE, HEAD_SIZE)
                x = q_ref[:, pl.ds(start, HEAD_SIZE)].astype(jnp.float32)
                turned = pltpu.roll(x, HEAD_SIZE // 2, 1)
                row = (at * q_per_kv + j) * rows
                out_ref[row : row + rows, :] = (x * cosine + turned * sine).astype(jnp.bfloat16)


def pack_queries(queries, group, order):
    rows = queries.shape[0]
    q_per_kv = HEADS // KVH
    cosine, sine = rotary_tables(rows, lax.axis_index("tok") * rows)
    return pl.pallas_call(
        functools.partial(pack_queries_kernel, order, q_per_kv, group),
        out_shape=[
            jax.ShapeDtypeStruct((len(offsets) * q_per_kv * rows, HEAD_SIZE), jnp.bfloat16)
            for offsets in order
        ],
        name="pack_queries",
        cost_estimate=pl.CostEstimate(
            flops=6 * queries.size, bytes_accessed=4 * queries.size, transcendentals=0
        ),
        compiler_params=pltpu.CompilerParams(vmem_limit_bytes=PACK_VMEM),
    )(cosine, sine, queries)


def pack_cache_kernel(order, group, k_ref, v_ref, *out_refs):
    own = lax.rem(lax.axis_index("tok"), group)
    keys = k_ref.shape[0]
    for offsets, out_ref in zip(order, out_refs):
        for at, offset in enumerate(offsets):
            start = pl.multiple_of((own ^ offset) * HEAD_SIZE, HEAD_SIZE)
            row = 2 * at * keys
            out_ref[row : row + keys, :] = k_ref[:, pl.ds(start, HEAD_SIZE)]
            out_ref[row + keys : row + 2 * keys, :] = v_ref[:, pl.ds(start, HEAD_SIZE)]


def pack_cache(keys, values, group, order):
    return pl.pallas_call(
        functools.partial(pack_cache_kernel, order, group),
        out_shape=[
            jax.ShapeDtypeStruct((len(offsets) * 2 * keys.shape[0], HEAD_SIZE), jnp.bfloat16)
            for offsets in order
        ],
        name="pack_cache",
        cost_estimate=pl.CostEstimate(
            flops=0, bytes_accessed=8 * keys.size, transcendentals=0
        ),
        compiler_params=pltpu.CompilerParams(vmem_limit_bytes=PACK_VMEM),
    )(keys, values)


def mask_kernel(calls, rows, slot_hbm, count_hbm, mask_ref, slot_ref, count_ref, sems):
    server = lax.axis_index("tok")
    group = slot_ref.shape[0]
    own = lax.rem(server, group)
    copies = [
        pltpu.make_async_copy(slot_hbm, slot_ref, sems.at[0]),
        pltpu.make_async_copy(count_hbm, count_ref, sems.at[1]),
    ]
    for copy in copies:
        copy.start()
    for copy in copies:
        copy.wait()
    for call, displacements in enumerate(calls):
        mask = jnp.int32(0)
        for i, displacement in enumerate(displacements):
            block = ((server ^ displacement) * rows) // QBLK
            for k in range(group):
                key_block = server ^ k
                slot = slot_ref[own, block, key_block]
                active = (slot >= 0) & (slot < count_ref[own, key_block])
                mask = mask | (active.astype(jnp.int32) << (i * group + k))
        mask_ref[call] = jnp.full(mask_ref.shape[1:], mask, jnp.int32)


def active_masks(task_slot, task_count, calls, rows):
    hbm = pl.BlockSpec(memory_space=pltpu.HBM)
    return pl.pallas_call(
        functools.partial(mask_kernel, calls, rows),
        out_shape=jax.ShapeDtypeStruct((len(calls), 8, HEAD_SIZE), jnp.int32),
        in_specs=[hbm] * 2,
        scratch_shapes=[
            pltpu.SMEM(task_slot.shape, task_slot.dtype),
            pltpu.SMEM(task_count.shape, task_count.dtype),
            pltpu.SemaphoreType.DMA((2,)),
        ],
        name="masks",
        cost_estimate=pl.CostEstimate(
            flops=0, bytes_accessed=4 * task_slot.size, transcendentals=0
        ),
        compiler_params=pltpu.CompilerParams(vmem_limit_bytes=4 << 20),
    )(task_slot, task_count)


def lay_cache_kernel(laid, *refs):
    *in_refs, _, k_ref, v_ref = refs
    keys = k_ref.shape[1]
    if laid:
        k_ref[:laid] = in_refs[0][...]
        v_ref[:laid] = in_refs[1][...]
        in_refs = in_refs[2:]
    for at, ref in enumerate(in_refs, laid):
        k_ref[at] = ref[:keys, :]
        v_ref[at, :HEAD_SIZE, :] = jnp.transpose(ref[keys:, :].astype(jnp.float32)).astype(
            jnp.bfloat16
        )
        v_ref[at, HEAD_SIZE:, :] = jnp.ones((SUM_ROWS, keys), jnp.bfloat16)


def lay_cache(pieces, after, before=()):
    vmem = pl.BlockSpec(memory_space=pltpu.VMEM)
    laid = before[0].shape[0] if before else 0
    group = laid + len(pieces)
    keys = pieces[0].shape[0] // 2
    return pl.pallas_call(
        functools.partial(lay_cache_kernel, laid),
        out_shape=[
            jax.ShapeDtypeStruct((group, keys, HEAD_SIZE), jnp.bfloat16),
            jax.ShapeDtypeStruct((group, HEAD_SIZE + SUM_ROWS, keys), jnp.bfloat16),
        ],
        in_specs=[vmem] * (len(before) + len(pieces)) + [pl.BlockSpec(memory_space=pl.ANY)],
        name="lay_cache",
        cost_estimate=pl.CostEstimate(
            flops=0, bytes_accessed=8 * group * keys * HEAD_SIZE, transcendentals=0
        ),
        compiler_params=pltpu.CompilerParams(vmem_limit_bytes=8 << 20),
    )(*before, *pieces, after)


def split_stat(stat, width):
    high = stat.astype(jnp.bfloat16).astype(jnp.float32)
    rest = stat - high
    middle = rest.astype(jnp.bfloat16).astype(jnp.float32)
    low = rest - middle
    row = lax.broadcasted_iota(jnp.int32, (STAT_ROWS, width), 0)
    spread = jnp.where(row == 0, high, jnp.where(row == 1, middle, jnp.where(row == 2, low, 0.0)))
    return spread.astype(jnp.bfloat16)


def join_stat(ref):
    stat = ref[HEAD_SIZE : HEAD_SIZE + STAT_ROWS, :].astype(jnp.float32)
    return stat[0:1] + stat[1:2] + stat[2:3]


def attention_kernel(plan, mask_ref, *refs):
    which, widths, slab, group, blocks, resumed, ended = plan
    n_chunks = sum(widths)
    n_in = len(widths)
    q_in_refs = refs[:n_in]
    k_ref, v_ref, _ = refs[n_in : n_in + 3]
    at = n_in + 3
    before_refs = refs[at : at + 2 * resumed]
    at += 2 * resumed
    n_out = n_chunks if ended else 2
    out_refs = refs[at : at + n_out]
    at += n_out
    if ended:
        m_ref, acc_ref = refs[at : at + 2]
        at += 2
    else:
        m_ref, acc_ref = out_refs
    list_ref, q_ref, *slots = refs[at:]
    width = q_ref.shape[1]
    scale = HEAD_SIZE ** (-0.5) * LOG2E

    mask = mask_ref[which, 0, 0]
    found = jnp.int32(0)
    for i in range(n_chunks):
        for k in blocks:
            entry = i * group + k
            list_ref[found] = entry
            found = found + ((mask >> entry) & 1)

    at = 0
    for q_in_ref, n in zip(q_in_refs, widths):
        for i in range(n):
            q_ref[at + i] = q_in_ref[i * width : (i + 1) * width, :]
        at += n
    if resumed:
        m_ref[...] = before_refs[0][...]
        acc_ref[...] = before_refs[1][...]
    else:
        m_ref[...] = jnp.full_like(m_ref, neg_fill)
        acc_ref[...] = jnp.zeros_like(acc_ref)

    def pair(i):
        entry = list_ref[i]
        return entry // group, lax.rem(entry, group)

    def score(i, slot):
        chunk, k = pair(i)
        s_ref, top_ref, fade_ref = slot
        for c in range(0, width, slab):
            scores = lax.dot_general(
                k_ref[k],
                q_ref[chunk, c : c + slab, :],
                (((1,), (1,)), ((), ())),
                preferred_element_type=jnp.float32,
            )
            s_ref[:, c : c + slab] = scores
            old = m_ref[chunk, :, c : c + slab]
            new = jnp.maximum(old, jnp.max(scores, axis=0, keepdims=True))
            m_ref[chunk, :, c : c + slab] = new
            top_ref[:, c : c + slab] = new
            fade_ref[:, c : c + slab] = jnp.exp2((old - new) * scale)

    def weigh(i, slot):
        chunk, k = pair(i)
        s_ref, top_ref, fade_ref = slot
        for c in range(0, width, slab):
            p = jnp.exp2((s_ref[:, c : c + slab] - top_ref[0:1, c : c + slab]) * scale)
            product = jnp.dot(
                v_ref[k], p.astype(jnp.bfloat16), preferred_element_type=jnp.float32
            )
            acc_ref[chunk, :, c : c + slab] = (
                acc_ref[chunk, :, c : c + slab] * fade_ref[0:1, c : c + slab] + product
            )

    even, odd = slots[:3], slots[3:]

    @pl.when(found > 0)
    def _():
        score(0, even)

    def step(i, here, there):
        @pl.when(i + 1 < found)
        def _():
            score(i + 1, there)
            weigh(i, here)

        @pl.when(i + 1 == found)
        def _():
            weigh(i, here)

    def two(j, carry):
        step(2 * j, even, odd)
        step(2 * j + 1, odd, even)
        return carry

    lax.fori_loop(0, (found + 1) // 2, two, 0)

    if not ended:
        return
    for i in range(n_chunks):
        total = acc_ref[i, HEAD_SIZE : HEAD_SIZE + 1, :]
        seen = total > 0.0
        safe = jnp.where(seen, total, 1.0)
        stat = jnp.where(seen, m_ref[i, 0:1, :] * scale + jnp.log2(safe), neg_fill)
        out_refs[i][:HEAD_SIZE, :] = (acc_ref[i, :HEAD_SIZE, :] * (1.0 / safe)).astype(jnp.bfloat16)
        out_refs[i][HEAD_SIZE:, :] = split_stat(stat, width)


def attention(chunks, which, cache, masks, width, after, group, blocks, before=(), ended=True):
    k, v = cache
    keys = k.shape[1]
    widths = tuple(chunk.shape[0] // width for chunk in chunks)
    n = sum(widths)
    vmem = pl.BlockSpec(memory_space=pltpu.VMEM)
    state = [(n, 8, width), (n, HEAD_SIZE + SUM_ROWS, width)]
    slot = [
        pltpu.VMEM((keys, width), jnp.float32),
        pltpu.VMEM((8, width), jnp.float32),
        pltpu.VMEM((8, width), jnp.float32),
    ]
    if ended:
        out_shape = [jax.ShapeDtypeStruct((HEAD_SIZE + STAT_ROWS, width), jnp.bfloat16)] * n
        scratch = [pltpu.VMEM(shape, jnp.float32) for shape in state]
    else:
        out_shape = [jax.ShapeDtypeStruct(shape, jnp.float32) for shape in state]
        scratch = []
    pairs = n * len(blocks)
    plan = (which, widths, min(256, width), group, tuple(blocks), bool(before), ended)
    return pl.pallas_call(
        functools.partial(attention_kernel, plan),
        out_shape=out_shape,
        in_specs=[vmem] * (len(chunks) + 3)
        + [pl.BlockSpec(memory_space=pl.ANY)]
        + [vmem] * len(before),
        out_specs=[vmem] * len(out_shape),
        scratch_shapes=scratch
        + [
            pltpu.SMEM((pairs + 1,), jnp.int32),
            pltpu.VMEM((n, width, HEAD_SIZE), jnp.bfloat16),
        ]
        + slot
        + slot,
        name="attention",
        cost_estimate=pl.CostEstimate(
            flops=4 * pairs * keys * width * HEAD_SIZE,
            bytes_accessed=4 * n * width * HEAD_SIZE + 4 * len(blocks) * keys * HEAD_SIZE,
            transcendentals=pairs * keys * width,
        ),
        compiler_params=pltpu.CompilerParams(vmem_limit_bytes=16 << 20),
    )(masks, *chunks, k, v, after, *before)


def merge_kernel(n_in, keep_stat, *refs):
    in_refs, out_refs = refs[:n_in], refs[n_in:]
    stats = [join_stat(ref) for ref in in_refs]
    largest = functools.reduce(jnp.maximum, stats)
    weights = [jnp.exp2(stat - largest) for stat in stats]
    total = functools.reduce(jnp.add, weights)
    inverse = 1.0 / total
    value = functools.reduce(
        jnp.add,
        [
            (weight * inverse) * ref[:HEAD_SIZE, :].astype(jnp.float32)
            for weight, ref in zip(weights, in_refs)
        ],
    ).astype(jnp.bfloat16)
    stat = largest + jnp.log2(total)
    part = out_refs[0].shape[1]
    for i, out_ref in enumerate(out_refs):
        lanes = slice(i * part, (i + 1) * part)
        out_ref[:HEAD_SIZE, :] = value[:, lanes]
        if keep_stat:
            out_ref[HEAD_SIZE:, :] = split_stat(stat[:, lanes], part)


def merge(messages, parts, keep_stat=True):
    height, width = messages[0].shape
    height = height if keep_stat else HEAD_SIZE
    size = len(messages) * height * width
    return pl.pallas_call(
        functools.partial(merge_kernel, len(messages), keep_stat),
        out_shape=[jax.ShapeDtypeStruct((height, width // parts), jnp.bfloat16)] * parts,
        name="merge" if keep_stat else "finish",
        cost_estimate=pl.CostEstimate(flops=4 * size, bytes_accessed=4 * size, transcendentals=0),
        compiler_params=pltpu.CompilerParams(vmem_limit_bytes=8 << 20),
    )(*messages)


def gather_kernel(rows, *refs):
    *piece_refs, out_ref = refs
    group = len(piece_refs)
    own = lax.rem(lax.axis_index("tok"), group)
    per = piece_refs[0].shape[1] // rows
    for offset in range(group):
        for j in range(per):
            block = jnp.transpose(
                piece_refs[offset][:, j * rows : (j + 1) * rows].astype(jnp.float32)
            )
            start = pl.multiple_of(((own ^ offset) * per + j) * HEAD_SIZE, HEAD_SIZE)
            out_ref[:, pl.ds(start, HEAD_SIZE)] = block.astype(jnp.bfloat16)


def gather(pieces, rows):
    width = sum(piece.shape[1] for piece in pieces) // rows * HEAD_SIZE
    return pl.pallas_call(
        functools.partial(gather_kernel, rows),
        out_shape=jax.ShapeDtypeStruct((rows, width), jnp.bfloat16),
        name="gather",
        cost_estimate=pl.CostEstimate(
            flops=0, bytes_accessed=4 * rows * width, transcendentals=0
        ),
        compiler_params=pltpu.CompilerParams(vmem_limit_bytes=4 << 20),
    )(*pieces)


def project_kernel(half, start, left_ref, w_ref, out_ref):
    columns = out_ref.shape[1]
    if half is not None:
        start = (lax.axis_index("head") ^ half) * (w_ref.shape[1] // 2) + start
    start = pl.multiple_of(start, HEAD_SIZE)
    out_ref[...] = jnp.dot(
        left_ref[...], w_ref[:, pl.ds(start, columns)], preferred_element_type=jnp.float32
    ).astype(out_ref.dtype)


def project(left, out_weight, half, start, columns, kind):
    rows, depth = left.shape
    return pl.pallas_call(
        functools.partial(project_kernel, half, start),
        out_shape=jax.ShapeDtypeStruct((rows, columns), kind),
        in_specs=[pl.BlockSpec(memory_space=pltpu.VMEM)] * 2,
        out_specs=pl.BlockSpec(memory_space=pltpu.VMEM),
        name="project",
        cost_estimate=pl.CostEstimate(
            flops=2 * rows * depth * columns,
            bytes_accessed=2 * depth * columns,
            transcendentals=0,
        ),
        compiler_params=pltpu.CompilerParams(vmem_limit_bytes=24 << 20),
    )(left, out_weight)


def swap(x, bits, servers):
    return lax.ppermute(x, "tok", [(i, i ^ bits) for i in range(servers)])


def attend_grouped(queries, keys, values, task_slot, task_count, move):
    core, column, near, far = 1, 2, 4, 8
    rows = queries.shape[0]
    q_per_kv = HEADS // KVH
    part = q_per_kv * rows
    width = 2 * part

    keep, give = pack_queries(queries, 4, ((0, 2), (1, 3)))
    pieces = pack_cache(keys, values, 4, ((0,), (core,), (column,), (column | core,)))
    got = move(give, core)
    own = jnp.concatenate([keep[:part], got[:part]], axis=0)
    other = move(jnp.concatenate([keep[part:], got[part:]], axis=0), column)
    across = move(pieces[2], column)
    beyond = move(pieces[3], column | core)
    own_far = move(own, far)
    beside = move(pieces[1], core)
    other_far = move(other, far)
    both_near = move(jnp.concatenate([own, other], axis=0), near)
    own_last = move(own_far, near)
    other_last = move(other_far, near)

    calls = ((0, column), (near, near | column), (far, far | column), (far | near,), (far | near | column,))
    masks = active_masks(task_slot, task_count, calls, rows)
    chip_cache = lay_cache([pieces[0], beside], masks)

    def first(chunks, which, after):
        return attention(chunks, which, chip_cache, masks, width, after, 4, (0, core), ended=False)

    def second(chunks, which, after, before):
        return attention(
            chunks, which, cache, masks, width, after, 4, (column, column | core), before
        )

    def call(chunks, which, after):
        return attention(chunks, which, cache, masks, width, after, 4, range(4))

    own_state = first([own, other], 0, masks)
    near_state = first([both_near], 1, own_state[0])
    far_state = first([own_far, other_far], 2, near_state[0])
    cache = lay_cache([across, beyond], far_state[0], chip_cache)
    near_a, near_b = second([both_near], 1, far_state[0], near_state)
    far_a, far_b = second([own_far, other_far], 2, near_a, far_state)
    own_a, own_b = second([own, other], 0, far_a, own_state)
    (last_a,) = call([own_last], 3, own_a)
    (last_b,) = call([other_last], 4, last_a)

    far_b = move(far_b, far | column)
    last_a = move(last_a, near)
    last_b = move(last_b, far | near | column)
    near_b = move(near_b, near | column)
    near_a = move(near_a, near)
    own_b = move(own_b, column)
    (far_a,) = merge([far_a, last_a], 1)
    far_a = move(far_a, far)
    b_own, b_other = merge([own_b, near_b, far_b, last_b], 2, False)
    b_other = move(b_other, core)
    a_own, a_other = merge([own_a, near_a, far_a], 2, False)
    a_other = move(a_other, core)
    return [a_own, a_other, b_own, b_other]


def attend_general(queries, keys, values, task_slot, task_count, move, servers):
    assert task_slot.shape[0] == 1
    rows = queries.shape[0]
    width = HEADS // KVH * rows
    step = min(4, servers)
    calls = tuple(tuple(range(i, i + step)) for i in range(0, servers, step))
    (own,) = pack_queries(queries, 1, ((0,),))
    masks = active_masks(task_slot, task_count, calls, rows)
    cache = lay_cache(pack_cache(keys, values, 1, ((0,),)), masks)
    held = {0: own}
    bit = servers // 2
    while bit:
        held.update({d ^ bit: move(chunk, bit) for d, chunk in held.items()})
        bit //= 2
    partial = {}
    for which, call in enumerate(calls):
        result = attention(
            [held[d] for d in call], which, cache, masks, width, masks, 1, range(1)
        )
        for j, d in enumerate(call):
            partial[d] = [result[j]]
    bit = 1
    while bit < servers:
        for d in sorted(partial, reverse=True):
            if d & bit:
                messages = partial.pop(d)
                message = messages[0] if len(messages) == 1 else merge(messages, 1)[0]
                partial[d ^ bit].append(move(message, bit))
        bit *= 2
    return merge(partial[0], 1, False)


def on_device(queries, keys, values, out_weight, task_slot, task_count):
    servers = lax.axis_size("tok")
    heads = lax.axis_size("head")
    rows = queries.shape[0]
    group = task_slot.shape[0]
    move = functools.partial(swap, servers=servers)
    if group == 4 and servers == 16:
        attended = attend_grouped(queries, keys, values, task_slot, task_count, move)
    else:
        attended = attend_general(queries, keys, values, task_slot, task_count, move, servers)
    left = gather(attended, rows)

    columns = out_weight.shape[1] // heads
    if heads == 2:
        return exchange_halves(left, out_weight, columns)
    share = project(left, out_weight, None, 0, out_weight.shape[1], jnp.bfloat16)
    return lax.psum_scatter(share, "head", scatter_dimension=1, tiled=True)


def exchange_halves(left, out_weight, columns):
    piece = columns // 2
    arrived = []
    for i in range(2):
        part = project(left, out_weight, 1, i * piece, piece, jnp.bfloat16)
        arrived.append(lax.ppermute(part, "head", [(0, 1), (1, 0)]))
    here = project(left, out_weight, 0, 0, columns, jnp.float32)
    return (here + jnp.concatenate(arrived, axis=1).astype(jnp.float32)).astype(jnp.bfloat16)


def solution(mesh):
    placed = (
        P("tok", "head"),
        P("tok", "head"),
        P("tok", "head"),
        P("head", None),
        P("head", None, None),
        P("head", None),
    )
    return jax.shard_map(
        on_device, mesh=mesh, in_specs=placed, out_specs=P("tok", "head"), check_vma=False
    )
```

```python
import functools
import math

import jax
import jax.numpy as jnp
from jax import lax
from jax.experimental import pallas as pl
from jax.experimental.pallas import tpu as pltpu
from jax.sharding import PartitionSpec as P


HEADS = 32
KVH = 8
HEAD_SIZE = 128
QBLK = 128

theta_base = 500000.0
neg_fill = -1e30
LOG2E = math.log2(math.e)
STAT_ROWS = 8
SUM_ROWS = 16
PACK_VMEM = 47 << 20


def rotary_tables(rows, first_row):
    half = HEAD_SIZE // 2
    frequency = theta_base ** (-(jnp.arange(half, dtype=jnp.float32) * (2.0 / HEAD_SIZE)))
    places = (first_row + jnp.arange(rows, dtype=jnp.int32)).astype(jnp.float32)
    angles = places[:, None] * frequency[None, :]
    cosine = jnp.cos(angles)
    sine = jnp.sin(angles)
    return (
        jnp.concatenate([cosine, cosine], axis=1),
        jnp.concatenate([-sine, sine], axis=1),
    )


def pack_queries_kernel(order, q_per_kv, group, cos_ref, sin_ref, q_ref, *out_refs):
    own = lax.rem(lax.axis_index("tok"), group)
    rows = q_ref.shape[0]
    cosine = cos_ref[...]
    sine = sin_ref[...]
    for offsets, out_ref in zip(order, out_refs):
        for at, offset in enumerate(offsets):
            head = own ^ offset
            for j in range(q_per_kv):
                start = pl.multiple_of((head * q_per_kv + j) * HEAD_SIZE, HEAD_SIZE)
                x = q_ref[:, pl.ds(start, HEAD_SIZE)].astype(jnp.float32)
                turned = pltpu.roll(x, HEAD_SIZE // 2, 1)
                row = (at * q_per_kv + j) * rows
                out_ref[row : row + rows, :] = (x * cosine + turned * sine).astype(jnp.bfloat16)


def pack_queries(queries, group, order):
    rows = queries.shape[0]
    q_per_kv = HEADS // KVH
    cosine, sine = rotary_tables(rows, lax.axis_index("tok") * rows)
    return pl.pallas_call(
        functools.partial(pack_queries_kernel, order, q_per_kv, group),
        out_shape=[
            jax.ShapeDtypeStruct((len(offsets) * q_per_kv * rows, HEAD_SIZE), jnp.bfloat16)
            for offsets in order
        ],
        name="pack_queries",
        cost_estimate=pl.CostEstimate(
            flops=6 * queries.size, bytes_accessed=4 * queries.size, transcendentals=0
        ),
        compiler_params=pltpu.CompilerParams(vmem_limit_bytes=PACK_VMEM),
    )(cosine, sine, queries)


def pack_cache_kernel(order, group, k_ref, v_ref, *out_refs):
    own = lax.rem(lax.axis_index("tok"), group)
    keys = k_ref.shape[0]
    for offsets, out_ref in zip(order, out_refs):
        for at, offset in enumerate(offsets):
            start = pl.multiple_of((own ^ offset) * HEAD_SIZE, HEAD_SIZE)
            row = 2 * at * keys
            out_ref[row : row + keys, :] = k_ref[:, pl.ds(start, HEAD_SIZE)]
            out_ref[row + keys : row + 2 * keys, :] = v_ref[:, pl.ds(start, HEAD_SIZE)]


def pack_cache(keys, values, group, order):
    return pl.pallas_call(
        functools.partial(pack_cache_kernel, order, group),
        out_shape=[
            jax.ShapeDtypeStruct((len(offsets) * 2 * keys.shape[0], HEAD_SIZE), jnp.bfloat16)
            for offsets in order
        ],
        name="pack_cache",
        cost_estimate=pl.CostEstimate(
            flops=0, bytes_accessed=8 * keys.size, transcendentals=0
        ),
        compiler_params=pltpu.CompilerParams(vmem_limit_bytes=PACK_VMEM),
    )(keys, values)


def mask_kernel(calls, rows, slot_hbm, count_hbm, mask_ref, slot_ref, count_ref, sems):
    server = lax.axis_index("tok")
    group = slot_ref.shape[0]
    own = lax.rem(server, group)
    copies = [
        pltpu.make_async_copy(slot_hbm, slot_ref, sems.at[0]),
        pltpu.make_async_copy(count_hbm, count_ref, sems.at[1]),
    ]
    for copy in copies:
        copy.start()
    for copy in copies:
        copy.wait()
    for call, displacements in enumerate(calls):
        mask = jnp.int32(0)
        for i, displacement in enumerate(displacements):
            block = ((server ^ displacement) * rows) // QBLK
            for k in range(group):
                key_block = server ^ k
                slot = slot_ref[own, block, key_block]
                active = (slot >= 0) & (slot < count_ref[own, key_block])
                mask = mask | (active.astype(jnp.int32) << (i * group + k))
        mask_ref[call] = jnp.full(mask_ref.shape[1:], mask, jnp.int32)


def active_masks(task_slot, task_count, calls, rows):
    hbm = pl.BlockSpec(memory_space=pltpu.HBM)
    return pl.pallas_call(
        functools.partial(mask_kernel, calls, rows),
        out_shape=jax.ShapeDtypeStruct((len(calls), 8, HEAD_SIZE), jnp.int32),
        in_specs=[hbm] * 2,
        scratch_shapes=[
            pltpu.SMEM(task_slot.shape, task_slot.dtype),
            pltpu.SMEM(task_count.shape, task_count.dtype),
            pltpu.SemaphoreType.DMA((2,)),
        ],
        name="masks",
        cost_estimate=pl.CostEstimate(
            flops=0, bytes_accessed=4 * task_slot.size, transcendentals=0
        ),
        compiler_params=pltpu.CompilerParams(vmem_limit_bytes=4 << 20),
    )(task_slot, task_count)


def lay_cache_kernel(laid, *refs):
    *in_refs, _, k_ref, v_ref = refs
    keys = k_ref.shape[1]
    if laid:
        k_ref[:laid] = in_refs[0][...]
        v_ref[:laid] = in_refs[1][...]
        in_refs = in_refs[2:]
    for at, ref in enumerate(in_refs, laid):
        k_ref[at] = ref[:keys, :]
        v_ref[at, :HEAD_SIZE, :] = jnp.transpose(ref[keys:, :].astype(jnp.float32)).astype(
            jnp.bfloat16
        )
        v_ref[at, HEAD_SIZE:, :] = jnp.ones((SUM_ROWS, keys), jnp.bfloat16)


def lay_cache(pieces, after, before=()):
    vmem = pl.BlockSpec(memory_space=pltpu.VMEM)
    laid = before[0].shape[0] if before else 0
    group = laid + len(pieces)
    keys = pieces[0].shape[0] // 2
    return pl.pallas_call(
        functools.partial(lay_cache_kernel, laid),
        out_shape=[
            jax.ShapeDtypeStruct((group, keys, HEAD_SIZE), jnp.bfloat16),
            jax.ShapeDtypeStruct((group, HEAD_SIZE + SUM_ROWS, keys), jnp.bfloat16),
        ],
        in_specs=[vmem] * (len(before) + len(pieces)) + [pl.BlockSpec(memory_space=pl.ANY)],
        name="lay_cache",
        cost_estimate=pl.CostEstimate(
            flops=0, bytes_accessed=8 * group * keys * HEAD_SIZE, transcendentals=0
        ),
        compiler_params=pltpu.CompilerParams(vmem_limit_bytes=8 << 20),
    )(*before, *pieces, after)


def split_stat(stat, width):
    high = stat.astype(jnp.bfloat16).astype(jnp.float32)
    rest = stat - high
    middle = rest.astype(jnp.bfloat16).astype(jnp.float32)
    low = rest - middle
    row = lax.broadcasted_iota(jnp.int32, (STAT_ROWS, width), 0)
    spread = jnp.where(row == 0, high, jnp.where(row == 1, middle, jnp.where(row == 2, low, 0.0)))
    return spread.astype(jnp.bfloat16)


def join_stat(ref):
    stat = ref[HEAD_SIZE : HEAD_SIZE + STAT_ROWS, :].astype(jnp.float32)
    return stat[0:1] + stat[1:2] + stat[2:3]


def attention_kernel(plan, mask_ref, *refs):
    which, widths, slab, group, blocks, resumed, ended = plan
    n_chunks = sum(widths)
    n_in = len(widths)
    q_in_refs = refs[:n_in]
    k_ref, v_ref, _ = refs[n_in : n_in + 3]
    at = n_in + 3
    before_refs = refs[at : at + 2 * resumed]
    at += 2 * resumed
    n_out = n_chunks if ended else 2
    out_refs = refs[at : at + n_out]
    at += n_out
    if ended:
        m_ref, acc_ref = refs[at : at + 2]
        at += 2
    else:
        m_ref, acc_ref = out_refs
    list_ref, q_ref, *slots = refs[at:]
    width = q_ref.shape[1]
    scale = HEAD_SIZE ** (-0.5) * LOG2E

    mask = mask_ref[which, 0, 0]
    found = jnp.int32(0)
    for i in range(n_chunks):
        for k in blocks:
            entry = i * group + k
            list_ref[found] = entry
            found = found + ((mask >> entry) & 1)

    at = 0
    for q_in_ref, n in zip(q_in_refs, widths):
        for i in range(n):
            q_ref[at + i] = q_in_ref[i * width : (i + 1) * width, :]
        at += n
    if resumed:
        m_ref[...] = before_refs[0][...]
        acc_ref[...] = before_refs[1][...]
    else:
        m_ref[...] = jnp.full_like(m_ref, neg_fill)
        acc_ref[...] = jnp.zeros_like(acc_ref)

    def pair(i):
        entry = list_ref[i]
        return entry // group, lax.rem(entry, group)

    def score(i, slot):
        chunk, k = pair(i)
        s_ref, top_ref, fade_ref = slot
        for c in range(0, width, slab):
            scores = lax.dot_general(
                k_ref[k],
                q_ref[chunk, c : c + slab, :],
                (((1,), (1,)), ((), ())),
                preferred_element_type=jnp.float32,
            )
            s_ref[:, c : c + slab] = scores
            old = m_ref[chunk, :, c : c + slab]
            new = jnp.maximum(old, jnp.max(scores, axis=0, keepdims=True))
            m_ref[chunk, :, c : c + slab] = new
            top_ref[:, c : c + slab] = new
            fade_ref[:, c : c + slab] = jnp.exp2((old - new) * scale)

    def weigh(i, slot):
        chunk, k = pair(i)
        s_ref, top_ref, fade_ref = slot
        for c in range(0, width, slab):
            p = jnp.exp2((s_ref[:, c : c + slab] - top_ref[0:1, c : c + slab]) * scale)
            product = jnp.dot(
                v_ref[k], p.astype(jnp.bfloat16), preferred_element_type=jnp.float32
            )
            acc_ref[chunk, :, c : c + slab] = (
                acc_ref[chunk, :, c : c + slab] * fade_ref[0:1, c : c + slab] + product
            )

    even, odd = slots[:3], slots[3:]

    @pl.when(found > 0)
    def _():
        score(0, even)

    def step(i, here, there):
        @pl.when(i + 1 < found)
        def _():
            score(i + 1, there)
            weigh(i, here)

        @pl.when(i + 1 == found)
        def _():
            weigh(i, here)

    def two(j, carry):
        step(2 * j, even, odd)
        step(2 * j + 1, odd, even)
        return carry

    lax.fori_loop(0, (found + 1) // 2, two, 0)

    if not ended:
        return
    for i in range(n_chunks):
        total = acc_ref[i, HEAD_SIZE : HEAD_SIZE + 1, :]
        seen = total > 0.0
        safe = jnp.where(seen, total, 1.0)
        stat = jnp.where(seen, m_ref[i, 0:1, :] * scale + jnp.log2(safe), neg_fill)
        out_refs[i][:HEAD_SIZE, :] = (acc_ref[i, :HEAD_SIZE, :] * (1.0 / safe)).astype(jnp.bfloat16)
        out_refs[i][HEAD_SIZE:, :] = split_stat(stat, width)


def attention(chunks, which, cache, masks, width, after, group, blocks, before=(), ended=True):
    k, v = cache
    keys = k.shape[1]
    widths = tuple(chunk.shape[0] // width for chunk in chunks)
    n = sum(widths)
    vmem = pl.BlockSpec(memory_space=pltpu.VMEM)
    state = [(n, 8, width), (n, HEAD_SIZE + SUM_ROWS, width)]
    slot = [
        pltpu.VMEM((keys, width), jnp.float32),
        pltpu.VMEM((8, width), jnp.float32),
        pltpu.VMEM((8, width), jnp.float32),
    ]
    if ended:
        out_shape = [jax.ShapeDtypeStruct((HEAD_SIZE + STAT_ROWS, width), jnp.bfloat16)] * n
        scratch = [pltpu.VMEM(shape, jnp.float32) for shape in state]
    else:
        out_shape = [jax.ShapeDtypeStruct(shape, jnp.float32) for shape in state]
        scratch = []
    pairs = n * len(blocks)
    plan = (which, widths, min(256, width), group, tuple(blocks), bool(before), ended)
    return pl.pallas_call(
        functools.partial(attention_kernel, plan),
        out_shape=out_shape,
        in_specs=[vmem] * (len(chunks) + 3)
        + [pl.BlockSpec(memory_space=pl.ANY)]
        + [vmem] * len(before),
        out_specs=[vmem] * len(out_shape),
        scratch_shapes=scratch
        + [
            pltpu.SMEM((pairs + 1,), jnp.int32),
            pltpu.VMEM((n, width, HEAD_SIZE), jnp.bfloat16),
        ]
        + slot
        + slot,
        name="attention",
        cost_estimate=pl.CostEstimate(
            flops=4 * pairs * keys * width * HEAD_SIZE,
            bytes_accessed=4 * n * width * HEAD_SIZE + 4 * len(blocks) * keys * HEAD_SIZE,
            transcendentals=pairs * keys * width,
        ),
        compiler_params=pltpu.CompilerParams(vmem_limit_bytes=16 << 20),
    )(masks, *chunks, k, v, after, *before)


def merge_kernel(lanes, keep_stat, *refs):
    in_refs, out_refs = refs[: len(lanes)], refs[len(lanes) :]
    in_refs = [ref.at[:, span] for ref, span in zip(in_refs, lanes)]
    stats = [join_stat(ref) for ref in in_refs]
    largest = functools.reduce(jnp.maximum, stats)
    weights = [jnp.exp2(stat - largest) for stat in stats]
    total = functools.reduce(jnp.add, weights)
    inverse = 1.0 / total
    value = functools.reduce(
        jnp.add,
        [
            (weight * inverse) * ref[:HEAD_SIZE, :].astype(jnp.float32)
            for weight, ref in zip(weights, in_refs)
        ],
    ).astype(jnp.bfloat16)
    stat = largest + jnp.log2(total)
    part = out_refs[0].shape[1]
    for i, out_ref in enumerate(out_refs):
        span = slice(i * part, (i + 1) * part)
        out_ref[:HEAD_SIZE, :] = value[:, span]
        if keep_stat:
            out_ref[HEAD_SIZE:, :] = split_stat(stat[:, span], part)


def merge(messages, parts, keep_stat=True):
    height, width = messages[0].shape
    height = height if keep_stat else HEAD_SIZE
    size = len(messages) * height * width
    pairs = [m if isinstance(m, tuple) else (m, 0) for m in messages]
    lanes = tuple(slice(i * width, (i + 1) * width) for _, i in pairs)
    return pl.pallas_call(
        functools.partial(merge_kernel, lanes, keep_stat),
        out_shape=[jax.ShapeDtypeStruct((height, width // parts), jnp.bfloat16)] * parts,
        name="merge" if keep_stat else "finish",
        cost_estimate=pl.CostEstimate(flops=4 * size, bytes_accessed=4 * size, transcendentals=0),
        compiler_params=pltpu.CompilerParams(vmem_limit_bytes=8 << 20),
    )(*[array for array, _ in pairs])


def gather_kernel(rows, *refs):
    *piece_refs, out_ref = refs
    group = len(piece_refs)
    own = lax.rem(lax.axis_index("tok"), group)
    per = piece_refs[0].shape[1] // rows
    for offset in range(group):
        for j in range(per):
            block = jnp.transpose(
                piece_refs[offset][:, j * rows : (j + 1) * rows].astype(jnp.float32)
            )
            start = pl.multiple_of(((own ^ offset) * per + j) * HEAD_SIZE, HEAD_SIZE)
            out_ref[:, pl.ds(start, HEAD_SIZE)] = block.astype(jnp.bfloat16)


def gather(pieces, rows):
    width = sum(piece.shape[1] for piece in pieces) // rows * HEAD_SIZE
    return pl.pallas_call(
        functools.partial(gather_kernel, rows),
        out_shape=jax.ShapeDtypeStruct((rows, width), jnp.bfloat16),
        name="gather",
        cost_estimate=pl.CostEstimate(
            flops=0, bytes_accessed=4 * rows * width, transcendentals=0
        ),
        compiler_params=pltpu.CompilerParams(vmem_limit_bytes=4 << 20),
    )(*pieces)


def project_kernel(half, start, left_ref, w_ref, out_ref):
    columns = out_ref.shape[1]
    if half is not None:
        start = (lax.axis_index("head") ^ half) * (w_ref.shape[1] // 2) + start
    start = pl.multiple_of(start, HEAD_SIZE)
    out_ref[...] = jnp.dot(
        left_ref[...], w_ref[:, pl.ds(start, columns)], preferred_element_type=jnp.float32
    ).astype(out_ref.dtype)


def project(left, out_weight, half, start, columns, kind):
    rows, depth = left.shape
    return pl.pallas_call(
        functools.partial(project_kernel, half, start),
        out_shape=jax.ShapeDtypeStruct((rows, columns), kind),
        in_specs=[pl.BlockSpec(memory_space=pltpu.VMEM)] * 2,
        out_specs=pl.BlockSpec(memory_space=pltpu.VMEM),
        name="project",
        cost_estimate=pl.CostEstimate(
            flops=2 * rows * depth * columns,
            bytes_accessed=2 * depth * columns,
            transcendentals=0,
        ),
        compiler_params=pltpu.CompilerParams(vmem_limit_bytes=24 << 20),
    )(left, out_weight)


def swap(x, bits, servers):
    return lax.ppermute(x, "tok", [(i, i ^ bits) for i in range(servers)])


def attend_grouped(queries, keys, values, task_slot, task_count, move):
    core, column, near, far = 1, 2, 4, 8
    rows = queries.shape[0]
    q_per_kv = HEADS // KVH
    part = q_per_kv * rows
    width = 2 * part

    keep, give = pack_queries(queries, 4, ((0, 2), (1, 3)))
    pieces = pack_cache(keys, values, 4, ((0,), (core,), (column,), (column | core,)))
    got = move(give, core)
    own = jnp.concatenate([keep[:part], got[:part]], axis=0)
    other = move(jnp.concatenate([keep[part:], got[part:]], axis=0), column)
    across = move(pieces[2], column)
    beyond = move(pieces[3], column | core)
    own_far = move(own, far)
    beside = move(pieces[1], core)
    other_far = move(other, far)
    own_near = move(own, near)
    other_near = move(other, near)
    own_last = move(own_far, near)
    other_last = move(other_far, near)

    calls = (
        (0, column),
        (near, far),
        (near | column, far | column),
        (far | near,),
        (far | near | column,),
    )
    masks = active_masks(task_slot, task_count, calls, rows)
    chip_cache = lay_cache([pieces[0], beside], masks)

    def first(chunks, which, after):
        return attention(chunks, which, chip_cache, masks, width, after, 4, (0, core), ended=False)

    def second(chunks, which, after, before):
        return attention(
            chunks, which, cache, masks, width, after, 4, (column, column | core), before
        )

    def call(chunks, which, after):
        return attention(chunks, which, cache, masks, width, after, 4, range(4))

    own_state = first([own, other], 0, masks)
    a_state = first([own_near, own_far], 1, own_state[0])
    b_state = first([other_near, other_far], 2, a_state[0])
    cache = lay_cache([across, beyond], b_state[0], chip_cache)
    near_b, far_b = second([other_near, other_far], 2, b_state[0], b_state)
    near_a, far_a = second([own_near, own_far], 1, far_b, a_state)
    own_a, own_b = second([own, other], 0, far_a, own_state)
    (last_a,) = call([own_last], 3, own_a)
    (last_b,) = call([other_last], 4, last_a)

    far_b = move(far_b, far | column)
    a_back = move(jnp.concatenate([near_a, last_a], axis=1), near)
    last_b = move(last_b, far | near | column)
    near_b = move(near_b, near | column)
    own_b = move(own_b, column)
    (far_a,) = merge([far_a, (a_back, 1)], 1)
    far_a = move(far_a, far)
    b_own, b_other = merge([own_b, near_b, far_b, last_b], 2, False)
    b_other = move(b_other, core)
    a_own, a_other = merge([own_a, (a_back, 0), far_a], 2, False)
    a_other = move(a_other, core)
    return [a_own, a_other, b_own, b_other]


def attend_general(queries, keys, values, task_slot, task_count, move, servers):
    assert task_slot.shape[0] == 1
    rows = queries.shape[0]
    width = HEADS // KVH * rows
    step = min(4, servers)
    calls = tuple(tuple(range(i, i + step)) for i in range(0, servers, step))
    (own,) = pack_queries(queries, 1, ((0,),))
    masks = active_masks(task_slot, task_count, calls, rows)
    cache = lay_cache(pack_cache(keys, values, 1, ((0,),)), masks)
    held = {0: own}
    bit = servers // 2
    while bit:
        held.update({d ^ bit: move(chunk, bit) for d, chunk in held.items()})
        bit //= 2
    partial = {}
    for which, call in enumerate(calls):
        result = attention(
            [held[d] for d in call], which, cache, masks, width, masks, 1, range(1)
        )
        for j, d in enumerate(call):
            partial[d] = [result[j]]
    bit = 1
    while bit < servers:
        for d in sorted(partial, reverse=True):
            if d & bit:
                messages = partial.pop(d)
                message = messages[0] if len(messages) == 1 else merge(messages, 1)[0]
                partial[d ^ bit].append(move(message, bit))
        bit *= 2
    return merge(partial[0], 1, False)


def on_device(queries, keys, values, out_weight, task_slot, task_count):
    servers = lax.axis_size("tok")
    heads = lax.axis_size("head")
    rows = queries.shape[0]
    group = task_slot.shape[0]
    move = functools.partial(swap, servers=servers)
    if group == 4 and servers == 16:
        attended = attend_grouped(queries, keys, values, task_slot, task_count, move)
    else:
        attended = attend_general(queries, keys, values, task_slot, task_count, move, servers)
    left = gather(attended, rows)

    columns = out_weight.shape[1] // heads
    if heads == 2:
        return exchange_halves(left, out_weight, columns)
    share = project(left, out_weight, None, 0, out_weight.shape[1], jnp.bfloat16)
    return lax.psum_scatter(share, "head", scatter_dimension=1, tiled=True)


def exchange_halves(left, out_weight, columns):
    piece = columns // 2
    arrived = []
    for i in range(2):
        part = project(left, out_weight, 1, i * piece, piece, jnp.bfloat16)
        arrived.append(lax.ppermute(part, "head", [(0, 1), (1, 0)]))
    here = project(left, out_weight, 0, 0, columns, jnp.float32)
    return (here + jnp.concatenate(arrived, axis=1).astype(jnp.float32)).astype(jnp.bfloat16)


def solution(mesh):
    placed = (
        P("tok", "head"),
        P("tok", "head"),
        P("tok", "head"),
        P("head", None),
        P("head", None, None),
        P("head", None),
    )
    return jax.shard_map(
        on_device, mesh=mesh, in_specs=placed, out_specs=P("tok", "head"), check_vma=False
    )
```

```python
import functools
import math

import jax
import jax.numpy as jnp
from jax import lax
from jax.experimental import pallas as pl
from jax.experimental.pallas import tpu as pltpu
from jax.sharding import PartitionSpec as P


HEADS = 32
KVH = 8
HEAD_SIZE = 128
QBLK = 128

theta_base = 500000.0
neg_fill = -1e30
LOG2E = math.log2(math.e)
STAT_ROWS = 8
SUM_ROWS = 16
PACK_VMEM = 47 << 20


def rotary_tables(rows, first_row):
    half = HEAD_SIZE // 2
    frequency = theta_base ** (-(jnp.arange(half, dtype=jnp.float32) * (2.0 / HEAD_SIZE)))
    places = (first_row + jnp.arange(rows, dtype=jnp.int32)).astype(jnp.float32)
    angles = places[:, None] * frequency[None, :]
    cosine = jnp.cos(angles)
    sine = jnp.sin(angles)
    return (
        jnp.concatenate([cosine, cosine], axis=1),
        jnp.concatenate([-sine, sine], axis=1),
    )


def pack_queries_kernel(order, q_per_kv, group, cos_ref, sin_ref, q_ref, *out_refs):
    own = lax.rem(lax.axis_index("tok"), group)
    rows = q_ref.shape[0]
    cosine = cos_ref[...]
    sine = sin_ref[...]
    for offsets, out_ref in zip(order, out_refs):
        for at, offset in enumerate(offsets):
            head = own ^ offset
            for j in range(q_per_kv):
                start = pl.multiple_of((head * q_per_kv + j) * HEAD_SIZE, HEAD_SIZE)
                x = q_ref[:, pl.ds(start, HEAD_SIZE)].astype(jnp.float32)
                turned = pltpu.roll(x, HEAD_SIZE // 2, 1)
                row = (at * q_per_kv + j) * rows
                out_ref[row : row + rows, :] = (x * cosine + turned * sine).astype(jnp.bfloat16)


def pack_queries(queries, group, order):
    rows = queries.shape[0]
    q_per_kv = HEADS // KVH
    cosine, sine = rotary_tables(rows, lax.axis_index("tok") * rows)
    return pl.pallas_call(
        functools.partial(pack_queries_kernel, order, q_per_kv, group),
        out_shape=[
            jax.ShapeDtypeStruct((len(offsets) * q_per_kv * rows, HEAD_SIZE), jnp.bfloat16)
            for offsets in order
        ],
        name="pack_queries",
        cost_estimate=pl.CostEstimate(
            flops=6 * queries.size, bytes_accessed=4 * queries.size, transcendentals=0
        ),
        compiler_params=pltpu.CompilerParams(vmem_limit_bytes=PACK_VMEM),
    )(cosine, sine, queries)


def pack_cache_kernel(order, group, k_ref, v_ref, *out_refs):
    own = lax.rem(lax.axis_index("tok"), group)
    keys = k_ref.shape[0]
    for offsets, out_ref in zip(order, out_refs):
        for at, offset in enumerate(offsets):
            start = pl.multiple_of((own ^ offset) * HEAD_SIZE, HEAD_SIZE)
            row = 2 * at * keys
            out_ref[row : row + keys, :] = k_ref[:, pl.ds(start, HEAD_SIZE)]
            out_ref[row + keys : row + 2 * keys, :] = v_ref[:, pl.ds(start, HEAD_SIZE)]


def pack_cache(keys, values, group, order):
    return pl.pallas_call(
        functools.partial(pack_cache_kernel, order, group),
        out_shape=[
            jax.ShapeDtypeStruct((len(offsets) * 2 * keys.shape[0], HEAD_SIZE), jnp.bfloat16)
            for offsets in order
        ],
        name="pack_cache",
        cost_estimate=pl.CostEstimate(
            flops=0, bytes_accessed=8 * keys.size, transcendentals=0
        ),
        compiler_params=pltpu.CompilerParams(vmem_limit_bytes=PACK_VMEM),
    )(keys, values)


def mask_kernel(calls, rows, slot_hbm, count_hbm, mask_ref, slot_ref, count_ref, sems):
    server = lax.axis_index("tok")
    group = slot_ref.shape[0]
    own = lax.rem(server, group)
    copies = [
        pltpu.make_async_copy(slot_hbm, slot_ref, sems.at[0]),
        pltpu.make_async_copy(count_hbm, count_ref, sems.at[1]),
    ]
    for copy in copies:
        copy.start()
    for copy in copies:
        copy.wait()
    for call, displacements in enumerate(calls):
        mask = jnp.int32(0)
        for i, displacement in enumerate(displacements):
            block = ((server ^ displacement) * rows) // QBLK
            for k in range(group):
                key_block = server ^ k
                slot = slot_ref[own, block, key_block]
                active = (slot >= 0) & (slot < count_ref[own, key_block])
                mask = mask | (active.astype(jnp.int32) << (i * group + k))
        mask_ref[call] = jnp.full(mask_ref.shape[1:], mask, jnp.int32)


def active_masks(task_slot, task_count, calls, rows):
    hbm = pl.BlockSpec(memory_space=pltpu.HBM)
    return pl.pallas_call(
        functools.partial(mask_kernel, calls, rows),
        out_shape=jax.ShapeDtypeStruct((len(calls), 8, HEAD_SIZE), jnp.int32),
        in_specs=[hbm] * 2,
        scratch_shapes=[
            pltpu.SMEM(task_slot.shape, task_slot.dtype),
            pltpu.SMEM(task_count.shape, task_count.dtype),
            pltpu.SemaphoreType.DMA((2,)),
        ],
        name="masks",
        cost_estimate=pl.CostEstimate(
            flops=0, bytes_accessed=4 * task_slot.size, transcendentals=0
        ),
        compiler_params=pltpu.CompilerParams(vmem_limit_bytes=4 << 20),
    )(task_slot, task_count)


def lay_cache_kernel(laid, *refs):
    *in_refs, _, k_ref, v_ref = refs
    keys = k_ref.shape[1]
    if laid:
        k_ref[:laid] = in_refs[0][...]
        v_ref[:laid] = in_refs[1][...]
        in_refs = in_refs[2:]
    for at, ref in enumerate(in_refs, laid):
        k_ref[at] = ref[:keys, :]
        v_ref[at, :HEAD_SIZE, :] = jnp.transpose(ref[keys:, :].astype(jnp.float32)).astype(
            jnp.bfloat16
        )
        v_ref[at, HEAD_SIZE:, :] = jnp.ones((SUM_ROWS, keys), jnp.bfloat16)


def lay_cache(pieces, after, before=()):
    vmem = pl.BlockSpec(memory_space=pltpu.VMEM)
    laid = before[0].shape[0] if before else 0
    group = laid + len(pieces)
    keys = pieces[0].shape[0] // 2
    return pl.pallas_call(
        functools.partial(lay_cache_kernel, laid),
        out_shape=[
            jax.ShapeDtypeStruct((group, keys, HEAD_SIZE), jnp.bfloat16),
            jax.ShapeDtypeStruct((group, HEAD_SIZE + SUM_ROWS, keys), jnp.bfloat16),
        ],
        in_specs=[vmem] * (len(before) + len(pieces)) + [pl.BlockSpec(memory_space=pl.ANY)],
        name="lay_cache",
        cost_estimate=pl.CostEstimate(
            flops=0, bytes_accessed=8 * group * keys * HEAD_SIZE, transcendentals=0
        ),
        compiler_params=pltpu.CompilerParams(vmem_limit_bytes=8 << 20),
    )(*before, *pieces, after)


def split_stat(stat, width):
    high = stat.astype(jnp.bfloat16).astype(jnp.float32)
    rest = stat - high
    middle = rest.astype(jnp.bfloat16).astype(jnp.float32)
    low = rest - middle
    row = lax.broadcasted_iota(jnp.int32, (STAT_ROWS, width), 0)
    spread = jnp.where(row == 0, high, jnp.where(row == 1, middle, jnp.where(row == 2, low, 0.0)))
    return spread.astype(jnp.bfloat16)


def join_stat(ref):
    stat = ref[HEAD_SIZE : HEAD_SIZE + STAT_ROWS, :].astype(jnp.float32)
    return stat[0:1] + stat[1:2] + stat[2:3]


def attention_kernel(plan, mask_ref, *refs):
    which, widths, slab, group, blocks, resumed, ended = plan
    n_chunks = sum(widths)
    n_in = len(widths)
    q_in_refs = refs[:n_in]
    k_ref, v_ref, _ = refs[n_in : n_in + 3]
    at = n_in + 3
    before_refs = refs[at : at + 2 * resumed]
    at += 2 * resumed
    n_out = n_chunks if ended else 2
    out_refs = refs[at : at + n_out]
    at += n_out
    if ended:
        m_ref, acc_ref = refs[at : at + 2]
        at += 2
    else:
        m_ref, acc_ref = out_refs
    list_ref, q_ref, *slots = refs[at:]
    width = q_ref.shape[1]
    scale = HEAD_SIZE ** (-0.5) * LOG2E

    mask = mask_ref[which, 0, 0]
    found = jnp.int32(0)
    for i in range(n_chunks):
        for k in blocks:
            entry = i * group + k
            list_ref[found] = entry
            found = found + ((mask >> entry) & 1)

    at = 0
    for q_in_ref, n in zip(q_in_refs, widths):
        for i in range(n):
            q_ref[at + i] = q_in_ref[i * width : (i + 1) * width, :]
        at += n
    if resumed:
        m_ref[...] = before_refs[0][...]
        acc_ref[...] = before_refs[1][...]
    else:
        m_ref[...] = jnp.full_like(m_ref, neg_fill)
        acc_ref[...] = jnp.zeros_like(acc_ref)

    def pair(i):
        entry = list_ref[i]
        return entry // group, lax.rem(entry, group)

    def score(i, slot):
        chunk, k = pair(i)
        s_ref, top_ref, fade_ref = slot
        for c in range(0, width, slab):
            scores = lax.dot_general(
                k_ref[k],
                q_ref[chunk, c : c + slab, :],
                (((1,), (1,)), ((), ())),
                preferred_element_type=jnp.float32,
            )
            s_ref[:, c : c + slab] = scores
            old = m_ref[chunk, :, c : c + slab]
            new = jnp.maximum(old, jnp.max(scores, axis=0, keepdims=True))
            m_ref[chunk, :, c : c + slab] = new
            top_ref[:, c : c + slab] = new
            fade_ref[:, c : c + slab] = jnp.exp2((old - new) * scale)

    def weigh(i, slot):
        chunk, k = pair(i)
        s_ref, top_ref, fade_ref = slot
        for c in range(0, width, slab):
            p = jnp.exp2((s_ref[:, c : c + slab] - top_ref[0:1, c : c + slab]) * scale)
            product = jnp.dot(
                v_ref[k], p.astype(jnp.bfloat16), preferred_element_type=jnp.float32
            )
            acc_ref[chunk, :, c : c + slab] = (
                acc_ref[chunk, :, c : c + slab] * fade_ref[0:1, c : c + slab] + product
            )

    even, odd = slots[:3], slots[3:]

    @pl.when(found > 0)
    def _():
        score(0, even)

    def step(i, here, there):
        @pl.when(i + 1 < found)
        def _():
            score(i + 1, there)
            weigh(i, here)

        @pl.when(i + 1 == found)
        def _():
            weigh(i, here)

    def two(j, carry):
        step(2 * j, even, odd)
        step(2 * j + 1, odd, even)
        return carry

    lax.fori_loop(0, (found + 1) // 2, two, 0)

    if not ended:
        return
    for i in range(n_chunks):
        total = acc_ref[i, HEAD_SIZE : HEAD_SIZE + 1, :]
        seen = total > 0.0
        safe = jnp.where(seen, total, 1.0)
        stat = jnp.where(seen, m_ref[i, 0:1, :] * scale + jnp.log2(safe), neg_fill)
        out_refs[i][:HEAD_SIZE, :] = (acc_ref[i, :HEAD_SIZE, :] * (1.0 / safe)).astype(jnp.bfloat16)
        out_refs[i][HEAD_SIZE:, :] = split_stat(stat, width)


def attention(chunks, which, cache, masks, width, after, group, blocks, before=(), ended=True):
    k, v = cache
    keys = k.shape[1]
    widths = tuple(chunk.shape[0] // width for chunk in chunks)
    n = sum(widths)
    vmem = pl.BlockSpec(memory_space=pltpu.VMEM)
    state = [(n, 8, width), (n, HEAD_SIZE + SUM_ROWS, width)]
    slot = [
        pltpu.VMEM((keys, width), jnp.float32),
        pltpu.VMEM((8, width), jnp.float32),
        pltpu.VMEM((8, width), jnp.float32),
    ]
    if ended:
        out_shape = [jax.ShapeDtypeStruct((HEAD_SIZE + STAT_ROWS, width), jnp.bfloat16)] * n
        scratch = [pltpu.VMEM(shape, jnp.float32) for shape in state]
    else:
        out_shape = [jax.ShapeDtypeStruct(shape, jnp.float32) for shape in state]
        scratch = []
    pairs = n * len(blocks)
    plan = (which, widths, min(256, width), group, tuple(blocks), bool(before), ended)
    return pl.pallas_call(
        functools.partial(attention_kernel, plan),
        out_shape=out_shape,
        in_specs=[vmem] * (len(chunks) + 3)
        + [pl.BlockSpec(memory_space=pl.ANY)]
        + [vmem] * len(before),
        out_specs=[vmem] * len(out_shape),
        scratch_shapes=scratch
        + [
            pltpu.SMEM((pairs + 1,), jnp.int32),
            pltpu.VMEM((n, width, HEAD_SIZE), jnp.bfloat16),
        ]
        + slot
        + slot,
        name="attention",
        cost_estimate=pl.CostEstimate(
            flops=4 * pairs * keys * width * HEAD_SIZE,
            bytes_accessed=4 * n * width * HEAD_SIZE + 4 * len(blocks) * keys * HEAD_SIZE,
            transcendentals=pairs * keys * width,
        ),
        compiler_params=pltpu.CompilerParams(vmem_limit_bytes=16 << 20),
    )(masks, *chunks, k, v, after, *before)


def merge_kernel(n_in, keep_stat, *refs):
    in_refs, out_refs = refs[:n_in], refs[n_in:]
    stats = [join_stat(ref) for ref in in_refs]
    largest = functools.reduce(jnp.maximum, stats)
    weights = [jnp.exp2(stat - largest) for stat in stats]
    total = functools.reduce(jnp.add, weights)
    inverse = 1.0 / total
    value = functools.reduce(
        jnp.add,
        [
            (weight * inverse) * ref[:HEAD_SIZE, :].astype(jnp.float32)
            for weight, ref in zip(weights, in_refs)
        ],
    ).astype(jnp.bfloat16)
    stat = largest + jnp.log2(total)
    part = out_refs[0].shape[1]
    for i, out_ref in enumerate(out_refs):
        span = slice(i * part, (i + 1) * part)
        out_ref[:HEAD_SIZE, :] = value[:, span]
        if keep_stat:
            out_ref[HEAD_SIZE:, :] = split_stat(stat[:, span], part)


def merge(messages, parts, keep_stat=True):
    height, width = messages[0].shape
    height = height if keep_stat else HEAD_SIZE
    size = len(messages) * height * width
    return pl.pallas_call(
        functools.partial(merge_kernel, len(messages), keep_stat),
        out_shape=[jax.ShapeDtypeStruct((height, width // parts), jnp.bfloat16)] * parts,
        name="merge" if keep_stat else "finish",
        cost_estimate=pl.CostEstimate(flops=4 * size, bytes_accessed=4 * size, transcendentals=0),
        compiler_params=pltpu.CompilerParams(vmem_limit_bytes=8 << 20),
    )(*messages)


def gather_kernel(rows, *refs):
    *piece_refs, out_ref = refs
    group = len(piece_refs)
    own = lax.rem(lax.axis_index("tok"), group)
    per = piece_refs[0].shape[1] // rows
    for offset in range(group):
        for j in range(per):
            block = jnp.transpose(
                piece_refs[offset][:, j * rows : (j + 1) * rows].astype(jnp.float32)
            )
            start = pl.multiple_of(((own ^ offset) * per + j) * HEAD_SIZE, HEAD_SIZE)
            out_ref[:, pl.ds(start, HEAD_SIZE)] = block.astype(jnp.bfloat16)


def gather(pieces, rows):
    width = sum(piece.shape[1] for piece in pieces) // rows * HEAD_SIZE
    return pl.pallas_call(
        functools.partial(gather_kernel, rows),
        out_shape=jax.ShapeDtypeStruct((rows, width), jnp.bfloat16),
        name="gather",
        cost_estimate=pl.CostEstimate(
            flops=0, bytes_accessed=4 * rows * width, transcendentals=0
        ),
        compiler_params=pltpu.CompilerParams(vmem_limit_bytes=4 << 20),
    )(*pieces)


def project_kernel(half, start, left_ref, w_ref, out_ref):
    columns = out_ref.shape[1]
    if half is not None:
        start = (lax.axis_index("head") ^ half) * (w_ref.shape[1] // 2) + start
    start = pl.multiple_of(start, HEAD_SIZE)
    out_ref[...] = jnp.dot(
        left_ref[...], w_ref[:, pl.ds(start, columns)], preferred_element_type=jnp.float32
    ).astype(out_ref.dtype)


def project(left, out_weight, half, start, columns, kind):
    rows, depth = left.shape
    return pl.pallas_call(
        functools.partial(project_kernel, half, start),
        out_shape=jax.ShapeDtypeStruct((rows, columns), kind),
        in_specs=[pl.BlockSpec(memory_space=pltpu.VMEM)] * 2,
        out_specs=pl.BlockSpec(memory_space=pltpu.VMEM),
        name="project",
        cost_estimate=pl.CostEstimate(
            flops=2 * rows * depth * columns,
            bytes_accessed=2 * depth * columns,
            transcendentals=0,
        ),
        compiler_params=pltpu.CompilerParams(vmem_limit_bytes=24 << 20),
    )(left, out_weight)


def swap(x, bits, servers):
    return lax.ppermute(x, "tok", [(i, i ^ bits) for i in range(servers)])


def attend_grouped(queries, keys, values, task_slot, task_count, move):
    core, column, near, far = 1, 2, 4, 8
    rows = queries.shape[0]
    q_per_kv = HEADS // KVH
    part = q_per_kv * rows
    width = 2 * part

    keep, give = pack_queries(queries, 4, ((0, 2), (1, 3)))
    pieces = pack_cache(keys, values, 4, ((0,), (core,), (column,), (column | core,)))
    got = move(give, core)
    own = jnp.concatenate([keep[:part], got[:part]], axis=0)
    other = move(jnp.concatenate([keep[part:], got[part:]], axis=0), column)
    across = move(pieces[2], column)
    beyond = move(pieces[3], column | core)
    own_far = move(own, far)
    beside = move(pieces[1], core)
    other_far = move(other, far)
    own_near = move(own, near)
    other_near = move(other, near)
    own_last = move(own_far, near)
    other_last = move(other_far, near)

    calls = (
        (0, column),
        (near, far),
        (near | column, far | column),
        (far | near,),
        (far | near | column,),
    )
    masks = active_masks(task_slot, task_count, calls, rows)
    chip_cache = lay_cache([pieces[0], beside], masks)

    def first(chunks, which, after):
        return attention(chunks, which, chip_cache, masks, width, after, 4, (0, core), ended=False)

    def second(chunks, which, after, before):
        return attention(
            chunks, which, cache, masks, width, after, 4, (column, column | core), before
        )

    def call(chunks, which, after):
        return attention(chunks, which, cache, masks, width, after, 4, range(4))

    own_state = first([own, other], 0, masks)
    a_state = first([own_near, own_far], 1, own_state[0])
    b_state = first([other_near, other_far], 2, a_state[0])
    cache = lay_cache([across, beyond], b_state[0], chip_cache)
    near_b, far_b = second([other_near, other_far], 2, b_state[0], b_state)
    near_a, far_a = second([own_near, own_far], 1, far_b, a_state)
    own_a, own_b = second([own, other], 0, far_a, own_state)
    (last_a,) = call([own_last], 3, own_a)
    (last_b,) = call([other_last], 4, last_a)

    far_b = move(far_b, far | column)
    last_a = move(last_a, near)
    last_b = move(last_b, far | near | column)
    near_b = move(near_b, near | column)
    near_a = move(near_a, near)
    own_b = move(own_b, column)
    (far_a,) = merge([far_a, last_a], 1)
    far_a = move(far_a, far)
    b_own, b_other = merge([own_b, near_b, far_b, last_b], 2, False)
    b_other = move(b_other, core)
    a_own, a_other = merge([own_a, near_a, far_a], 2, False)
    a_other = move(a_other, core)
    return [a_own, a_other, b_own, b_other]


def attend_general(queries, keys, values, task_slot, task_count, move, servers):
    assert task_slot.shape[0] == 1
    rows = queries.shape[0]
    width = HEADS // KVH * rows
    step = min(4, servers)
    calls = tuple(tuple(range(i, i + step)) for i in range(0, servers, step))
    (own,) = pack_queries(queries, 1, ((0,),))
    masks = active_masks(task_slot, task_count, calls, rows)
    cache = lay_cache(pack_cache(keys, values, 1, ((0,),)), masks)
    held = {0: own}
    bit = servers // 2
    while bit:
        held.update({d ^ bit: move(chunk, bit) for d, chunk in held.items()})
        bit //= 2
    partial = {}
    for which, call in enumerate(calls):
        result = attention(
            [held[d] for d in call], which, cache, masks, width, masks, 1, range(1)
        )
        for j, d in enumerate(call):
            partial[d] = [result[j]]
    bit = 1
    while bit < servers:
        for d in sorted(partial, reverse=True):
            if d & bit:
                messages = partial.pop(d)
                message = messages[0] if len(messages) == 1 else merge(messages, 1)[0]
                partial[d ^ bit].append(move(message, bit))
        bit *= 2
    return merge(partial[0], 1, False)


def on_device(queries, keys, values, out_weight, task_slot, task_count):
    servers = lax.axis_size("tok")
    heads = lax.axis_size("head")
    rows = queries.shape[0]
    group = task_slot.shape[0]
    move = functools.partial(swap, servers=servers)
    if group == 4 and servers == 16:
        attended = attend_grouped(queries, keys, values, task_slot, task_count, move)
    else:
        attended = attend_general(queries, keys, values, task_slot, task_count, move, servers)
    left = gather(attended, rows)

    columns = out_weight.shape[1] // heads
    if heads == 2:
        return exchange_halves(left, out_weight, columns)
    share = project(left, out_weight, None, 0, out_weight.shape[1], jnp.bfloat16)
    return lax.psum_scatter(share, "head", scatter_dimension=1, tiled=True)


def exchange_halves(left, out_weight, columns):
    piece = columns // 2
    arrived = []
    for i in range(2):
        part = project(left, out_weight, 1, i * piece, piece, jnp.bfloat16)
        arrived.append(lax.ppermute(part, "head", [(0, 1), (1, 0)]))
    here = project(left, out_weight, 0, 0, columns, jnp.float32)
    return (here + jnp.concatenate(arrived, axis=1).astype(jnp.float32)).astype(jnp.bfloat16)


def solution(mesh):
    placed = (
        P("tok", "head"),
        P("tok", "head"),
        P("tok", "head"),
        P("head", None),
        P("head", None, None),
        P("head", None),
    )
    return jax.shard_map(
        on_device, mesh=mesh, in_specs=placed, out_specs=P("tok", "head"), check_vma=False
    )
```

```python
import functools
import math

import jax
import jax.numpy as jnp
from jax import lax
from jax.experimental import pallas as pl
from jax.experimental.pallas import tpu as pltpu
from jax.sharding import PartitionSpec as P


HEADS = 32
KVH = 8
HEAD_SIZE = 128
QBLK = 128

theta_base = 500000.0
neg_fill = -1e30
LOG2E = math.log2(math.e)
STAT_ROWS = 8
SUM_ROWS = 16
PACK_VMEM = 47 << 20


def rotary_tables(rows, first_row):
    half = HEAD_SIZE // 2
    frequency = theta_base ** (-(jnp.arange(half, dtype=jnp.float32) * (2.0 / HEAD_SIZE)))
    places = (first_row + jnp.arange(rows, dtype=jnp.int32)).astype(jnp.float32)
    angles = places[:, None] * frequency[None, :]
    cosine = jnp.cos(angles)
    sine = jnp.sin(angles)
    return (
        jnp.concatenate([cosine, cosine], axis=1),
        jnp.concatenate([-sine, sine], axis=1),
    )


def pack_queries_kernel(order, q_per_kv, group, cos_ref, sin_ref, q_ref, *out_refs):
    own = lax.rem(lax.axis_index("tok"), group)
    rows = q_ref.shape[0]
    cosine = cos_ref[...]
    sine = sin_ref[...]
    for offsets, out_ref in zip(order, out_refs):
        for at, offset in enumerate(offsets):
            head = own ^ offset
            for j in range(q_per_kv):
                start = pl.multiple_of((head * q_per_kv + j) * HEAD_SIZE, HEAD_SIZE)
                x = q_ref[:, pl.ds(start, HEAD_SIZE)].astype(jnp.float32)
                turned = pltpu.roll(x, HEAD_SIZE // 2, 1)
                row = (at * q_per_kv + j) * rows
                out_ref[row : row + rows, :] = (x * cosine + turned * sine).astype(jnp.bfloat16)


def pack_queries(queries, group, order):
    rows = queries.shape[0]
    q_per_kv = HEADS // KVH
    cosine, sine = rotary_tables(rows, lax.axis_index("tok") * rows)
    return pl.pallas_call(
        functools.partial(pack_queries_kernel, order, q_per_kv, group),
        out_shape=[
            jax.ShapeDtypeStruct((len(offsets) * q_per_kv * rows, HEAD_SIZE), jnp.bfloat16)
            for offsets in order
        ],
        name="pack_queries",
        cost_estimate=pl.CostEstimate(
            flops=6 * queries.size, bytes_accessed=4 * queries.size, transcendentals=0
        ),
        compiler_params=pltpu.CompilerParams(vmem_limit_bytes=PACK_VMEM),
    )(cosine, sine, queries)


def pack_cache_kernel(order, group, k_ref, v_ref, *out_refs):
    own = lax.rem(lax.axis_index("tok"), group)
    keys = k_ref.shape[0]
    for offsets, out_ref in zip(order, out_refs):
        for at, offset in enumerate(offsets):
            start = pl.multiple_of((own ^ offset) * HEAD_SIZE, HEAD_SIZE)
            row = 2 * at * keys
            out_ref[row : row + keys, :] = k_ref[:, pl.ds(start, HEAD_SIZE)]
            out_ref[row + keys : row + 2 * keys, :] = v_ref[:, pl.ds(start, HEAD_SIZE)]


def pack_cache(keys, values, group, order):
    return pl.pallas_call(
        functools.partial(pack_cache_kernel, order, group),
        out_shape=[
            jax.ShapeDtypeStruct((len(offsets) * 2 * keys.shape[0], HEAD_SIZE), jnp.bfloat16)
            for offsets in order
        ],
        name="pack_cache",
        cost_estimate=pl.CostEstimate(
            flops=0, bytes_accessed=8 * keys.size, transcendentals=0
        ),
        compiler_params=pltpu.CompilerParams(vmem_limit_bytes=PACK_VMEM),
    )(keys, values)


def mask_kernel(calls, rows, slot_hbm, count_hbm, mask_ref, slot_ref, count_ref, sems):
    server = lax.axis_index("tok")
    group = slot_ref.shape[0]
    own = lax.rem(server, group)
    copies = [
        pltpu.make_async_copy(slot_hbm, slot_ref, sems.at[0]),
        pltpu.make_async_copy(count_hbm, count_ref, sems.at[1]),
    ]
    for copy in copies:
        copy.start()
    for copy in copies:
        copy.wait()
    for call, displacements in enumerate(calls):
        mask = jnp.int32(0)
        for i, displacement in enumerate(displacements):
            block = ((server ^ displacement) * rows) // QBLK
            for k in range(group):
                key_block = server ^ k
                slot = slot_ref[own, block, key_block]
                active = (slot >= 0) & (slot < count_ref[own, key_block])
                mask = mask | (active.astype(jnp.int32) << (i * group + k))
        mask_ref[call] = jnp.full(mask_ref.shape[1:], mask, jnp.int32)


def active_masks(task_slot, task_count, calls, rows):
    hbm = pl.BlockSpec(memory_space=pltpu.HBM)
    return pl.pallas_call(
        functools.partial(mask_kernel, calls, rows),
        out_shape=jax.ShapeDtypeStruct((len(calls), 8, HEAD_SIZE), jnp.int32),
        in_specs=[hbm] * 2,
        scratch_shapes=[
            pltpu.SMEM(task_slot.shape, task_slot.dtype),
            pltpu.SMEM(task_count.shape, task_count.dtype),
            pltpu.SemaphoreType.DMA((2,)),
        ],
        name="masks",
        cost_estimate=pl.CostEstimate(
            flops=0, bytes_accessed=4 * task_slot.size, transcendentals=0
        ),
        compiler_params=pltpu.CompilerParams(vmem_limit_bytes=4 << 20),
    )(task_slot, task_count)


def lay_cache_kernel(laid, *refs):
    *in_refs, _, k_ref, v_ref = refs
    keys = k_ref.shape[1]
    if laid:
        k_ref[:laid] = in_refs[0][...]
        v_ref[:laid] = in_refs[1][...]
        in_refs = in_refs[2:]
    for at, ref in enumerate(in_refs, laid):
        k_ref[at] = ref[:keys, :]
        v_ref[at, :HEAD_SIZE, :] = jnp.transpose(ref[keys:, :].astype(jnp.float32)).astype(
            jnp.bfloat16
        )
        v_ref[at, HEAD_SIZE:, :] = jnp.ones((SUM_ROWS, keys), jnp.bfloat16)


def lay_cache(pieces, after, before=()):
    vmem = pl.BlockSpec(memory_space=pltpu.VMEM)
    laid = before[0].shape[0] if before else 0
    group = laid + len(pieces)
    keys = pieces[0].shape[0] // 2
    return pl.pallas_call(
        functools.partial(lay_cache_kernel, laid),
        out_shape=[
            jax.ShapeDtypeStruct((group, keys, HEAD_SIZE), jnp.bfloat16),
            jax.ShapeDtypeStruct((group, HEAD_SIZE + SUM_ROWS, keys), jnp.bfloat16),
        ],
        in_specs=[vmem] * (len(before) + len(pieces)) + [pl.BlockSpec(memory_space=pl.ANY)],
        name="lay_cache",
        cost_estimate=pl.CostEstimate(
            flops=0, bytes_accessed=8 * group * keys * HEAD_SIZE, transcendentals=0
        ),
        compiler_params=pltpu.CompilerParams(vmem_limit_bytes=8 << 20),
    )(*before, *pieces, after)


def split_stat(stat, width):
    high = stat.astype(jnp.bfloat16).astype(jnp.float32)
    rest = stat - high
    middle = rest.astype(jnp.bfloat16).astype(jnp.float32)
    low = rest - middle
    row = lax.broadcasted_iota(jnp.int32, (STAT_ROWS, width), 0)
    spread = jnp.where(row == 0, high, jnp.where(row == 1, middle, jnp.where(row == 2, low, 0.0)))
    return spread.astype(jnp.bfloat16)


def join_stat(ref):
    stat = ref[HEAD_SIZE : HEAD_SIZE + STAT_ROWS, :].astype(jnp.float32)
    return stat[0:1] + stat[1:2] + stat[2:3]


def attention_kernel(plan, mask_ref, *refs):
    which, offset, widths, slab, group, blocks, resumed, ended = plan
    n_chunks = sum(widths)
    n_in = len(widths)
    q_in_refs = refs[:n_in]
    k_ref, v_ref, _ = refs[n_in : n_in + 3]
    at = n_in + 3
    before_refs = refs[at : at + resumed]
    at += resumed
    n_out = n_chunks if ended else 2
    out_refs = refs[at : at + n_out]
    at += n_out
    if ended:
        m_ref, acc_ref = refs[at : at + 2]
        at += 2
    else:
        m_ref, acc_ref = out_refs
    list_ref, q_ref, *slots = refs[at:]
    width = q_ref.shape[1]
    scale = HEAD_SIZE ** (-0.5) * LOG2E

    mask = mask_ref[which, 0, 0]
    found = jnp.int32(0)
    for i in range(n_chunks):
        for k in blocks:
            entry = i * group + k
            list_ref[found] = entry
            found = found + ((mask >> (offset * group + entry)) & 1)

    at = 0
    for q_in_ref, n in zip(q_in_refs, widths):
        for i in range(n):
            q_ref[at + i] = q_in_ref[i * width : (i + 1) * width, :]
        at += n
    if resumed:
        at = 0
        for m_before, acc_before in zip(before_refs[::2], before_refs[1::2]):
            n = m_before.shape[0]
            m_ref[at : at + n] = m_before[...]
            acc_ref[at : at + n] = acc_before[...]
            at += n
    else:
        m_ref[...] = jnp.full_like(m_ref, neg_fill)
        acc_ref[...] = jnp.zeros_like(acc_ref)

    def pair(i):
        entry = list_ref[i]
        return entry // group, lax.rem(entry, group)

    def score(i, slot, slabs=range(0, width, slab)):
        chunk, k = pair(i)
        s_ref, top_ref, fade_ref = slot
        for c in slabs:
            scores = lax.dot_general(
                k_ref[k],
                q_ref[chunk, c : c + slab, :],
                (((1,), (1,)), ((), ())),
                preferred_element_type=jnp.float32,
            )
            s_ref[:, c : c + slab] = scores
            old = m_ref[chunk, :, c : c + slab]
            new = jnp.maximum(old, jnp.max(scores, axis=0, keepdims=True))
            m_ref[chunk, :, c : c + slab] = new
            top_ref[:, c : c + slab] = new
            fade_ref[:, c : c + slab] = jnp.exp2((old - new) * scale)

    def weigh(i, slot, slabs=range(0, width, slab)):
        chunk, k = pair(i)
        s_ref, top_ref, fade_ref = slot
        for c in slabs:
            p = jnp.exp2((s_ref[:, c : c + slab] - top_ref[0:1, c : c + slab]) * scale)
            product = jnp.dot(
                v_ref[k], p.astype(jnp.bfloat16), preferred_element_type=jnp.float32
            )
            acc_ref[chunk, :, c : c + slab] = (
                acc_ref[chunk, :, c : c + slab] * fade_ref[0:1, c : c + slab] + product
            )

    even, odd = slots[:3], slots[3:]

    @pl.when(found > 0)
    def _():
        score(0, even)

    def step(i, here, there):
        @pl.when(i + 1 < found)
        def _():
            for c in range(0, width, slab):
                score(i + 1, there, (c,))
                weigh(i, here, (c,))

        @pl.when(i + 1 == found)
        def _():
            weigh(i, here)

    def two(j, carry):
        step(2 * j, even, odd)
        step(2 * j + 1, odd, even)
        return carry

    lax.fori_loop(0, (found + 1) // 2, two, 0)

    if not ended:
        return
    for i in range(n_chunks):
        total = acc_ref[i, HEAD_SIZE : HEAD_SIZE + 1, :]
        seen = total > 0.0
        safe = jnp.where(seen, total, 1.0)
        stat = jnp.where(seen, m_ref[i, 0:1, :] * scale + jnp.log2(safe), neg_fill)
        out_refs[i][:HEAD_SIZE, :] = (acc_ref[i, :HEAD_SIZE, :] * (1.0 / safe)).astype(jnp.bfloat16)
        out_refs[i][HEAD_SIZE:, :] = split_stat(stat, width)


def attention(
    chunks, which, cache, masks, width, after, group, blocks, offset=0, before=(), ended=True
):
    k, v = cache
    keys = k.shape[1]
    widths = tuple(chunk.shape[0] // width for chunk in chunks)
    n = sum(widths)
    vmem = pl.BlockSpec(memory_space=pltpu.VMEM)
    state = [(n, 8, width), (n, HEAD_SIZE + SUM_ROWS, width)]
    slot = [
        pltpu.VMEM((keys, width), jnp.float32),
        pltpu.VMEM((8, width), jnp.float32),
        pltpu.VMEM((8, width), jnp.float32),
    ]
    if ended:
        out_shape = [jax.ShapeDtypeStruct((HEAD_SIZE + STAT_ROWS, width), jnp.bfloat16)] * n
        scratch = [pltpu.VMEM(shape, jnp.float32) for shape in state]
    else:
        out_shape = [jax.ShapeDtypeStruct(shape, jnp.float32) for shape in state]
        scratch = []
    pairs = n * len(blocks)
    plan = (which, offset, widths, min(256, width), group, tuple(blocks), len(before), ended)
    return pl.pallas_call(
        functools.partial(attention_kernel, plan),
        out_shape=out_shape,
        in_specs=[vmem] * (len(chunks) + 3)
        + [pl.BlockSpec(memory_space=pl.ANY)]
        + [vmem] * len(before),
        out_specs=[vmem] * len(out_shape),
        scratch_shapes=scratch
        + [
            pltpu.SMEM((pairs + 1,), jnp.int32),
            pltpu.VMEM((n, width, HEAD_SIZE), jnp.bfloat16),
        ]
        + slot
        + slot,
        name="attention",
        cost_estimate=pl.CostEstimate(
            flops=4 * pairs * keys * width * HEAD_SIZE,
            bytes_accessed=4 * n * width * HEAD_SIZE + 4 * len(blocks) * keys * HEAD_SIZE,
            transcendentals=pairs * keys * width,
        ),
        compiler_params=pltpu.CompilerParams(vmem_limit_bytes=20 << 20),
    )(masks, *chunks, k, v, after, *before)


def merge_kernel(n_in, keep_stat, *refs):
    in_refs, out_refs = refs[:n_in], refs[n_in:]
    stats = [join_stat(ref) for ref in in_refs]
    largest = functools.reduce(jnp.maximum, stats)
    weights = [jnp.exp2(stat - largest) for stat in stats]
    total = functools.reduce(jnp.add, weights)
    inverse = 1.0 / total
    value = functools.reduce(
        jnp.add,
        [
            (weight * inverse) * ref[:HEAD_SIZE, :].astype(jnp.float32)
            for weight, ref in zip(weights, in_refs)
        ],
    ).astype(jnp.bfloat16)
    stat = largest + jnp.log2(total)
    part = out_refs[0].shape[1]
    for i, out_ref in enumerate(out_refs):
        span = slice(i * part, (i + 1) * part)
        out_ref[:HEAD_SIZE, :] = value[:, span]
        if keep_stat:
            out_ref[HEAD_SIZE:, :] = split_stat(stat[:, span], part)


def merge(messages, parts, keep_stat=True):
    height, width = messages[0].shape
    height = height if keep_stat else HEAD_SIZE
    size = len(messages) * height * width
    return pl.pallas_call(
        functools.partial(merge_kernel, len(messages), keep_stat),
        out_shape=[jax.ShapeDtypeStruct((height, width // parts), jnp.bfloat16)] * parts,
        name="merge" if keep_stat else "finish",
        cost_estimate=pl.CostEstimate(flops=4 * size, bytes_accessed=4 * size, transcendentals=0),
        compiler_params=pltpu.CompilerParams(vmem_limit_bytes=8 << 20),
    )(*messages)


def gather_kernel(rows, *refs):
    *piece_refs, out_ref = refs
    group = len(piece_refs)
    own = lax.rem(lax.axis_index("tok"), group)
    per = piece_refs[0].shape[1] // rows
    for offset in range(group):
        for j in range(per):
            block = jnp.transpose(
                piece_refs[offset][:, j * rows : (j + 1) * rows].astype(jnp.float32)
            )
            start = pl.multiple_of(((own ^ offset) * per + j) * HEAD_SIZE, HEAD_SIZE)
            out_ref[:, pl.ds(start, HEAD_SIZE)] = block.astype(jnp.bfloat16)


def gather(pieces, rows):
    width = sum(piece.shape[1] for piece in pieces) // rows * HEAD_SIZE
    return pl.pallas_call(
        functools.partial(gather_kernel, rows),
        out_shape=jax.ShapeDtypeStruct((rows, width), jnp.bfloat16),
        name="gather",
        cost_estimate=pl.CostEstimate(
            flops=0, bytes_accessed=4 * rows * width, transcendentals=0
        ),
        compiler_params=pltpu.CompilerParams(vmem_limit_bytes=4 << 20),
    )(*pieces)


def project_kernel(half, start, left_ref, w_ref, out_ref):
    columns = out_ref.shape[1]
    if half is not None:
        start = (lax.axis_index("head") ^ half) * (w_ref.shape[1] // 2) + start
    start = pl.multiple_of(start, HEAD_SIZE)
    out_ref[...] = jnp.dot(
        left_ref[...], w_ref[:, pl.ds(start, columns)], preferred_element_type=jnp.float32
    ).astype(out_ref.dtype)


def project(left, out_weight, half, start, columns, kind):
    rows, depth = left.shape
    return pl.pallas_call(
        functools.partial(project_kernel, half, start),
        out_shape=jax.ShapeDtypeStruct((rows, columns), kind),
        in_specs=[pl.BlockSpec(memory_space=pltpu.VMEM)] * 2,
        out_specs=pl.BlockSpec(memory_space=pltpu.VMEM),
        name="project",
        cost_estimate=pl.CostEstimate(
            flops=2 * rows * depth * columns,
            bytes_accessed=2 * depth * columns,
            transcendentals=0,
        ),
        compiler_params=pltpu.CompilerParams(vmem_limit_bytes=24 << 20),
    )(left, out_weight)


def swap(x, bits, servers):
    return lax.ppermute(x, "tok", [(i, i ^ bits) for i in range(servers)])


def attend_grouped(queries, keys, values, task_slot, task_count, move):
    core, column, near, far = 1, 2, 4, 8
    rows = queries.shape[0]
    q_per_kv = HEADS // KVH
    part = q_per_kv * rows
    width = 2 * part

    keep, give = pack_queries(queries, 4, ((0, 2), (1, 3)))
    pieces = pack_cache(keys, values, 4, ((0,), (core,), (column,), (column | core,)))
    got = move(give, core)
    own = jnp.concatenate([keep[:part], got[:part]], axis=0)
    other = move(jnp.concatenate([keep[part:], got[part:]], axis=0), column)
    across = move(pieces[2], column)
    beyond = move(pieces[3], column | core)
    own_far = move(own, far)
    beside = move(pieces[1], core)
    other_far = move(other, far)
    own_near = move(own, near)
    other_near = move(other, near)
    own_last = move(own_far, near)
    other_last = move(other_far, near)

    calls = (
        (0, column, near, far, near | column, far | column),
        (far | near,),
        (far | near | column,),
    )
    masks = active_masks(task_slot, task_count, calls, rows)
    chip_cache = lay_cache([pieces[0], beside], masks)

    def first(chunks, offset, after):
        return attention(
            chunks, 0, chip_cache, masks, width, after, 4, (0, core), offset, ended=False
        )

    def call(chunks, which, after):
        return attention(chunks, which, cache, masks, width, after, 4, range(4))

    chunks = [own, other, own_near, own_far, other_near, other_far]
    own_state = first(chunks[:2], 0, masks)
    a_state = first(chunks[2:4], 2, own_state[0])
    b_state = first(chunks[4:], 4, a_state[0])
    cache = lay_cache([across, beyond], b_state[0], chip_cache)
    own_a, own_b, near_a, far_a, near_b, far_b = attention(
        chunks,
        0,
        cache,
        masks,
        width,
        b_state[0],
        4,
        (column, column | core),
        before=(*own_state, *a_state, *b_state),
    )
    (last_a,) = call([own_last], 1, far_b)
    (last_b,) = call([other_last], 2, last_a)

    far_b = move(far_b, far | column)
    last_a = move(last_a, near)
    last_b = move(last_b, far | near | column)
    near_b = move(near_b, near | column)
    near_a = move(near_a, near)
    own_b = move(own_b, column)
    (far_a,) = merge([far_a, last_a], 1)
    far_a = move(far_a, far)
    b_own, b_other = merge([own_b, near_b, far_b, last_b], 2, False)
    b_other = move(b_other, core)
    a_own, a_other = merge([own_a, near_a, far_a], 2, False)
    a_other = move(a_other, core)
    return [a_own, a_other, b_own, b_other]


def attend_general(queries, keys, values, task_slot, task_count, move, servers):
    assert task_slot.shape[0] == 1
    rows = queries.shape[0]
    width = HEADS // KVH * rows
    step = min(4, servers)
    calls = tuple(tuple(range(i, i + step)) for i in range(0, servers, step))
    (own,) = pack_queries(queries, 1, ((0,),))
    masks = active_masks(task_slot, task_count, calls, rows)
    cache = lay_cache(pack_cache(keys, values, 1, ((0,),)), masks)
    held = {0: own}
    bit = servers // 2
    while bit:
        held.update({d ^ bit: move(chunk, bit) for d, chunk in held.items()})
        bit //= 2
    partial = {}
    for which, call in enumerate(calls):
        result = attention(
            [held[d] for d in call], which, cache, masks, width, masks, 1, range(1)
        )
        for j, d in enumerate(call):
            partial[d] = [result[j]]
    bit = 1
    while bit < servers:
        for d in sorted(partial, reverse=True):
            if d & bit:
                messages = partial.pop(d)
                message = messages[0] if len(messages) == 1 else merge(messages, 1)[0]
                partial[d ^ bit].append(move(message, bit))
        bit *= 2
    return merge(partial[0], 1, False)


def on_device(queries, keys, values, out_weight, task_slot, task_count):
    servers = lax.axis_size("tok")
    heads = lax.axis_size("head")
    rows = queries.shape[0]
    group = task_slot.shape[0]
    move = functools.partial(swap, servers=servers)
    if group == 4 and servers == 16:
        attended = attend_grouped(queries, keys, values, task_slot, task_count, move)
    else:
        attended = attend_general(queries, keys, values, task_slot, task_count, move, servers)
    left = gather(attended, rows)

    columns = out_weight.shape[1] // heads
    if heads == 2:
        return exchange_halves(left, out_weight, columns)
    share = project(left, out_weight, None, 0, out_weight.shape[1], jnp.bfloat16)
    return lax.psum_scatter(share, "head", scatter_dimension=1, tiled=True)


def exchange_halves(left, out_weight, columns):
    piece = columns // 2
    arrived = []
    for i in range(2):
        part = project(left, out_weight, 1, i * piece, piece, jnp.bfloat16)
        arrived.append(lax.ppermute(part, "head", [(0, 1), (1, 0)]))
    here = project(left, out_weight, 0, 0, columns, jnp.float32)
    return (here + jnp.concatenate(arrived, axis=1).astype(jnp.float32)).astype(jnp.bfloat16)


def solution(mesh):
    placed = (
        P("tok", "head"),
        P("tok", "head"),
        P("tok", "head"),
        P("head", None),
        P("head", None, None),
        P("head", None),
    )
    return jax.shard_map(
        on_device, mesh=mesh, in_specs=placed, out_specs=P("tok", "head"), check_vma=False
    )
```

```python
import functools
import math

import jax
import jax.numpy as jnp
from jax import lax
from jax.experimental import pallas as pl
from jax.experimental.pallas import tpu as pltpu
from jax.sharding import PartitionSpec as P


HEADS = 32
KVH = 8
HEAD_SIZE = 128
QBLK = 128

theta_base = 500000.0
neg_fill = -1e30
LOG2E = math.log2(math.e)
STAT_ROWS = 8
SUM_ROWS = 16
PACK_VMEM = 47 << 20


def rotary_tables(rows, first_row):
    half = HEAD_SIZE // 2
    frequency = theta_base ** (-(jnp.arange(half, dtype=jnp.float32) * (2.0 / HEAD_SIZE)))
    places = (first_row + jnp.arange(rows, dtype=jnp.int32)).astype(jnp.float32)
    angles = places[:, None] * frequency[None, :]
    cosine = jnp.cos(angles)
    sine = jnp.sin(angles)
    return (
        jnp.concatenate([cosine, cosine], axis=1),
        jnp.concatenate([-sine, sine], axis=1),
    )


def pack_queries_kernel(order, q_per_kv, group, cos_ref, sin_ref, q_ref, *out_refs):
    own = lax.rem(lax.axis_index("tok"), group)
    rows = q_ref.shape[0]
    cosine = cos_ref[...]
    sine = sin_ref[...]
    for offsets, out_ref in zip(order, out_refs):
        for at, offset in enumerate(offsets):
            head = own ^ offset
            for j in range(q_per_kv):
                start = pl.multiple_of((head * q_per_kv + j) * HEAD_SIZE, HEAD_SIZE)
                x = q_ref[:, pl.ds(start, HEAD_SIZE)].astype(jnp.float32)
                turned = pltpu.roll(x, HEAD_SIZE // 2, 1)
                row = (at * q_per_kv + j) * rows
                out_ref[row : row + rows, :] = (x * cosine + turned * sine).astype(jnp.bfloat16)


def pack_queries(queries, group, order):
    rows = queries.shape[0]
    q_per_kv = HEADS // KVH
    cosine, sine = rotary_tables(rows, lax.axis_index("tok") * rows)
    return pl.pallas_call(
        functools.partial(pack_queries_kernel, order, q_per_kv, group),
        out_shape=[
            jax.ShapeDtypeStruct((len(offsets) * q_per_kv * rows, HEAD_SIZE), jnp.bfloat16)
            for offsets in order
        ],
        name="pack_queries",
        cost_estimate=pl.CostEstimate(
            flops=6 * queries.size, bytes_accessed=4 * queries.size, transcendentals=0
        ),
        compiler_params=pltpu.CompilerParams(vmem_limit_bytes=PACK_VMEM),
    )(cosine, sine, queries)


def pack_cache_kernel(order, group, k_ref, v_ref, *out_refs):
    own = lax.rem(lax.axis_index("tok"), group)
    keys = k_ref.shape[0]
    for offsets, out_ref in zip(order, out_refs):
        for at, offset in enumerate(offsets):
            start = pl.multiple_of((own ^ offset) * HEAD_SIZE, HEAD_SIZE)
            row = 2 * at * keys
            out_ref[row : row + keys, :] = k_ref[:, pl.ds(start, HEAD_SIZE)]
            out_ref[row + keys : row + 2 * keys, :] = v_ref[:, pl.ds(start, HEAD_SIZE)]


def pack_cache(keys, values, group, order):
    return pl.pallas_call(
        functools.partial(pack_cache_kernel, order, group),
        out_shape=[
            jax.ShapeDtypeStruct((len(offsets) * 2 * keys.shape[0], HEAD_SIZE), jnp.bfloat16)
            for offsets in order
        ],
        name="pack_cache",
        cost_estimate=pl.CostEstimate(
            flops=0, bytes_accessed=8 * keys.size, transcendentals=0
        ),
        compiler_params=pltpu.CompilerParams(vmem_limit_bytes=PACK_VMEM),
    )(keys, values)


def mask_kernel(calls, rows, slot_hbm, count_hbm, mask_ref, slot_ref, count_ref, sems):
    server = lax.axis_index("tok")
    group = slot_ref.shape[0]
    own = lax.rem(server, group)
    copies = [
        pltpu.make_async_copy(slot_hbm, slot_ref, sems.at[0]),
        pltpu.make_async_copy(count_hbm, count_ref, sems.at[1]),
    ]
    for copy in copies:
        copy.start()
    for copy in copies:
        copy.wait()
    for call, displacements in enumerate(calls):
        mask = jnp.int32(0)
        for i, displacement in enumerate(displacements):
            block = ((server ^ displacement) * rows) // QBLK
            for k in range(group):
                key_block = server ^ k
                slot = slot_ref[own, block, key_block]
                active = (slot >= 0) & (slot < count_ref[own, key_block])
                mask = mask | (active.astype(jnp.int32) << (i * group + k))
        mask_ref[call] = jnp.full(mask_ref.shape[1:], mask, jnp.int32)


def active_masks(task_slot, task_count, calls, rows):
    hbm = pl.BlockSpec(memory_space=pltpu.HBM)
    return pl.pallas_call(
        functools.partial(mask_kernel, calls, rows),
        out_shape=jax.ShapeDtypeStruct((len(calls), 8, HEAD_SIZE), jnp.int32),
        in_specs=[hbm] * 2,
        scratch_shapes=[
            pltpu.SMEM(task_slot.shape, task_slot.dtype),
            pltpu.SMEM(task_count.shape, task_count.dtype),
            pltpu.SemaphoreType.DMA((2,)),
        ],
        name="masks",
        cost_estimate=pl.CostEstimate(
            flops=0, bytes_accessed=4 * task_slot.size, transcendentals=0
        ),
        compiler_params=pltpu.CompilerParams(vmem_limit_bytes=4 << 20),
    )(task_slot, task_count)


def lay_cache_kernel(laid, *refs):
    *in_refs, _, k_ref, v_ref = refs
    keys = k_ref.shape[1]
    if laid:
        k_ref[:laid] = in_refs[0][...]
        v_ref[:laid] = in_refs[1][...]
        in_refs = in_refs[2:]
    for at, ref in enumerate(in_refs, laid):
        k_ref[at] = ref[:keys, :]
        v_ref[at, :HEAD_SIZE, :] = jnp.transpose(ref[keys:, :].astype(jnp.float32)).astype(
            jnp.bfloat16
        )
        v_ref[at, HEAD_SIZE:, :] = jnp.ones((SUM_ROWS, keys), jnp.bfloat16)


def lay_cache(pieces, after, before=()):
    vmem = pl.BlockSpec(memory_space=pltpu.VMEM)
    laid = before[0].shape[0] if before else 0
    group = laid + len(pieces)
    keys = pieces[0].shape[0] // 2
    return pl.pallas_call(
        functools.partial(lay_cache_kernel, laid),
        out_shape=[
            jax.ShapeDtypeStruct((group, keys, HEAD_SIZE), jnp.bfloat16),
            jax.ShapeDtypeStruct((group, HEAD_SIZE + SUM_ROWS, keys), jnp.bfloat16),
        ],
        in_specs=[vmem] * (len(before) + len(pieces)) + [pl.BlockSpec(memory_space=pl.ANY)],
        name="lay_cache",
        cost_estimate=pl.CostEstimate(
            flops=0, bytes_accessed=8 * group * keys * HEAD_SIZE, transcendentals=0
        ),
        compiler_params=pltpu.CompilerParams(vmem_limit_bytes=8 << 20),
    )(*before, *pieces, after)


def split_stat(stat, width):
    high = stat.astype(jnp.bfloat16).astype(jnp.float32)
    rest = stat - high
    middle = rest.astype(jnp.bfloat16).astype(jnp.float32)
    low = rest - middle
    row = lax.broadcasted_iota(jnp.int32, (STAT_ROWS, width), 0)
    spread = jnp.where(row == 0, high, jnp.where(row == 1, middle, jnp.where(row == 2, low, 0.0)))
    return spread.astype(jnp.bfloat16)


def join_stat(ref):
    stat = ref[HEAD_SIZE : HEAD_SIZE + STAT_ROWS, :].astype(jnp.float32)
    return stat[0:1] + stat[1:2] + stat[2:3]


def attention_kernel(plan, mask_ref, *refs):
    which, offset, widths, slab, group, blocks, resumed, ended = plan
    n_chunks = sum(widths)
    n_in = len(widths)
    q_in_refs = refs[:n_in]
    k_ref, v_ref, _ = refs[n_in : n_in + 3]
    at = n_in + 3
    before_refs = refs[at : at + resumed]
    at += resumed
    n_out = n_chunks if ended else 2
    out_refs = refs[at : at + n_out]
    at += n_out
    if ended:
        m_ref, acc_ref = refs[at : at + 2]
        at += 2
    else:
        m_ref, acc_ref = out_refs
    list_ref, q_ref, *slots = refs[at:]
    width = q_ref.shape[1]
    scale = HEAD_SIZE ** (-0.5) * LOG2E

    mask = mask_ref[which, 0, 0]
    found = jnp.int32(0)
    for i in range(n_chunks):
        for k in blocks:
            entry = i * group + k
            list_ref[found] = entry
            found = found + ((mask >> (offset * group + entry)) & 1)

    at = 0
    for q_in_ref, n in zip(q_in_refs, widths):
        for i in range(n):
            q_ref[at + i] = q_in_ref[i * width : (i + 1) * width, :]
        at += n
    if resumed:
        at = 0
        for m_before, acc_before in zip(before_refs[::2], before_refs[1::2]):
            n = m_before.shape[0]
            m_ref[at : at + n] = m_before[...]
            acc_ref[at : at + n] = acc_before[...]
            at += n
    else:
        m_ref[...] = jnp.full_like(m_ref, neg_fill)
        acc_ref[...] = jnp.zeros_like(acc_ref)

    def pair(i):
        entry = list_ref[i]
        return entry // group, lax.rem(entry, group)

    def score(i, slot, slabs=range(0, width, slab)):
        chunk, k = pair(i)
        s_ref, top_ref, fade_ref = slot
        for c in slabs:
            scores = lax.dot_general(
                k_ref[k],
                q_ref[chunk, c : c + slab, :],
                (((1,), (1,)), ((), ())),
                preferred_element_type=jnp.float32,
            )
            s_ref[:, c : c + slab] = scores
            old = m_ref[chunk, :, c : c + slab]
            new = jnp.maximum(old, jnp.max(scores, axis=0, keepdims=True))
            m_ref[chunk, :, c : c + slab] = new
            top_ref[:, c : c + slab] = new
            fade_ref[:, c : c + slab] = jnp.exp2((old - new) * scale)

    def weigh(i, slot, slabs=range(0, width, slab)):
        chunk, k = pair(i)
        s_ref, top_ref, fade_ref = slot
        for c in slabs:
            p = jnp.exp2((s_ref[:, c : c + slab] - top_ref[0:1, c : c + slab]) * scale)
            product = jnp.dot(
                v_ref[k], p.astype(jnp.bfloat16), preferred_element_type=jnp.float32
            )
            acc_ref[chunk, :, c : c + slab] = (
                acc_ref[chunk, :, c : c + slab] * fade_ref[0:1, c : c + slab] + product
            )

    even, odd = slots[:3], slots[3:]

    @pl.when(found > 0)
    def _():
        score(0, even)

    def step(i, here, there):
        @pl.when(i + 1 < found)
        def _():
            for c in range(0, width, slab):
                score(i + 1, there, (c,))
                weigh(i, here, (c,))

        @pl.when(i + 1 == found)
        def _():
            weigh(i, here)

    def two(j, carry):
        step(2 * j, even, odd)
        step(2 * j + 1, odd, even)
        return carry

    lax.fori_loop(0, (found + 1) // 2, two, 0)

    if not ended:
        return
    for i in range(n_chunks):
        total = acc_ref[i, HEAD_SIZE : HEAD_SIZE + 1, :]
        seen = total > 0.0
        safe = jnp.where(seen, total, 1.0)
        stat = jnp.where(seen, m_ref[i, 0:1, :] * scale + jnp.log2(safe), neg_fill)
        out_refs[i][:HEAD_SIZE, :] = (acc_ref[i, :HEAD_SIZE, :] * (1.0 / safe)).astype(jnp.bfloat16)
        out_refs[i][HEAD_SIZE:, :] = split_stat(stat, width)


def attention(
    chunks, which, cache, masks, width, after, group, blocks, offset=0, before=(), ended=True
):
    k, v = cache
    keys = k.shape[1]
    widths = tuple(chunk.shape[0] // width for chunk in chunks)
    n = sum(widths)
    vmem = pl.BlockSpec(memory_space=pltpu.VMEM)
    state = [(n, 8, width), (n, HEAD_SIZE + SUM_ROWS, width)]
    slot = [
        pltpu.VMEM((keys, width), jnp.float32),
        pltpu.VMEM((8, width), jnp.float32),
        pltpu.VMEM((8, width), jnp.float32),
    ]
    if ended:
        out_shape = [jax.ShapeDtypeStruct((HEAD_SIZE + STAT_ROWS, width), jnp.bfloat16)] * n
        scratch = [pltpu.VMEM(shape, jnp.float32) for shape in state]
    else:
        out_shape = [jax.ShapeDtypeStruct(shape, jnp.float32) for shape in state]
        scratch = []
    pairs = n * len(blocks)
    plan = (which, offset, widths, min(256, width), group, tuple(blocks), len(before), ended)
    return pl.pallas_call(
        functools.partial(attention_kernel, plan),
        out_shape=out_shape,
        in_specs=[vmem] * (len(chunks) + 3)
        + [pl.BlockSpec(memory_space=pl.ANY)]
        + [vmem] * len(before),
        out_specs=[vmem] * len(out_shape),
        scratch_shapes=scratch
        + [
            pltpu.SMEM((pairs + 1,), jnp.int32),
            pltpu.VMEM((n, width, HEAD_SIZE), jnp.bfloat16),
        ]
        + slot
        + slot,
        name="attention",
        cost_estimate=pl.CostEstimate(
            flops=4 * pairs * keys * width * HEAD_SIZE,
            bytes_accessed=4 * n * width * HEAD_SIZE + 4 * len(blocks) * keys * HEAD_SIZE,
            transcendentals=pairs * keys * width,
        ),
        compiler_params=pltpu.CompilerParams(vmem_limit_bytes=20 << 20),
    )(masks, *chunks, k, v, after, *before)


def merge_kernel(n_in, keep_stat, *refs):
    in_refs, out_refs = refs[:n_in], refs[n_in + 1 :]
    stats = [join_stat(ref) for ref in in_refs]
    largest = functools.reduce(jnp.maximum, stats)
    weights = [jnp.exp2(stat - largest) for stat in stats]
    total = functools.reduce(jnp.add, weights)
    inverse = 1.0 / total
    value = functools.reduce(
        jnp.add,
        [
            (weight * inverse) * ref[:HEAD_SIZE, :].astype(jnp.float32)
            for weight, ref in zip(weights, in_refs)
        ],
    ).astype(jnp.bfloat16)
    stat = largest + jnp.log2(total)
    part = out_refs[0].shape[1]
    for i, out_ref in enumerate(out_refs):
        span = slice(i * part, (i + 1) * part)
        out_ref[:HEAD_SIZE, :] = value[:, span]
        if keep_stat:
            out_ref[HEAD_SIZE:, :] = split_stat(stat[:, span], part)


def merge(messages, parts, keep_stat=True, after=None):
    vmem = pl.BlockSpec(memory_space=pltpu.VMEM)
    after = messages[0] if after is None else after
    height, width = messages[0].shape
    height = height if keep_stat else HEAD_SIZE
    size = len(messages) * height * width
    return pl.pallas_call(
        functools.partial(merge_kernel, len(messages), keep_stat),
        out_shape=[jax.ShapeDtypeStruct((height, width // parts), jnp.bfloat16)] * parts,
        in_specs=[vmem] * len(messages) + [pl.BlockSpec(memory_space=pl.ANY)],
        name="merge" if keep_stat else "finish",
        cost_estimate=pl.CostEstimate(flops=4 * size, bytes_accessed=4 * size, transcendentals=0),
        compiler_params=pltpu.CompilerParams(vmem_limit_bytes=8 << 20),
    )(*messages, after)


def gather_kernel(rows, *refs):
    *piece_refs, out_ref = refs
    core = lax.rem(lax.axis_index("tok"), len(piece_refs))
    per = piece_refs[0].shape[1] // rows
    for offset, piece_ref in enumerate(piece_refs):
        for j in range(per):
            block = jnp.transpose(piece_ref[:, j * rows : (j + 1) * rows].astype(jnp.float32))
            start = pl.multiple_of(((core ^ offset) * per + j) * HEAD_SIZE, HEAD_SIZE)
            out_ref[:, pl.ds(start, HEAD_SIZE)] = block.astype(jnp.bfloat16)


def gather(pieces, rows):
    width = sum(piece.shape[1] for piece in pieces) // rows * HEAD_SIZE
    return pl.pallas_call(
        functools.partial(gather_kernel, rows),
        out_shape=jax.ShapeDtypeStruct((rows, width), jnp.bfloat16),
        name="gather",
        cost_estimate=pl.CostEstimate(
            flops=0, bytes_accessed=4 * rows * width, transcendentals=0
        ),
        compiler_params=pltpu.CompilerParams(vmem_limit_bytes=4 << 20),
    )(*pieces)


def project_kernel(plan, left_ref, w_ref, *refs):
    half, start, away = plan
    out_ref = refs[-1]
    columns = out_ref.shape[1]
    depth = left_ref.shape[1]
    base_start = start
    if half is not None:
        start = (lax.axis_index("head") ^ half) * (w_ref.shape[1] // 2) + start
    start = pl.multiple_of(start, HEAD_SIZE)
    row = 0
    if depth < w_ref.shape[0]:
        group = w_ref.shape[0] // depth * 2
        row = pl.multiple_of((lax.rem(lax.axis_index("tok"), group) // 2 ^ away) * depth, depth)
    total = jnp.dot(
        left_ref[...],
        w_ref[pl.ds(row, depth), pl.ds(start, columns)],
        preferred_element_type=jnp.float32,
    )
    if len(refs) == 2:
        total = total + refs[0][:, base_start : base_start + columns]
    out_ref[...] = total.astype(out_ref.dtype)


def project(left, out_weight, half, start, columns, kind, away=0, base=None):
    rows, depth = left.shape
    operands = (left, out_weight) if base is None else (left, out_weight, base)
    return pl.pallas_call(
        functools.partial(project_kernel, (half, start, away)),
        out_shape=jax.ShapeDtypeStruct((rows, columns), kind),
        in_specs=[pl.BlockSpec(memory_space=pltpu.VMEM)] * len(operands),
        out_specs=pl.BlockSpec(memory_space=pltpu.VMEM),
        name="project",
        cost_estimate=pl.CostEstimate(
            flops=2 * rows * depth * columns,
            bytes_accessed=2 * depth * columns,
            transcendentals=0,
        ),
        compiler_params=pltpu.CompilerParams(vmem_limit_bytes=24 << 20),
    )(*operands)


def swap(x, bits, servers):
    return lax.ppermute(x, "tok", [(i, i ^ bits) for i in range(servers)])


def attend_grouped(queries, keys, values, out_weight, task_slot, task_count, move):
    core, column, near, far = 1, 2, 4, 8
    rows = queries.shape[0]
    q_per_kv = HEADS // KVH
    part = q_per_kv * rows
    width = 2 * part

    keep, give = pack_queries(queries, 4, ((0, 2), (1, 3)))
    pieces = pack_cache(keys, values, 4, ((0,), (core,), (column,), (column | core,)))
    got = move(give, core)
    own = jnp.concatenate([keep[:part], got[:part]], axis=0)
    other = move(jnp.concatenate([keep[part:], got[part:]], axis=0), column)
    across = move(pieces[2], column)
    beyond = move(pieces[3], column | core)
    own_far = move(own, far)
    beside = move(pieces[1], core)
    other_far = move(other, far)
    own_near = move(own, near)
    other_near = move(other, near)
    own_last = move(own_far, near)
    other_last = move(other_far, near)

    calls = (
        (0, column, near, far, near | column, far | column),
        (far | near,),
        (far | near | column,),
    )
    masks = active_masks(task_slot, task_count, calls, rows)
    chip_cache = lay_cache([pieces[0], beside], masks)

    def first(chunks, offset, after):
        return attention(
            chunks, 0, chip_cache, masks, width, after, 4, (0, core), offset, ended=False
        )

    def call(chunks, which, after):
        return attention(chunks, which, cache, masks, width, after, 4, range(4))

    chunks = [own, other, own_near, own_far, other_near, other_far]
    own_state = first(chunks[:2], 0, masks)
    a_state = first(chunks[2:4], 2, own_state[0])
    b_state = first(chunks[4:], 4, a_state[0])
    cache = lay_cache([across, beyond], b_state[0], chip_cache)
    own_a, own_b, near_a, far_a, near_b, far_b = attention(
        chunks,
        0,
        cache,
        masks,
        width,
        b_state[0],
        4,
        (column, column | core),
        before=(*own_state, *a_state, *b_state),
    )
    (last_a,) = call([own_last], 1, far_b)
    (last_b,) = call([other_last], 2, last_a)

    far_b = move(far_b, far | column)
    last_a = move(last_a, near)
    last_b = move(last_b, far | near | column)
    near_b = move(near_b, near | column)
    near_a = move(near_a, near)
    own_b = move(own_b, column)
    (far_a,) = merge([far_a, last_a], 1)
    far_a = move(far_a, far)
    b_own, b_other = merge([own_b, near_b, far_b, last_b], 2, False)
    b_other = move(b_other, core)
    left_b = gather([b_own, b_other], rows)
    columns = out_weight.shape[1] // 2
    base = project(left_b, out_weight, 1, 0, columns, jnp.float32, away=1)
    a_own, a_other = merge([own_a, near_a, far_a], 2, False, after=base)
    a_other = move(a_other, core)
    left_a = gather([a_own, a_other], rows)

    piece = columns // 2
    arrived = []
    for i in range(2):
        part = project(left_a, out_weight, 1, i * piece, piece, jnp.bfloat16, base=base)
        arrived.append(lax.ppermute(part, "head", [(0, 1), (1, 0)]))
    here = project(left_b, out_weight, 0, 0, columns, jnp.float32, away=1)
    here = project(left_a, out_weight, 0, 0, columns, jnp.float32, base=here)
    return (here + jnp.concatenate(arrived, axis=1).astype(jnp.float32)).astype(jnp.bfloat16)


def attend_general(queries, keys, values, task_slot, task_count, move, servers):
    assert task_slot.shape[0] == 1
    rows = queries.shape[0]
    width = HEADS // KVH * rows
    step = min(4, servers)
    calls = tuple(tuple(range(i, i + step)) for i in range(0, servers, step))
    (own,) = pack_queries(queries, 1, ((0,),))
    masks = active_masks(task_slot, task_count, calls, rows)
    cache = lay_cache(pack_cache(keys, values, 1, ((0,),)), masks)
    held = {0: own}
    bit = servers // 2
    while bit:
        held.update({d ^ bit: move(chunk, bit) for d, chunk in held.items()})
        bit //= 2
    partial = {}
    for which, call in enumerate(calls):
        result = attention(
            [held[d] for d in call], which, cache, masks, width, masks, 1, range(1)
        )
        for j, d in enumerate(call):
            partial[d] = [result[j]]
    bit = 1
    while bit < servers:
        for d in sorted(partial, reverse=True):
            if d & bit:
                messages = partial.pop(d)
                message = messages[0] if len(messages) == 1 else merge(messages, 1)[0]
                partial[d ^ bit].append(move(message, bit))
        bit *= 2
    return merge(partial[0], 1, False)


def on_device(queries, keys, values, out_weight, task_slot, task_count):
    servers = lax.axis_size("tok")
    heads = lax.axis_size("head")
    rows = queries.shape[0]
    group = task_slot.shape[0]
    move = functools.partial(swap, servers=servers)
    if group == 4 and servers == 16 and heads == 2:
        return attend_grouped(
            queries, keys, values, out_weight, task_slot, task_count, move
        )
    attended = attend_general(queries, keys, values, task_slot, task_count, move, servers)
    left = gather(attended, rows)
    share = project(left, out_weight, None, 0, out_weight.shape[1], jnp.bfloat16)
    return lax.psum_scatter(share, "head", scatter_dimension=1, tiled=True)


def solution(mesh):
    placed = (
        P("tok", "head"),
        P("tok", "head"),
        P("tok", "head"),
        P("head", None),
        P("head", None, None),
        P("head", None),
    )
    return jax.shard_map(
        on_device, mesh=mesh, in_specs=placed, out_specs=P("tok", "head"), check_vma=False
    )
```

```python
import functools
import math

import jax
import jax.numpy as jnp
from jax import lax
from jax.experimental import pallas as pl
from jax.experimental.pallas import tpu as pltpu
from jax.sharding import PartitionSpec as P


HEADS = 32
KVH = 8
HEAD_SIZE = 128
QBLK = 128

theta_base = 500000.0
neg_fill = -1e30
LOG2E = math.log2(math.e)
STAT_ROWS = 8
SUM_ROWS = 16
PACK_VMEM = 47 << 20


def rotary_tables(rows, first_row):
    half = HEAD_SIZE // 2
    frequency = theta_base ** (-(jnp.arange(half, dtype=jnp.float32) * (2.0 / HEAD_SIZE)))
    places = (first_row + jnp.arange(rows, dtype=jnp.int32)).astype(jnp.float32)
    angles = places[:, None] * frequency[None, :]
    cosine = jnp.cos(angles)
    sine = jnp.sin(angles)
    return (
        jnp.concatenate([cosine, cosine], axis=1),
        jnp.concatenate([-sine, sine], axis=1),
    )


def pack_queries_kernel(order, q_per_kv, group, cos_ref, sin_ref, q_ref, *out_refs):
    own = lax.rem(lax.axis_index("tok"), group)
    rows = q_ref.shape[0]
    cosine = cos_ref[...]
    sine = sin_ref[...]
    for offsets, out_ref in zip(order, out_refs):
        for at, offset in enumerate(offsets):
            head = own ^ offset
            for j in range(q_per_kv):
                start = pl.multiple_of((head * q_per_kv + j) * HEAD_SIZE, HEAD_SIZE)
                x = q_ref[:, pl.ds(start, HEAD_SIZE)].astype(jnp.float32)
                turned = pltpu.roll(x, HEAD_SIZE // 2, 1)
                row = (at * q_per_kv + j) * rows
                out_ref[row : row + rows, :] = (x * cosine + turned * sine).astype(jnp.bfloat16)


def pack_queries(queries, group, order):
    rows = queries.shape[0]
    q_per_kv = HEADS // KVH
    cosine, sine = rotary_tables(rows, lax.axis_index("tok") * rows)
    return pl.pallas_call(
        functools.partial(pack_queries_kernel, order, q_per_kv, group),
        out_shape=[
            jax.ShapeDtypeStruct((len(offsets) * q_per_kv * rows, HEAD_SIZE), jnp.bfloat16)
            for offsets in order
        ],
        name="pack_queries",
        cost_estimate=pl.CostEstimate(
            flops=6 * queries.size, bytes_accessed=4 * queries.size, transcendentals=0
        ),
        compiler_params=pltpu.CompilerParams(vmem_limit_bytes=PACK_VMEM),
    )(cosine, sine, queries)


def pack_cache_kernel(order, group, k_ref, v_ref, *out_refs):
    own = lax.rem(lax.axis_index("tok"), group)
    keys = k_ref.shape[0]
    for offsets, out_ref in zip(order, out_refs):
        for at, offset in enumerate(offsets):
            start = pl.multiple_of((own ^ offset) * HEAD_SIZE, HEAD_SIZE)
            row = 2 * at * keys
            out_ref[row : row + keys, :] = k_ref[:, pl.ds(start, HEAD_SIZE)]
            out_ref[row + keys : row + 2 * keys, :] = v_ref[:, pl.ds(start, HEAD_SIZE)]


def pack_cache(keys, values, group, order):
    return pl.pallas_call(
        functools.partial(pack_cache_kernel, order, group),
        out_shape=[
            jax.ShapeDtypeStruct((len(offsets) * 2 * keys.shape[0], HEAD_SIZE), jnp.bfloat16)
            for offsets in order
        ],
        name="pack_cache",
        cost_estimate=pl.CostEstimate(
            flops=0, bytes_accessed=8 * keys.size, transcendentals=0
        ),
        compiler_params=pltpu.CompilerParams(vmem_limit_bytes=PACK_VMEM),
    )(keys, values)


def mask_kernel(calls, rows, slot_hbm, count_hbm, mask_ref, slot_ref, count_ref, sems):
    server = lax.axis_index("tok")
    group = slot_ref.shape[0]
    own = lax.rem(server, group)
    copies = [
        pltpu.make_async_copy(slot_hbm, slot_ref, sems.at[0]),
        pltpu.make_async_copy(count_hbm, count_ref, sems.at[1]),
    ]
    for copy in copies:
        copy.start()
    for copy in copies:
        copy.wait()
    for call, displacements in enumerate(calls):
        mask = jnp.int32(0)
        for i, displacement in enumerate(displacements):
            block = ((server ^ displacement) * rows) // QBLK
            for k in range(group):
                key_block = server ^ k
                slot = slot_ref[own, block, key_block]
                active = (slot >= 0) & (slot < count_ref[own, key_block])
                mask = mask | (active.astype(jnp.int32) << (i * group + k))
        mask_ref[call] = jnp.full(mask_ref.shape[1:], mask, jnp.int32)


def active_masks(task_slot, task_count, calls, rows):
    hbm = pl.BlockSpec(memory_space=pltpu.HBM)
    return pl.pallas_call(
        functools.partial(mask_kernel, calls, rows),
        out_shape=jax.ShapeDtypeStruct((len(calls), 8, HEAD_SIZE), jnp.int32),
        in_specs=[hbm] * 2,
        scratch_shapes=[
            pltpu.SMEM(task_slot.shape, task_slot.dtype),
            pltpu.SMEM(task_count.shape, task_count.dtype),
            pltpu.SemaphoreType.DMA((2,)),
        ],
        name="masks",
        cost_estimate=pl.CostEstimate(
            flops=0, bytes_accessed=4 * task_slot.size, transcendentals=0
        ),
        compiler_params=pltpu.CompilerParams(vmem_limit_bytes=4 << 20),
    )(task_slot, task_count)


def lay_cache_kernel(laid, *refs):
    *in_refs, _, k_ref, v_ref = refs
    keys = k_ref.shape[1]
    if laid:
        k_ref[:laid] = in_refs[0][...]
        v_ref[:laid] = in_refs[1][...]
        in_refs = in_refs[2:]
    for at, ref in enumerate(in_refs, laid):
        k_ref[at] = ref[:keys, :]
        v_ref[at, :HEAD_SIZE, :] = jnp.transpose(ref[keys:, :].astype(jnp.float32)).astype(
            jnp.bfloat16
        )
        v_ref[at, HEAD_SIZE:, :] = jnp.ones((SUM_ROWS, keys), jnp.bfloat16)


def lay_cache(pieces, after, before=()):
    vmem = pl.BlockSpec(memory_space=pltpu.VMEM)
    laid = before[0].shape[0] if before else 0
    group = laid + len(pieces)
    keys = pieces[0].shape[0] // 2
    return pl.pallas_call(
        functools.partial(lay_cache_kernel, laid),
        out_shape=[
            jax.ShapeDtypeStruct((group, keys, HEAD_SIZE), jnp.bfloat16),
            jax.ShapeDtypeStruct((group, HEAD_SIZE + SUM_ROWS, keys), jnp.bfloat16),
        ],
        in_specs=[vmem] * (len(before) + len(pieces)) + [pl.BlockSpec(memory_space=pl.ANY)],
        name="lay_cache",
        cost_estimate=pl.CostEstimate(
            flops=0, bytes_accessed=8 * group * keys * HEAD_SIZE, transcendentals=0
        ),
        compiler_params=pltpu.CompilerParams(vmem_limit_bytes=8 << 20),
    )(*before, *pieces, after)


def split_stat(stat, width):
    high = stat.astype(jnp.bfloat16).astype(jnp.float32)
    rest = stat - high
    middle = rest.astype(jnp.bfloat16).astype(jnp.float32)
    low = rest - middle
    row = lax.broadcasted_iota(jnp.int32, (STAT_ROWS, width), 0)
    spread = jnp.where(row == 0, high, jnp.where(row == 1, middle, jnp.where(row == 2, low, 0.0)))
    return spread.astype(jnp.bfloat16)


def join_stat(ref):
    stat = ref[HEAD_SIZE : HEAD_SIZE + STAT_ROWS, :].astype(jnp.float32)
    return stat[0:1] + stat[1:2] + stat[2:3]


def attention_kernel(plan, mask_ref, *refs):
    which, offset, widths, slab, group, blocks, resumed, ended = plan
    n_chunks = sum(widths)
    n_in = len(widths)
    q_in_refs = refs[:n_in]
    k_ref, v_ref, _ = refs[n_in : n_in + 3]
    at = n_in + 3
    before_refs = refs[at : at + resumed]
    at += resumed
    n_out = n_chunks if ended else 2
    out_refs = refs[at : at + n_out]
    at += n_out
    if ended:
        m_ref, acc_ref = refs[at : at + 2]
        at += 2
    else:
        m_ref, acc_ref = out_refs
    list_ref, q_ref, *slots = refs[at:]
    width = q_ref.shape[1]
    scale = HEAD_SIZE ** (-0.5) * LOG2E

    mask = mask_ref[which, 0, 0]
    found = jnp.int32(0)
    for i in range(n_chunks):
        for k in blocks:
            entry = i * group + k
            list_ref[found] = entry
            found = found + ((mask >> (offset * group + entry)) & 1)

    at = 0
    for q_in_ref, n in zip(q_in_refs, widths):
        for i in range(n):
            q_ref[at + i] = q_in_ref[i * width : (i + 1) * width, :]
        at += n
    if resumed:
        at = 0
        for m_before, acc_before in zip(before_refs[::2], before_refs[1::2]):
            n = m_before.shape[0]
            m_ref[at : at + n] = m_before[...]
            acc_ref[at : at + n] = acc_before[...]
            at += n
    else:
        m_ref[...] = jnp.full_like(m_ref, neg_fill)
        acc_ref[...] = jnp.zeros_like(acc_ref)

    def pair(i):
        entry = list_ref[i]
        return entry // group, lax.rem(entry, group)

    def score(i, slot, slabs=range(0, width, slab)):
        chunk, k = pair(i)
        s_ref, top_ref, fade_ref = slot
        for c in slabs:
            scores = lax.dot_general(
                k_ref[k],
                q_ref[chunk, c : c + slab, :],
                (((1,), (1,)), ((), ())),
                preferred_element_type=jnp.float32,
            )
            s_ref[:, c : c + slab] = scores
            old = m_ref[chunk, :, c : c + slab]
            new = jnp.maximum(old, jnp.max(scores, axis=0, keepdims=True))
            m_ref[chunk, :, c : c + slab] = new
            top_ref[:, c : c + slab] = new
            fade_ref[:, c : c + slab] = jnp.exp2((old - new) * scale)

    def weigh(i, slot, slabs=range(0, width, slab)):
        chunk, k = pair(i)
        s_ref, top_ref, fade_ref = slot
        for c in slabs:
            p = jnp.exp2((s_ref[:, c : c + slab] - top_ref[0:1, c : c + slab]) * scale)
            product = jnp.dot(
                v_ref[k], p.astype(jnp.bfloat16), preferred_element_type=jnp.float32
            )
            acc_ref[chunk, :, c : c + slab] = (
                acc_ref[chunk, :, c : c + slab] * fade_ref[0:1, c : c + slab] + product
            )

    even, odd = slots[:3], slots[3:]

    @pl.when(found > 0)
    def _():
        score(0, even)

    def step(i, here, there):
        @pl.when(i + 1 < found)
        def _():
            for c in range(0, width, slab):
                score(i + 1, there, (c,))
                weigh(i, here, (c,))

        @pl.when(i + 1 == found)
        def _():
            weigh(i, here)

    def two(j, carry):
        step(2 * j, even, odd)
        step(2 * j + 1, odd, even)
        return carry

    lax.fori_loop(0, (found + 1) // 2, two, 0)

    if not ended:
        return
    for i in range(n_chunks):
        total = acc_ref[i, HEAD_SIZE : HEAD_SIZE + 1, :]
        seen = total > 0.0
        safe = jnp.where(seen, total, 1.0)
        stat = jnp.where(seen, m_ref[i, 0:1, :] * scale + jnp.log2(safe), neg_fill)
        out_refs[i][:HEAD_SIZE, :] = (acc_ref[i, :HEAD_SIZE, :] * (1.0 / safe)).astype(jnp.bfloat16)
        out_refs[i][HEAD_SIZE:, :] = split_stat(stat, width)


def attention(
    chunks, which, cache, masks, width, after, group, blocks, offset=0, before=(), ended=True
):
    k, v = cache
    keys = k.shape[1]
    widths = tuple(chunk.shape[0] // width for chunk in chunks)
    n = sum(widths)
    vmem = pl.BlockSpec(memory_space=pltpu.VMEM)
    state = [(n, 8, width), (n, HEAD_SIZE + SUM_ROWS, width)]
    slot = [
        pltpu.VMEM((keys, width), jnp.float32),
        pltpu.VMEM((8, width), jnp.float32),
        pltpu.VMEM((8, width), jnp.float32),
    ]
    if ended:
        out_shape = [jax.ShapeDtypeStruct((HEAD_SIZE + STAT_ROWS, width), jnp.bfloat16)] * n
        scratch = [pltpu.VMEM(shape, jnp.float32) for shape in state]
    else:
        out_shape = [jax.ShapeDtypeStruct(shape, jnp.float32) for shape in state]
        scratch = []
    pairs = n * len(blocks)
    plan = (which, offset, widths, min(256, width), group, tuple(blocks), len(before), ended)
    return pl.pallas_call(
        functools.partial(attention_kernel, plan),
        out_shape=out_shape,
        in_specs=[vmem] * (len(chunks) + 3)
        + [pl.BlockSpec(memory_space=pl.ANY)]
        + [vmem] * len(before),
        out_specs=[vmem] * len(out_shape),
        scratch_shapes=scratch
        + [
            pltpu.SMEM((pairs + 1,), jnp.int32),
            pltpu.VMEM((n, width, HEAD_SIZE), jnp.bfloat16),
        ]
        + slot
        + slot,
        name="attention",
        cost_estimate=pl.CostEstimate(
            flops=4 * pairs * keys * width * HEAD_SIZE,
            bytes_accessed=4 * n * width * HEAD_SIZE + 4 * len(blocks) * keys * HEAD_SIZE,
            transcendentals=pairs * keys * width,
        ),
        compiler_params=pltpu.CompilerParams(vmem_limit_bytes=20 << 20),
    )(masks, *chunks, k, v, after, *before)


def merge_kernel(n_in, keep_stat, *refs):
    in_refs, out_refs = refs[:n_in], refs[n_in + 1 :]
    stats = [join_stat(ref) for ref in in_refs]
    largest = functools.reduce(jnp.maximum, stats)
    weights = [jnp.exp2(stat - largest) for stat in stats]
    total = functools.reduce(jnp.add, weights)
    inverse = 1.0 / total
    value = functools.reduce(
        jnp.add,
        [
            (weight * inverse) * ref[:HEAD_SIZE, :].astype(jnp.float32)
            for weight, ref in zip(weights, in_refs)
        ],
    ).astype(jnp.bfloat16)
    stat = largest + jnp.log2(total)
    part = out_refs[0].shape[1]
    for i, out_ref in enumerate(out_refs):
        span = slice(i * part, (i + 1) * part)
        out_ref[:HEAD_SIZE, :] = value[:, span]
        if keep_stat:
            out_ref[HEAD_SIZE:, :] = split_stat(stat[:, span], part)


def merge(messages, parts, keep_stat=True, after=None):
    vmem = pl.BlockSpec(memory_space=pltpu.VMEM)
    after = messages[0] if after is None else after
    height, width = messages[0].shape
    height = height if keep_stat else HEAD_SIZE
    size = len(messages) * height * width
    return pl.pallas_call(
        functools.partial(merge_kernel, len(messages), keep_stat),
        out_shape=[jax.ShapeDtypeStruct((height, width // parts), jnp.bfloat16)] * parts,
        in_specs=[vmem] * len(messages) + [pl.BlockSpec(memory_space=pl.ANY)],
        name="merge" if keep_stat else "finish",
        cost_estimate=pl.CostEstimate(flops=4 * size, bytes_accessed=4 * size, transcendentals=0),
        compiler_params=pltpu.CompilerParams(vmem_limit_bytes=8 << 20),
    )(*messages, after)


def gather_kernel(rows, *refs):
    *piece_refs, out_ref = refs
    core = lax.rem(lax.axis_index("tok"), len(piece_refs))
    per = piece_refs[0].shape[1] // rows
    for offset, piece_ref in enumerate(piece_refs):
        for j in range(per):
            block = jnp.transpose(piece_ref[:, j * rows : (j + 1) * rows].astype(jnp.float32))
            start = pl.multiple_of(((core ^ offset) * per + j) * HEAD_SIZE, HEAD_SIZE)
            out_ref[:, pl.ds(start, HEAD_SIZE)] = block.astype(jnp.bfloat16)


def gather(pieces, rows):
    width = sum(piece.shape[1] for piece in pieces) // rows * HEAD_SIZE
    return pl.pallas_call(
        functools.partial(gather_kernel, rows),
        out_shape=jax.ShapeDtypeStruct((rows, width), jnp.bfloat16),
        name="gather",
        cost_estimate=pl.CostEstimate(
            flops=0, bytes_accessed=4 * rows * width, transcendentals=0
        ),
        compiler_params=pltpu.CompilerParams(vmem_limit_bytes=4 << 20),
    )(*pieces)


def project_kernel(plan, left_ref, w_ref, *refs):
    half, start, away = plan
    out_ref = refs[-1]
    columns = out_ref.shape[1]
    depth = left_ref.shape[1]
    base_start = start
    if half is not None:
        start = (lax.axis_index("head") ^ half) * (w_ref.shape[1] // 2) + start
    start = pl.multiple_of(start, HEAD_SIZE)
    row = 0
    if depth < w_ref.shape[0]:
        group = w_ref.shape[0] // depth * 2
        row = pl.multiple_of((lax.rem(lax.axis_index("tok"), group) // 2 ^ away) * depth, depth)
    total = jnp.dot(
        left_ref[...],
        w_ref[pl.ds(row, depth), pl.ds(start, columns)],
        preferred_element_type=jnp.float32,
    )
    if len(refs) == 2:
        total = total + refs[0][:, base_start : base_start + columns]
    out_ref[...] = total.astype(out_ref.dtype)


def project(left, out_weight, half, start, columns, kind, away=0, base=None):
    rows, depth = left.shape
    operands = (left, out_weight) if base is None else (left, out_weight, base)
    return pl.pallas_call(
        functools.partial(project_kernel, (half, start, away)),
        out_shape=jax.ShapeDtypeStruct((rows, columns), kind),
        in_specs=[pl.BlockSpec(memory_space=pltpu.VMEM)] * len(operands),
        out_specs=pl.BlockSpec(memory_space=pltpu.VMEM),
        name="project",
        cost_estimate=pl.CostEstimate(
            flops=2 * rows * depth * columns,
            bytes_accessed=2 * depth * columns,
            transcendentals=0,
        ),
        compiler_params=pltpu.CompilerParams(vmem_limit_bytes=24 << 20),
    )(*operands)


def swap(x, bits, servers):
    return lax.ppermute(x, "tok", [(i, i ^ bits) for i in range(servers)])


def attend_grouped(queries, keys, values, out_weight, task_slot, task_count, move):
    core, column, near, far = 1, 2, 4, 8
    rows = queries.shape[0]
    q_per_kv = HEADS // KVH
    part = q_per_kv * rows
    width = 2 * part

    keep, give = pack_queries(queries, 4, ((0, 2), (1, 3)))
    pieces = pack_cache(keys, values, 4, ((0,), (core,), (column,), (column | core,)))
    got = move(give, core)
    own = jnp.concatenate([keep[:part], got[:part]], axis=0)
    other = move(jnp.concatenate([keep[part:], got[part:]], axis=0), column)
    across = move(pieces[2], column)
    beyond = move(pieces[3], column | core)
    own_far = move(own, far)
    beside = move(pieces[1], core)
    other_far = move(other, far)
    own_near = move(own, near)
    other_near = move(other, near)
    own_last = move(own_far, near)
    other_last = move(other_far, near)

    calls = (
        (0, column, near, far, near | column, far | column),
        (far | near,),
        (far | near | column,),
    )
    masks = active_masks(task_slot, task_count, calls, rows)
    chip_cache = lay_cache([pieces[0], beside], masks)

    def first(chunks, offset, after):
        return attention(
            chunks, 0, chip_cache, masks, width, after, 4, (0, core), offset, ended=False
        )

    def call(chunks, which, after):
        return attention(chunks, which, cache, masks, width, after, 4, range(4))

    chunks = [own, other, own_near, own_far, other_near, other_far]
    own_state = first(chunks[:2], 0, masks)
    a_state = first(chunks[2:4], 2, own_state[0])
    b_state = first(chunks[4:], 4, a_state[0])
    cache = lay_cache([across, beyond], b_state[0], chip_cache)
    own_a, own_b, near_a, far_a, near_b, far_b = attention(
        chunks,
        0,
        cache,
        masks,
        width,
        b_state[0],
        4,
        (column, column | core),
        before=(*own_state, *a_state, *b_state),
    )
    (last_a,) = call([own_last], 1, far_b)
    (last_b,) = call([other_last], 2, last_a)

    last_a = move(last_a, near)
    last_b = move(last_b, near)
    near_b = move(near_b, near | column)
    near_a = move(near_a, near)
    own_b = move(own_b, column)
    (far_a,) = merge([far_a, last_a], 1)
    far_a = move(far_a, far)
    (far_b,) = merge([far_b, last_b], 1)
    far_b = move(far_b, far | column)
    b_own, b_other = merge([own_b, near_b, far_b], 2, False)
    b_other = move(b_other, core)
    left_b = gather([b_own, b_other], rows)
    columns = out_weight.shape[1] // 2
    base = project(left_b, out_weight, 1, 0, columns, jnp.float32, away=1)
    a_own, a_other = merge([own_a, near_a, far_a], 2, False, after=base)
    a_other = move(a_other, core)
    left_a = gather([a_own, a_other], rows)

    piece = columns // 2
    arrived = []
    for i in range(2):
        part = project(left_a, out_weight, 1, i * piece, piece, jnp.bfloat16, base=base)
        arrived.append(lax.ppermute(part, "head", [(0, 1), (1, 0)]))
    here = project(left_b, out_weight, 0, 0, columns, jnp.float32, away=1)
    here = project(left_a, out_weight, 0, 0, columns, jnp.float32, base=here)
    return (here + jnp.concatenate(arrived, axis=1).astype(jnp.float32)).astype(jnp.bfloat16)


def attend_general(queries, keys, values, task_slot, task_count, move, servers):
    assert task_slot.shape[0] == 1
    rows = queries.shape[0]
    width = HEADS // KVH * rows
    step = min(4, servers)
    calls = tuple(tuple(range(i, i + step)) for i in range(0, servers, step))
    (own,) = pack_queries(queries, 1, ((0,),))
    masks = active_masks(task_slot, task_count, calls, rows)
    cache = lay_cache(pack_cache(keys, values, 1, ((0,),)), masks)
    held = {0: own}
    bit = servers // 2
    while bit:
        held.update({d ^ bit: move(chunk, bit) for d, chunk in held.items()})
        bit //= 2
    partial = {}
    for which, call in enumerate(calls):
        result = attention(
            [held[d] for d in call], which, cache, masks, width, masks, 1, range(1)
        )
        for j, d in enumerate(call):
            partial[d] = [result[j]]
    bit = 1
    while bit < servers:
        for d in sorted(partial, reverse=True):
            if d & bit:
                messages = partial.pop(d)
                message = messages[0] if len(messages) == 1 else merge(messages, 1)[0]
                partial[d ^ bit].append(move(message, bit))
        bit *= 2
    return merge(partial[0], 1, False)


def on_device(queries, keys, values, out_weight, task_slot, task_count):
    servers = lax.axis_size("tok")
    heads = lax.axis_size("head")
    rows = queries.shape[0]
    group = task_slot.shape[0]
    move = functools.partial(swap, servers=servers)
    if group == 4 and servers == 16 and heads == 2:
        return attend_grouped(
            queries, keys, values, out_weight, task_slot, task_count, move
        )
    attended = attend_general(queries, keys, values, task_slot, task_count, move, servers)
    left = gather(attended, rows)
    share = project(left, out_weight, None, 0, out_weight.shape[1], jnp.bfloat16)
    return lax.psum_scatter(share, "head", scatter_dimension=1, tiled=True)


def solution(mesh):
    placed = (
        P("tok", "head"),
        P("tok", "head"),
        P("tok", "head"),
        P("head", None),
        P("head", None, None),
        P("head", None),
    )
    return jax.shard_map(
        on_device, mesh=mesh, in_specs=placed, out_specs=P("tok", "head"), check_vma=False
    )
```

```python
import functools
import math

import jax
import jax.numpy as jnp
from jax import lax
from jax.experimental import pallas as pl
from jax.experimental.pallas import tpu as pltpu
from jax.sharding import PartitionSpec as P


HEADS = 32
KVH = 8
HEAD_SIZE = 128
QBLK = 128

theta_base = 500000.0
neg_fill = -1e30
LOG2E = math.log2(math.e)
STAT_ROWS = 8
SUM_ROWS = 16
PACK_VMEM = 47 << 20


def rotary_tables(rows, first_row):
    half = HEAD_SIZE // 2
    frequency = theta_base ** (-(jnp.arange(half, dtype=jnp.float32) * (2.0 / HEAD_SIZE)))
    places = (first_row + jnp.arange(rows, dtype=jnp.int32)).astype(jnp.float32)
    angles = places[:, None] * frequency[None, :]
    cosine = jnp.cos(angles)
    sine = jnp.sin(angles)
    return (
        jnp.concatenate([cosine, cosine], axis=1),
        jnp.concatenate([-sine, sine], axis=1),
    )


def pack_queries_kernel(order, q_per_kv, group, cos_ref, sin_ref, q_ref, *out_refs):
    own = lax.rem(lax.axis_index("tok"), group)
    rows = q_ref.shape[0]
    cosine = cos_ref[...]
    sine = sin_ref[...]
    for offsets, out_ref in zip(order, out_refs):
        for at, offset in enumerate(offsets):
            head = own ^ offset
            for j in range(q_per_kv):
                start = pl.multiple_of((head * q_per_kv + j) * HEAD_SIZE, HEAD_SIZE)
                x = q_ref[:, pl.ds(start, HEAD_SIZE)].astype(jnp.float32)
                turned = pltpu.roll(x, HEAD_SIZE // 2, 1)
                row = (at * q_per_kv + j) * rows
                out_ref[row : row + rows, :] = (x * cosine + turned * sine).astype(jnp.bfloat16)


def pack_queries(queries, group, order):
    rows = queries.shape[0]
    q_per_kv = HEADS // KVH
    cosine, sine = rotary_tables(rows, lax.axis_index("tok") * rows)
    return pl.pallas_call(
        functools.partial(pack_queries_kernel, order, q_per_kv, group),
        out_shape=[
            jax.ShapeDtypeStruct((len(offsets) * q_per_kv * rows, HEAD_SIZE), jnp.bfloat16)
            for offsets in order
        ],
        name="pack_queries",
        cost_estimate=pl.CostEstimate(
            flops=6 * queries.size, bytes_accessed=4 * queries.size, transcendentals=0
        ),
        compiler_params=pltpu.CompilerParams(vmem_limit_bytes=PACK_VMEM),
    )(cosine, sine, queries)


def pack_cache_kernel(order, group, k_ref, v_ref, *out_refs):
    own = lax.rem(lax.axis_index("tok"), group)
    keys = k_ref.shape[0]
    for offsets, out_ref in zip(order, out_refs):
        for at, offset in enumerate(offsets):
            start = pl.multiple_of((own ^ offset) * HEAD_SIZE, HEAD_SIZE)
            row = 2 * at * keys
            out_ref[row : row + keys, :] = k_ref[:, pl.ds(start, HEAD_SIZE)]
            out_ref[row + keys : row + 2 * keys, :] = v_ref[:, pl.ds(start, HEAD_SIZE)]


def pack_cache(keys, values, group, order):
    return pl.pallas_call(
        functools.partial(pack_cache_kernel, order, group),
        out_shape=[
            jax.ShapeDtypeStruct((len(offsets) * 2 * keys.shape[0], HEAD_SIZE), jnp.bfloat16)
            for offsets in order
        ],
        name="pack_cache",
        cost_estimate=pl.CostEstimate(
            flops=0, bytes_accessed=8 * keys.size, transcendentals=0
        ),
        compiler_params=pltpu.CompilerParams(vmem_limit_bytes=PACK_VMEM),
    )(keys, values)


def mask_kernel(calls, rows, slot_hbm, count_hbm, mask_ref, slot_ref, count_ref, sems):
    server = lax.axis_index("tok")
    group = slot_ref.shape[0]
    own = lax.rem(server, group)
    copies = [
        pltpu.make_async_copy(slot_hbm, slot_ref, sems.at[0]),
        pltpu.make_async_copy(count_hbm, count_ref, sems.at[1]),
    ]
    for copy in copies:
        copy.start()
    for copy in copies:
        copy.wait()
    for call, displacements in enumerate(calls):
        mask = jnp.int32(0)
        for i, displacement in enumerate(displacements):
            block = ((server ^ displacement) * rows) // QBLK
            for k in range(group):
                key_block = server ^ k
                slot = slot_ref[own, block, key_block]
                active = (slot >= 0) & (slot < count_ref[own, key_block])
                mask = mask | (active.astype(jnp.int32) << (i * group + k))
        mask_ref[call] = jnp.full(mask_ref.shape[1:], mask, jnp.int32)


def active_masks(task_slot, task_count, calls, rows):
    hbm = pl.BlockSpec(memory_space=pltpu.HBM)
    return pl.pallas_call(
        functools.partial(mask_kernel, calls, rows),
        out_shape=jax.ShapeDtypeStruct((len(calls), 8, HEAD_SIZE), jnp.int32),
        in_specs=[hbm] * 2,
        scratch_shapes=[
            pltpu.SMEM(task_slot.shape, task_slot.dtype),
            pltpu.SMEM(task_count.shape, task_count.dtype),
            pltpu.SemaphoreType.DMA((2,)),
        ],
        name="masks",
        cost_estimate=pl.CostEstimate(
            flops=0, bytes_accessed=4 * task_slot.size, transcendentals=0
        ),
        compiler_params=pltpu.CompilerParams(vmem_limit_bytes=4 << 20),
    )(task_slot, task_count)


def lay_cache_kernel(laid, *refs):
    *in_refs, _, k_ref, v_ref = refs
    keys = k_ref.shape[1]
    if laid:
        k_ref[:laid] = in_refs[0][...]
        v_ref[:laid] = in_refs[1][...]
        in_refs = in_refs[2:]
    for at, ref in enumerate(in_refs, laid):
        k_ref[at] = ref[:keys, :]
        v_ref[at, :HEAD_SIZE, :] = jnp.transpose(ref[keys:, :].astype(jnp.float32)).astype(
            jnp.bfloat16
        )
        v_ref[at, HEAD_SIZE:, :] = jnp.ones((SUM_ROWS, keys), jnp.bfloat16)


def lay_cache(pieces, after, before=()):
    vmem = pl.BlockSpec(memory_space=pltpu.VMEM)
    laid = before[0].shape[0] if before else 0
    group = laid + len(pieces)
    keys = pieces[0].shape[0] // 2
    return pl.pallas_call(
        functools.partial(lay_cache_kernel, laid),
        out_shape=[
            jax.ShapeDtypeStruct((group, keys, HEAD_SIZE), jnp.bfloat16),
            jax.ShapeDtypeStruct((group, HEAD_SIZE + SUM_ROWS, keys), jnp.bfloat16),
        ],
        in_specs=[vmem] * (len(before) + len(pieces)) + [pl.BlockSpec(memory_space=pl.ANY)],
        name="lay_cache",
        cost_estimate=pl.CostEstimate(
            flops=0, bytes_accessed=8 * group * keys * HEAD_SIZE, transcendentals=0
        ),
        compiler_params=pltpu.CompilerParams(vmem_limit_bytes=8 << 20),
    )(*before, *pieces, after)


def split_stat(stat, width):
    high = stat.astype(jnp.bfloat16).astype(jnp.float32)
    rest = stat - high
    middle = rest.astype(jnp.bfloat16).astype(jnp.float32)
    low = rest - middle
    row = lax.broadcasted_iota(jnp.int32, (STAT_ROWS, width), 0)
    spread = jnp.where(row == 0, high, jnp.where(row == 1, middle, jnp.where(row == 2, low, 0.0)))
    return spread.astype(jnp.bfloat16)


def join_stat(ref):
    stat = ref[HEAD_SIZE : HEAD_SIZE + STAT_ROWS, :].astype(jnp.float32)
    return stat[0:1] + stat[1:2] + stat[2:3]


def attention_kernel(plan, mask_ref, *refs):
    which, offset, widths, slab, group, blocks, resumed, ended = plan
    n_chunks = sum(widths)
    n_in = len(widths)
    q_in_refs = refs[:n_in]
    k_ref, v_ref, _ = refs[n_in : n_in + 3]
    at = n_in + 3
    before_refs = refs[at : at + resumed]
    at += resumed
    n_out = n_chunks if ended else 2
    out_refs = refs[at : at + n_out]
    at += n_out
    if ended:
        m_ref, acc_ref = refs[at : at + 2]
        at += 2
    else:
        m_ref, acc_ref = out_refs
    list_ref, q_ref, *slots = refs[at:]
    width = q_ref.shape[1]
    scale = HEAD_SIZE ** (-0.5) * LOG2E

    mask = mask_ref[which, 0, 0]
    found = jnp.int32(0)
    for i in range(n_chunks):
        for k in blocks:
            entry = i * group + k
            list_ref[found] = entry
            found = found + ((mask >> (offset * group + entry)) & 1)

    at = 0
    for q_in_ref, n in zip(q_in_refs, widths):
        for i in range(n):
            q_ref[at + i] = q_in_ref[i * width : (i + 1) * width, :]
        at += n
    if resumed:
        at = 0
        for m_before, acc_before in zip(before_refs[::2], before_refs[1::2]):
            n = m_before.shape[0]
            m_ref[at : at + n] = m_before[...]
            acc_ref[at : at + n] = acc_before[...]
            at += n
    else:
        m_ref[...] = jnp.full_like(m_ref, neg_fill)
        acc_ref[...] = jnp.zeros_like(acc_ref)

    def pair(i):
        entry = list_ref[i]
        return entry // group, lax.rem(entry, group)

    def score(i, slot, slabs=range(0, width, slab)):
        chunk, k = pair(i)
        s_ref, top_ref, fade_ref = slot
        for c in slabs:
            scores = lax.dot_general(
                k_ref[k],
                q_ref[chunk, c : c + slab, :],
                (((1,), (1,)), ((), ())),
                preferred_element_type=jnp.float32,
            )
            s_ref[:, c : c + slab] = scores
            old = m_ref[chunk, :, c : c + slab]
            new = jnp.maximum(old, jnp.max(scores, axis=0, keepdims=True))
            m_ref[chunk, :, c : c + slab] = new
            top_ref[:, c : c + slab] = new
            fade_ref[:, c : c + slab] = jnp.exp2((old - new) * scale)

    def weigh(i, slot, slabs=range(0, width, slab)):
        chunk, k = pair(i)
        s_ref, top_ref, fade_ref = slot
        for c in slabs:
            p = jnp.exp2((s_ref[:, c : c + slab] - top_ref[0:1, c : c + slab]) * scale)
            product = jnp.dot(
                v_ref[k], p.astype(jnp.bfloat16), preferred_element_type=jnp.float32
            )
            acc_ref[chunk, :, c : c + slab] = (
                acc_ref[chunk, :, c : c + slab] * fade_ref[0:1, c : c + slab] + product
            )

    even, odd = slots[:3], slots[3:]

    @pl.when(found > 0)
    def _():
        score(0, even)

    def step(i, here, there):
        @pl.when(i + 1 < found)
        def _():
            for c in range(0, width, slab):
                score(i + 1, there, (c,))
                weigh(i, here, (c,))

        @pl.when(i + 1 == found)
        def _():
            weigh(i, here)

    def two(j, carry):
        step(2 * j, even, odd)
        step(2 * j + 1, odd, even)
        return carry

    lax.fori_loop(0, (found + 1) // 2, two, 0)

    if not ended:
        return
    for i in range(n_chunks):
        total = acc_ref[i, HEAD_SIZE : HEAD_SIZE + 1, :]
        seen = total > 0.0
        safe = jnp.where(seen, total, 1.0)
        stat = jnp.where(seen, m_ref[i, 0:1, :] * scale + jnp.log2(safe), neg_fill)
        out_refs[i][:HEAD_SIZE, :] = (acc_ref[i, :HEAD_SIZE, :] * (1.0 / safe)).astype(jnp.bfloat16)
        out_refs[i][HEAD_SIZE:, :] = split_stat(stat, width)


def attention(
    chunks, which, cache, masks, width, after, group, blocks, offset=0, before=(), ended=True
):
    k, v = cache
    keys = k.shape[1]
    widths = tuple(chunk.shape[0] // width for chunk in chunks)
    n = sum(widths)
    vmem = pl.BlockSpec(memory_space=pltpu.VMEM)
    state = [(n, 8, width), (n, HEAD_SIZE + SUM_ROWS, width)]
    slot = [
        pltpu.VMEM((keys, width), jnp.float32),
        pltpu.VMEM((8, width), jnp.float32),
        pltpu.VMEM((8, width), jnp.float32),
    ]
    if ended:
        out_shape = [jax.ShapeDtypeStruct((HEAD_SIZE + STAT_ROWS, width), jnp.bfloat16)] * n
        scratch = [pltpu.VMEM(shape, jnp.float32) for shape in state]
    else:
        out_shape = [jax.ShapeDtypeStruct(shape, jnp.float32) for shape in state]
        scratch = []
    pairs = n * len(blocks)
    plan = (which, offset, widths, min(256, width), group, tuple(blocks), len(before), ended)
    return pl.pallas_call(
        functools.partial(attention_kernel, plan),
        out_shape=out_shape,
        in_specs=[vmem] * (len(chunks) + 3)
        + [pl.BlockSpec(memory_space=pl.ANY)]
        + [vmem] * len(before),
        out_specs=[vmem] * len(out_shape),
        scratch_shapes=scratch
        + [
            pltpu.SMEM((pairs + 1,), jnp.int32),
            pltpu.VMEM((n, width, HEAD_SIZE), jnp.bfloat16),
        ]
        + slot
        + slot,
        name="attention",
        cost_estimate=pl.CostEstimate(
            flops=4 * pairs * keys * width * HEAD_SIZE,
            bytes_accessed=4 * n * width * HEAD_SIZE + 4 * len(blocks) * keys * HEAD_SIZE,
            transcendentals=pairs * keys * width,
        ),
        compiler_params=pltpu.CompilerParams(vmem_limit_bytes=20 << 20),
    )(masks, *chunks, k, v, after, *before)


def merge_kernel(lanes, keep_stat, *refs):
    in_refs, out_refs = refs[: len(lanes)], refs[len(lanes) + 1 :]
    in_refs = [ref.at[:, span] for ref, span in zip(in_refs, lanes)]
    stats = [join_stat(ref) for ref in in_refs]
    largest = functools.reduce(jnp.maximum, stats)
    weights = [jnp.exp2(stat - largest) for stat in stats]
    total = functools.reduce(jnp.add, weights)
    inverse = 1.0 / total
    value = functools.reduce(
        jnp.add,
        [
            (weight * inverse) * ref[:HEAD_SIZE, :].astype(jnp.float32)
            for weight, ref in zip(weights, in_refs)
        ],
    ).astype(jnp.bfloat16)
    stat = largest + jnp.log2(total)
    part = out_refs[0].shape[1]
    for i, out_ref in enumerate(out_refs):
        span = slice(i * part, (i + 1) * part)
        out_ref[:HEAD_SIZE, :] = value[:, span]
        if keep_stat:
            out_ref[HEAD_SIZE:, :] = split_stat(stat[:, span], part)


def merge(messages, parts, keep_stat=True, after=None):
    vmem = pl.BlockSpec(memory_space=pltpu.VMEM)
    after = messages[0] if after is None else after
    height, width = messages[0].shape
    height = height if keep_stat else HEAD_SIZE
    size = len(messages) * height * width
    pairs = [m if isinstance(m, tuple) else (m, 0) for m in messages]
    lanes = tuple(slice(i * width, (i + 1) * width) for _, i in pairs)
    return pl.pallas_call(
        functools.partial(merge_kernel, lanes, keep_stat),
        out_shape=[jax.ShapeDtypeStruct((height, width // parts), jnp.bfloat16)] * parts,
        in_specs=[vmem] * len(messages) + [pl.BlockSpec(memory_space=pl.ANY)],
        name="merge" if keep_stat else "finish",
        cost_estimate=pl.CostEstimate(flops=4 * size, bytes_accessed=4 * size, transcendentals=0),
        compiler_params=pltpu.CompilerParams(vmem_limit_bytes=8 << 20),
    )(*[array for array, _ in pairs], after)


def gather_kernel(rows, *refs):
    *piece_refs, out_ref = refs
    core = lax.rem(lax.axis_index("tok"), len(piece_refs))
    per = piece_refs[0].shape[1] // rows
    for offset, piece_ref in enumerate(piece_refs):
        for j in range(per):
            block = jnp.transpose(piece_ref[:, j * rows : (j + 1) * rows].astype(jnp.float32))
            start = pl.multiple_of(((core ^ offset) * per + j) * HEAD_SIZE, HEAD_SIZE)
            out_ref[:, pl.ds(start, HEAD_SIZE)] = block.astype(jnp.bfloat16)


def gather(pieces, rows):
    width = sum(piece.shape[1] for piece in pieces) // rows * HEAD_SIZE
    return pl.pallas_call(
        functools.partial(gather_kernel, rows),
        out_shape=jax.ShapeDtypeStruct((rows, width), jnp.bfloat16),
        name="gather",
        cost_estimate=pl.CostEstimate(
            flops=0, bytes_accessed=4 * rows * width, transcendentals=0
        ),
        compiler_params=pltpu.CompilerParams(vmem_limit_bytes=4 << 20),
    )(*pieces)


def project_kernel(plan, left_ref, w_ref, *refs):
    half, start, away = plan
    out_ref = refs[-1]
    columns = out_ref.shape[1]
    depth = left_ref.shape[1]
    base_start = start
    if half is not None:
        start = (lax.axis_index("head") ^ half) * (w_ref.shape[1] // 2) + start
    start = pl.multiple_of(start, HEAD_SIZE)
    row = 0
    if depth < w_ref.shape[0]:
        group = w_ref.shape[0] // depth * 2
        row = pl.multiple_of((lax.rem(lax.axis_index("tok"), group) // 2 ^ away) * depth, depth)
    total = jnp.dot(
        left_ref[...],
        w_ref[pl.ds(row, depth), pl.ds(start, columns)],
        preferred_element_type=jnp.float32,
    )
    if len(refs) == 2:
        total = total + refs[0][:, base_start : base_start + columns]
    out_ref[...] = total.astype(out_ref.dtype)


def project(left, out_weight, half, start, columns, kind, away=0, base=None):
    rows, depth = left.shape
    operands = (left, out_weight) if base is None else (left, out_weight, base)
    return pl.pallas_call(
        functools.partial(project_kernel, (half, start, away)),
        out_shape=jax.ShapeDtypeStruct((rows, columns), kind),
        in_specs=[pl.BlockSpec(memory_space=pltpu.VMEM)] * len(operands),
        out_specs=pl.BlockSpec(memory_space=pltpu.VMEM),
        name="project",
        cost_estimate=pl.CostEstimate(
            flops=2 * rows * depth * columns,
            bytes_accessed=2 * depth * columns,
            transcendentals=0,
        ),
        compiler_params=pltpu.CompilerParams(vmem_limit_bytes=24 << 20),
    )(*operands)


def swap(x, bits, servers):
    return lax.ppermute(x, "tok", [(i, i ^ bits) for i in range(servers)])


def attend_grouped(queries, keys, values, out_weight, task_slot, task_count, move):
    core, column, near, far = 1, 2, 4, 8
    rows = queries.shape[0]
    q_per_kv = HEADS // KVH
    part = q_per_kv * rows
    width = 2 * part

    keep, give = pack_queries(queries, 4, ((0, 2), (1, 3)))
    pieces = pack_cache(keys, values, 4, ((0,), (core,), (column,), (column | core,)))
    got = move(give, core)
    own = jnp.concatenate([keep[:part], got[:part]], axis=0)
    other = move(jnp.concatenate([keep[part:], got[part:]], axis=0), column)
    across = move(pieces[2], column)
    beyond = move(pieces[3], column | core)
    own_far = move(own, far)
    beside = move(pieces[1], core)
    other_far = move(other, far)
    own_near = move(own, near)
    other_near = move(other, near)
    own_last = move(own_far, near)
    other_last = move(other_far, near)

    calls = (
        (0, column, near, far, near | column, far | column),
        (far | near,),
        (far | near | column,),
    )
    masks = active_masks(task_slot, task_count, calls, rows)
    chip_cache = lay_cache([pieces[0], beside], masks)

    def first(chunks, offset, after):
        return attention(
            chunks, 0, chip_cache, masks, width, after, 4, (0, core), offset, ended=False
        )

    def call(chunks, which, after):
        return attention(chunks, which, cache, masks, width, after, 4, range(4))

    chunks = [own, other, own_near, own_far, other_near, other_far]
    own_state = first(chunks[:2], 0, masks)
    a_state = first(chunks[2:4], 2, own_state[0])
    b_state = first(chunks[4:], 4, a_state[0])
    cache = lay_cache([across, beyond], b_state[0], chip_cache)
    own_a, own_b, near_a, far_a, near_b, far_b = attention(
        chunks,
        0,
        cache,
        masks,
        width,
        b_state[0],
        4,
        (column, column | core),
        before=(*own_state, *a_state, *b_state),
    )
    (last_a,) = call([own_last], 1, far_b)
    (last_b,) = call([other_last], 2, last_a)

    far_b = move(far_b, far | column)
    last_a = move(last_a, near)
    last_b = move(last_b, far | near | column)
    near_both = move(jnp.concatenate([near_a, near_b], axis=1), near)
    (own_b,) = merge([own_b, (near_both, 1)], 1)
    own_b = move(own_b, column)
    (far_a,) = merge([far_a, last_a], 1)
    far_a = move(far_a, far)
    b_own, b_other = merge([own_b, far_b, last_b], 2, False)
    b_other = move(b_other, core)
    left_b = gather([b_own, b_other], rows)
    columns = out_weight.shape[1] // 2
    base = project(left_b, out_weight, 1, 0, columns, jnp.float32, away=1)
    a_own, a_other = merge([own_a, (near_both, 0), far_a], 2, False, after=base)
    a_other = move(a_other, core)
    left_a = gather([a_own, a_other], rows)

    piece = columns // 2
    arrived = []
    for i in range(2):
        part = project(left_a, out_weight, 1, i * piece, piece, jnp.bfloat16, base=base)
        arrived.append(lax.ppermute(part, "head", [(0, 1), (1, 0)]))
    here = project(left_b, out_weight, 0, 0, columns, jnp.float32, away=1)
    here = project(left_a, out_weight, 0, 0, columns, jnp.float32, base=here)
    return (here + jnp.concatenate(arrived, axis=1).astype(jnp.float32)).astype(jnp.bfloat16)


def attend_general(queries, keys, values, task_slot, task_count, move, servers):
    assert task_slot.shape[0] == 1
    rows = queries.shape[0]
    width = HEADS // KVH * rows
    step = min(4, servers)
    calls = tuple(tuple(range(i, i + step)) for i in range(0, servers, step))
    (own,) = pack_queries(queries, 1, ((0,),))
    masks = active_masks(task_slot, task_count, calls, rows)
    cache = lay_cache(pack_cache(keys, values, 1, ((0,),)), masks)
    held = {0: own}
    bit = servers // 2
    while bit:
        held.update({d ^ bit: move(chunk, bit) for d, chunk in held.items()})
        bit //= 2
    partial = {}
    for which, call in enumerate(calls):
        result = attention(
            [held[d] for d in call], which, cache, masks, width, masks, 1, range(1)
        )
        for j, d in enumerate(call):
            partial[d] = [result[j]]
    bit = 1
    while bit < servers:
        for d in sorted(partial, reverse=True):
            if d & bit:
                messages = partial.pop(d)
                message = messages[0] if len(messages) == 1 else merge(messages, 1)[0]
                partial[d ^ bit].append(move(message, bit))
        bit *= 2
    return merge(partial[0], 1, False)


def on_device(queries, keys, values, out_weight, task_slot, task_count):
    servers = lax.axis_size("tok")
    heads = lax.axis_size("head")
    rows = queries.shape[0]
    group = task_slot.shape[0]
    move = functools.partial(swap, servers=servers)
    if group == 4 and servers == 16 and heads == 2:
        return attend_grouped(
            queries, keys, values, out_weight, task_slot, task_count, move
        )
    attended = attend_general(queries, keys, values, task_slot, task_count, move, servers)
    left = gather(attended, rows)
    share = project(left, out_weight, None, 0, out_weight.shape[1], jnp.bfloat16)
    return lax.psum_scatter(share, "head", scatter_dimension=1, tiled=True)


def solution(mesh):
    placed = (
        P("tok", "head"),
        P("tok", "head"),
        P("tok", "head"),
        P("head", None),
        P("head", None, None),
        P("head", None),
    )
    return jax.shard_map(
        on_device, mesh=mesh, in_specs=placed, out_specs=P("tok", "head"), check_vma=False
    )
```

```python
import functools
import math

import jax
import jax.numpy as jnp
from jax import lax
from jax.experimental import pallas as pl
from jax.experimental.pallas import tpu as pltpu
from jax.sharding import PartitionSpec as P


HEADS = 32
KVH = 8
HEAD_SIZE = 128
QBLK = 128

theta_base = 500000.0
neg_fill = -1e30
LOG2E = math.log2(math.e)
STAT_ROWS = 8
SUM_ROWS = 16
PACK_VMEM = 47 << 20


def rotary_tables(rows, first_row):
    half = HEAD_SIZE // 2
    frequency = theta_base ** (-(jnp.arange(half, dtype=jnp.float32) * (2.0 / HEAD_SIZE)))
    places = (first_row + jnp.arange(rows, dtype=jnp.int32)).astype(jnp.float32)
    angles = places[:, None] * frequency[None, :]
    cosine = jnp.cos(angles)
    sine = jnp.sin(angles)
    return (
        jnp.concatenate([cosine, cosine], axis=1),
        jnp.concatenate([-sine, sine], axis=1),
    )


def pack_queries_kernel(order, q_per_kv, group, cos_ref, sin_ref, q_ref, *out_refs):
    own = lax.rem(lax.axis_index("tok"), group)
    rows = q_ref.shape[0]
    cosine = cos_ref[...]
    sine = sin_ref[...]
    for offsets, out_ref in zip(order, out_refs):
        for at, offset in enumerate(offsets):
            head = own ^ offset
            for j in range(q_per_kv):
                start = pl.multiple_of((head * q_per_kv + j) * HEAD_SIZE, HEAD_SIZE)
                x = q_ref[:, pl.ds(start, HEAD_SIZE)].astype(jnp.float32)
                turned = pltpu.roll(x, HEAD_SIZE // 2, 1)
                row = (at * q_per_kv + j) * rows
                out_ref[row : row + rows, :] = (x * cosine + turned * sine).astype(jnp.bfloat16)


def pack_queries(queries, group, order):
    rows = queries.shape[0]
    q_per_kv = HEADS // KVH
    cosine, sine = rotary_tables(rows, lax.axis_index("tok") * rows)
    return pl.pallas_call(
        functools.partial(pack_queries_kernel, order, q_per_kv, group),
        out_shape=[
            jax.ShapeDtypeStruct((len(offsets) * q_per_kv * rows, HEAD_SIZE), jnp.bfloat16)
            for offsets in order
        ],
        name="pack_queries",
        cost_estimate=pl.CostEstimate(
            flops=6 * queries.size, bytes_accessed=4 * queries.size, transcendentals=0
        ),
        compiler_params=pltpu.CompilerParams(vmem_limit_bytes=PACK_VMEM),
    )(cosine, sine, queries)


def pack_cache_kernel(order, group, k_ref, v_ref, *out_refs):
    own = lax.rem(lax.axis_index("tok"), group)
    keys = k_ref.shape[0]
    for offsets, out_ref in zip(order, out_refs):
        for at, offset in enumerate(offsets):
            start = pl.multiple_of((own ^ offset) * HEAD_SIZE, HEAD_SIZE)
            row = 2 * at * keys
            out_ref[row : row + keys, :] = k_ref[:, pl.ds(start, HEAD_SIZE)]
            out_ref[row + keys : row + 2 * keys, :] = v_ref[:, pl.ds(start, HEAD_SIZE)]


def pack_cache(keys, values, group, order):
    return pl.pallas_call(
        functools.partial(pack_cache_kernel, order, group),
        out_shape=[
            jax.ShapeDtypeStruct((len(offsets) * 2 * keys.shape[0], HEAD_SIZE), jnp.bfloat16)
            for offsets in order
        ],
        name="pack_cache",
        cost_estimate=pl.CostEstimate(
            flops=0, bytes_accessed=8 * keys.size, transcendentals=0
        ),
        compiler_params=pltpu.CompilerParams(vmem_limit_bytes=PACK_VMEM),
    )(keys, values)


def mask_kernel(calls, rows, slot_hbm, count_hbm, mask_ref, slot_ref, count_ref, sems):
    server = lax.axis_index("tok")
    group = slot_ref.shape[0]
    own = lax.rem(server, group)
    copies = [
        pltpu.make_async_copy(slot_hbm, slot_ref, sems.at[0]),
        pltpu.make_async_copy(count_hbm, count_ref, sems.at[1]),
    ]
    for copy in copies:
        copy.start()
    for copy in copies:
        copy.wait()
    for call, displacements in enumerate(calls):
        mask = jnp.int32(0)
        for i, displacement in enumerate(displacements):
            block = ((server ^ displacement) * rows) // QBLK
            for k in range(group):
                key_block = server ^ k
                slot = slot_ref[own, block, key_block]
                active = (slot >= 0) & (slot < count_ref[own, key_block])
                mask = mask | (active.astype(jnp.int32) << (i * group + k))
        mask_ref[call] = jnp.full(mask_ref.shape[1:], mask, jnp.int32)


def active_masks(task_slot, task_count, calls, rows):
    hbm = pl.BlockSpec(memory_space=pltpu.HBM)
    return pl.pallas_call(
        functools.partial(mask_kernel, calls, rows),
        out_shape=jax.ShapeDtypeStruct((len(calls), 8, HEAD_SIZE), jnp.int32),
        in_specs=[hbm] * 2,
        scratch_shapes=[
            pltpu.SMEM(task_slot.shape, task_slot.dtype),
            pltpu.SMEM(task_count.shape, task_count.dtype),
            pltpu.SemaphoreType.DMA((2,)),
        ],
        name="masks",
        cost_estimate=pl.CostEstimate(
            flops=0, bytes_accessed=4 * task_slot.size, transcendentals=0
        ),
        compiler_params=pltpu.CompilerParams(vmem_limit_bytes=4 << 20),
    )(task_slot, task_count)


def lay_cache_kernel(laid, *refs):
    *in_refs, _, k_ref, v_ref = refs
    keys = k_ref.shape[1]
    if laid:
        k_ref[:laid] = in_refs[0][...]
        v_ref[:laid] = in_refs[1][...]
        in_refs = in_refs[2:]
    for at, ref in enumerate(in_refs, laid):
        k_ref[at] = ref[:keys, :]
        v_ref[at, :HEAD_SIZE, :] = jnp.transpose(ref[keys:, :].astype(jnp.float32)).astype(
            jnp.bfloat16
        )
        v_ref[at, HEAD_SIZE:, :] = jnp.ones((SUM_ROWS, keys), jnp.bfloat16)


def lay_cache(pieces, after, before=()):
    vmem = pl.BlockSpec(memory_space=pltpu.VMEM)
    laid = before[0].shape[0] if before else 0
    group = laid + len(pieces)
    keys = pieces[0].shape[0] // 2
    return pl.pallas_call(
        functools.partial(lay_cache_kernel, laid),
        out_shape=[
            jax.ShapeDtypeStruct((group, keys, HEAD_SIZE), jnp.bfloat16),
            jax.ShapeDtypeStruct((group, HEAD_SIZE + SUM_ROWS, keys), jnp.bfloat16),
        ],
        in_specs=[vmem] * (len(before) + len(pieces)) + [pl.BlockSpec(memory_space=pl.ANY)],
        name="lay_cache",
        cost_estimate=pl.CostEstimate(
            flops=0, bytes_accessed=8 * group * keys * HEAD_SIZE, transcendentals=0
        ),
        compiler_params=pltpu.CompilerParams(vmem_limit_bytes=8 << 20),
    )(*before, *pieces, after)


def split_stat(stat, width):
    high = stat.astype(jnp.bfloat16).astype(jnp.float32)
    rest = stat - high
    middle = rest.astype(jnp.bfloat16).astype(jnp.float32)
    low = rest - middle
    row = lax.broadcasted_iota(jnp.int32, (STAT_ROWS, width), 0)
    spread = jnp.where(row == 0, high, jnp.where(row == 1, middle, jnp.where(row == 2, low, 0.0)))
    return spread.astype(jnp.bfloat16)


def join_stat(ref):
    stat = ref[HEAD_SIZE : HEAD_SIZE + STAT_ROWS, :].astype(jnp.float32)
    return stat[0:1] + stat[1:2] + stat[2:3]


def attention_kernel(plan, mask_ref, *refs):
    which, offset, widths, slab, group, blocks, resumed, ended = plan
    n_chunks = sum(widths)
    n_in = len(widths)
    q_in_refs = refs[:n_in]
    k_ref, v_ref, _ = refs[n_in : n_in + 3]
    at = n_in + 3
    before_refs = refs[at : at + resumed]
    at += resumed
    n_out = n_chunks if ended else 2
    out_refs = refs[at : at + n_out]
    at += n_out
    if ended:
        m_ref, acc_ref = refs[at : at + 2]
        at += 2
    else:
        m_ref, acc_ref = out_refs
    list_ref, q_ref, *slots = refs[at:]
    width = q_ref.shape[1]
    scale = HEAD_SIZE ** (-0.5) * LOG2E

    mask = mask_ref[which, 0, 0]
    found = jnp.int32(0)
    for i in range(n_chunks):
        for k in blocks:
            entry = i * group + k
            list_ref[found] = entry
            found = found + ((mask >> (offset * group + entry)) & 1)

    at = 0
    for q_in_ref, n in zip(q_in_refs, widths):
        for i in range(n):
            q_ref[at + i] = q_in_ref[i * width : (i + 1) * width, :]
        at += n
    if resumed:
        at = 0
        for m_before, acc_before in zip(before_refs[::2], before_refs[1::2]):
            n = m_before.shape[0]
            m_ref[at : at + n] = m_before[...]
            acc_ref[at : at + n] = acc_before[...]
            at += n
    else:
        m_ref[...] = jnp.full_like(m_ref, neg_fill)
        acc_ref[...] = jnp.zeros_like(acc_ref)

    def pair(i):
        entry = list_ref[i]
        return entry // group, lax.rem(entry, group)

    def score(i, slot, slabs=range(0, width, slab)):
        chunk, k = pair(i)
        s_ref, top_ref, fade_ref = slot
        for c in slabs:
            scores = lax.dot_general(
                k_ref[k],
                q_ref[chunk, c : c + slab, :],
                (((1,), (1,)), ((), ())),
                preferred_element_type=jnp.float32,
            )
            s_ref[:, c : c + slab] = scores
            old = m_ref[chunk, :, c : c + slab]
            new = jnp.maximum(old, jnp.max(scores, axis=0, keepdims=True))
            m_ref[chunk, :, c : c + slab] = new
            top_ref[:, c : c + slab] = new
            fade_ref[:, c : c + slab] = jnp.exp2((old - new) * scale)

    def weigh(i, slot, slabs=range(0, width, slab)):
        chunk, k = pair(i)
        s_ref, top_ref, fade_ref = slot
        for c in slabs:
            p = jnp.exp2((s_ref[:, c : c + slab] - top_ref[0:1, c : c + slab]) * scale)
            product = jnp.dot(
                v_ref[k], p.astype(jnp.bfloat16), preferred_element_type=jnp.float32
            )
            acc_ref[chunk, :, c : c + slab] = (
                acc_ref[chunk, :, c : c + slab] * fade_ref[0:1, c : c + slab] + product
            )

    even, odd = slots[:3], slots[3:]

    @pl.when(found > 0)
    def _():
        score(0, even)

    def step(i, here, there):
        @pl.when(i + 1 < found)
        def _():
            for c in range(0, width, slab):
                score(i + 1, there, (c,))
                weigh(i, here, (c,))

        @pl.when(i + 1 == found)
        def _():
            weigh(i, here)

    def two(j, carry):
        step(2 * j, even, odd)
        step(2 * j + 1, odd, even)
        return carry

    lax.fori_loop(0, (found + 1) // 2, two, 0)

    if not ended:
        return
    for i in range(n_chunks):
        total = acc_ref[i, HEAD_SIZE : HEAD_SIZE + 1, :]
        seen = total > 0.0
        safe = jnp.where(seen, total, 1.0)
        stat = jnp.where(seen, m_ref[i, 0:1, :] * scale + jnp.log2(safe), neg_fill)
        out_refs[i][:HEAD_SIZE, :] = (acc_ref[i, :HEAD_SIZE, :] * (1.0 / safe)).astype(jnp.bfloat16)
        out_refs[i][HEAD_SIZE:, :] = split_stat(stat, width)


def attention(
    chunks, which, cache, masks, width, after, group, blocks, offset=0, before=(), ended=True
):
    k, v = cache
    keys = k.shape[1]
    widths = tuple(chunk.shape[0] // width for chunk in chunks)
    n = sum(widths)
    vmem = pl.BlockSpec(memory_space=pltpu.VMEM)
    state = [(n, 8, width), (n, HEAD_SIZE + SUM_ROWS, width)]
    slot = [
        pltpu.VMEM((keys, width), jnp.float32),
        pltpu.VMEM((8, width), jnp.float32),
        pltpu.VMEM((8, width), jnp.float32),
    ]
    if ended:
        out_shape = [jax.ShapeDtypeStruct((HEAD_SIZE + STAT_ROWS, width), jnp.bfloat16)] * n
        scratch = [pltpu.VMEM(shape, jnp.float32) for shape in state]
    else:
        out_shape = [jax.ShapeDtypeStruct(shape, jnp.float32) for shape in state]
        scratch = []
    pairs = n * len(blocks)
    plan = (which, offset, widths, min(256, width), group, tuple(blocks), len(before), ended)
    return pl.pallas_call(
        functools.partial(attention_kernel, plan),
        out_shape=out_shape,
        in_specs=[vmem] * (len(chunks) + 3)
        + [pl.BlockSpec(memory_space=pl.ANY)]
        + [vmem] * len(before),
        out_specs=[vmem] * len(out_shape),
        scratch_shapes=scratch
        + [
            pltpu.SMEM((pairs + 1,), jnp.int32),
            pltpu.VMEM((n, width, HEAD_SIZE), jnp.bfloat16),
        ]
        + slot
        + slot,
        name="attention",
        cost_estimate=pl.CostEstimate(
            flops=4 * pairs * keys * width * HEAD_SIZE,
            bytes_accessed=4 * n * width * HEAD_SIZE + 4 * len(blocks) * keys * HEAD_SIZE,
            transcendentals=pairs * keys * width,
        ),
        compiler_params=pltpu.CompilerParams(vmem_limit_bytes=20 << 20),
    )(masks, *chunks, k, v, after, *before)


def merge_kernel(n_in, keep_stat, *refs):
    in_refs, out_refs = refs[:n_in], refs[n_in + 1 :]
    stats = [join_stat(ref) for ref in in_refs]
    largest = functools.reduce(jnp.maximum, stats)
    weights = [jnp.exp2(stat - largest) for stat in stats]
    total = functools.reduce(jnp.add, weights)
    inverse = 1.0 / total
    value = functools.reduce(
        jnp.add,
        [
            (weight * inverse) * ref[:HEAD_SIZE, :].astype(jnp.float32)
            for weight, ref in zip(weights, in_refs)
        ],
    ).astype(jnp.bfloat16)
    stat = largest + jnp.log2(total)
    part = out_refs[0].shape[1]
    for i, out_ref in enumerate(out_refs):
        span = slice(i * part, (i + 1) * part)
        out_ref[:HEAD_SIZE, :] = value[:, span]
        if keep_stat:
            out_ref[HEAD_SIZE:, :] = split_stat(stat[:, span], part)


def merge(messages, parts, keep_stat=True, after=None):
    vmem = pl.BlockSpec(memory_space=pltpu.VMEM)
    after = messages[0] if after is None else after
    height, width = messages[0].shape
    height = height if keep_stat else HEAD_SIZE
    size = len(messages) * height * width
    return pl.pallas_call(
        functools.partial(merge_kernel, len(messages), keep_stat),
        out_shape=[jax.ShapeDtypeStruct((height, width // parts), jnp.bfloat16)] * parts,
        in_specs=[vmem] * len(messages) + [pl.BlockSpec(memory_space=pl.ANY)],
        name="merge" if keep_stat else "finish",
        cost_estimate=pl.CostEstimate(flops=4 * size, bytes_accessed=4 * size, transcendentals=0),
        compiler_params=pltpu.CompilerParams(vmem_limit_bytes=8 << 20),
    )(*messages, after)


def gather_kernel(rows, *refs):
    *piece_refs, out_ref = refs
    core = lax.rem(lax.axis_index("tok"), len(piece_refs))
    per = piece_refs[0].shape[1] // rows
    for offset, piece_ref in enumerate(piece_refs):
        for j in range(per):
            block = jnp.transpose(piece_ref[:, j * rows : (j + 1) * rows].astype(jnp.float32))
            start = pl.multiple_of(((core ^ offset) * per + j) * HEAD_SIZE, HEAD_SIZE)
            out_ref[:, pl.ds(start, HEAD_SIZE)] = block.astype(jnp.bfloat16)


def gather(pieces, rows):
    width = sum(piece.shape[1] for piece in pieces) // rows * HEAD_SIZE
    return pl.pallas_call(
        functools.partial(gather_kernel, rows),
        out_shape=jax.ShapeDtypeStruct((rows, width), jnp.bfloat16),
        name="gather",
        cost_estimate=pl.CostEstimate(
            flops=0, bytes_accessed=4 * rows * width, transcendentals=0
        ),
        compiler_params=pltpu.CompilerParams(vmem_limit_bytes=4 << 20),
    )(*pieces)


def project_kernel(plan, left_ref, w_ref, *refs):
    half, start, away = plan
    out_ref = refs[-1]
    columns = out_ref.shape[1]
    depth = left_ref.shape[1]
    base_start = start
    if half is not None:
        start = (lax.axis_index("head") ^ half) * (w_ref.shape[1] // 2) + start
    start = pl.multiple_of(start, HEAD_SIZE)
    row = 0
    if depth < w_ref.shape[0]:
        group = w_ref.shape[0] // depth * 2
        row = pl.multiple_of((lax.rem(lax.axis_index("tok"), group) // 2 ^ away) * depth, depth)
    total = jnp.dot(
        left_ref[...],
        w_ref[pl.ds(row, depth), pl.ds(start, columns)],
        preferred_element_type=jnp.float32,
    )
    if len(refs) == 2:
        total = total + refs[0][:, base_start : base_start + columns]
    out_ref[...] = total.astype(out_ref.dtype)


def project(left, out_weight, half, start, columns, kind, away=0, base=None):
    rows, depth = left.shape
    operands = (left, out_weight) if base is None else (left, out_weight, base)
    return pl.pallas_call(
        functools.partial(project_kernel, (half, start, away)),
        out_shape=jax.ShapeDtypeStruct((rows, columns), kind),
        in_specs=[pl.BlockSpec(memory_space=pltpu.VMEM)] * len(operands),
        out_specs=pl.BlockSpec(memory_space=pltpu.VMEM),
        name="project",
        cost_estimate=pl.CostEstimate(
            flops=2 * rows * depth * columns,
            bytes_accessed=2 * depth * columns,
            transcendentals=0,
        ),
        compiler_params=pltpu.CompilerParams(vmem_limit_bytes=24 << 20),
    )(*operands)


def swap(x, bits, servers):
    return lax.ppermute(x, "tok", [(i, i ^ bits) for i in range(servers)])


def attend_grouped(queries, keys, values, out_weight, task_slot, task_count, move):
    core, column, near, far = 1, 2, 4, 8
    rows = queries.shape[0]
    q_per_kv = HEADS // KVH
    part = q_per_kv * rows
    width = 2 * part

    keep, give = pack_queries(queries, 4, ((0, 2), (1, 3)))
    pieces = pack_cache(keys, values, 4, ((0,), (core,), (column,), (column | core,)))
    got = move(give, core)
    own = jnp.concatenate([keep[:part], got[:part]], axis=0)
    other = move(jnp.concatenate([keep[part:], got[part:]], axis=0), column)
    across = move(pieces[2], column)
    beyond = move(pieces[3], column | core)
    own_far = move(own, far)
    beside = move(pieces[1], core)
    other_far = move(other, far)
    own_near = move(own, near)
    other_near = move(other, near)
    own_last = move(own_far, near)
    other_last = move(other_far, near)

    calls = (
        (0, column, near, far, near | column, far | column),
        (far | near,),
        (far | near | column,),
    )
    masks = active_masks(task_slot, task_count, calls, rows)
    chip_cache = lay_cache([pieces[0], beside], masks)

    def first(chunks, offset, after):
        return attention(
            chunks, 0, chip_cache, masks, width, after, 4, (0, core), offset, ended=False
        )

    def call(chunks, which, after):
        return attention(chunks, which, cache, masks, width, after, 4, range(4))

    chunks = [own, other, own_near, own_far, other_near, other_far]
    a_state = first(chunks[:4], 0, masks)
    b_state = first(chunks[4:], 4, a_state[0])
    cache = lay_cache([across, beyond], b_state[0], chip_cache)
    own_a, own_b, near_a, far_a, near_b, far_b = attention(
        chunks,
        0,
        cache,
        masks,
        width,
        b_state[0],
        4,
        (column, column | core),
        before=(*a_state, *b_state),
    )
    (last_a,) = call([own_last], 1, far_b)
    (last_b,) = call([other_last], 2, last_a)

    far_b = move(far_b, far | column)
    last_a = move(last_a, near)
    last_b = move(last_b, far | near | column)
    near_b = move(near_b, near | column)
    near_a = move(near_a, near)
    own_b = move(own_b, column)
    (far_a,) = merge([far_a, last_a], 1)
    far_a = move(far_a, far)
    b_own, b_other = merge([own_b, near_b, far_b, last_b], 2, False)
    b_other = move(b_other, core)
    left_b = gather([b_own, b_other], rows)
    columns = out_weight.shape[1] // 2
    base = project(left_b, out_weight, 1, 0, columns, jnp.float32, away=1)
    a_own, a_other = merge([own_a, near_a, far_a], 2, False, after=base)
    a_other = move(a_other, core)
    left_a = gather([a_own, a_other], rows)

    cuts = (0, columns // 4, columns)
    arrived = []
    for start, end in zip(cuts, cuts[1:]):
        part = project(left_a, out_weight, 1, start, end - start, jnp.bfloat16, base=base)
        arrived.append(lax.ppermute(part, "head", [(0, 1), (1, 0)]))
    here = project(left_b, out_weight, 0, 0, columns, jnp.float32, away=1)
    here = project(left_a, out_weight, 0, 0, columns, jnp.float32, base=here)
    return (here + jnp.concatenate(arrived, axis=1).astype(jnp.float32)).astype(jnp.bfloat16)


def attend_general(queries, keys, values, task_slot, task_count, move, servers):
    assert task_slot.shape[0] == 1
    rows = queries.shape[0]
    width = HEADS // KVH * rows
    step = min(4, servers)
    calls = tuple(tuple(range(i, i + step)) for i in range(0, servers, step))
    (own,) = pack_queries(queries, 1, ((0,),))
    masks = active_masks(task_slot, task_count, calls, rows)
    cache = lay_cache(pack_cache(keys, values, 1, ((0,),)), masks)
    held = {0: own}
    bit = servers // 2
    while bit:
        held.update({d ^ bit: move(chunk, bit) for d, chunk in held.items()})
        bit //= 2
    partial = {}
    for which, call in enumerate(calls):
        result = attention(
            [held[d] for d in call], which, cache, masks, width, masks, 1, range(1)
        )
        for j, d in enumerate(call):
            partial[d] = [result[j]]
    bit = 1
    while bit < servers:
        for d in sorted(partial, reverse=True):
            if d & bit:
                messages = partial.pop(d)
                message = messages[0] if len(messages) == 1 else merge(messages, 1)[0]
                partial[d ^ bit].append(move(message, bit))
        bit *= 2
    return merge(partial[0], 1, False)


def on_device(queries, keys, values, out_weight, task_slot, task_count):
    servers = lax.axis_size("tok")
    heads = lax.axis_size("head")
    rows = queries.shape[0]
    group = task_slot.shape[0]
    move = functools.partial(swap, servers=servers)
    if group == 4 and servers == 16 and heads == 2:
        return attend_grouped(
            queries, keys, values, out_weight, task_slot, task_count, move
        )
    attended = attend_general(queries, keys, values, task_slot, task_count, move, servers)
    left = gather(attended, rows)
    share = project(left, out_weight, None, 0, out_weight.shape[1], jnp.bfloat16)
    return lax.psum_scatter(share, "head", scatter_dimension=1, tiled=True)


def solution(mesh):
    placed = (
        P("tok", "head"),
        P("tok", "head"),
        P("tok", "head"),
        P("head", None),
        P("head", None, None),
        P("head", None),
    )
    return jax.shard_map(
        on_device, mesh=mesh, in_specs=placed, out_specs=P("tok", "head"), check_vma=False
    )
```

```python
import functools
import math

import jax
import jax.numpy as jnp
from jax import lax
from jax.experimental import pallas as pl
from jax.experimental.pallas import tpu as pltpu
from jax.sharding import PartitionSpec as P


HEADS = 32
KVH = 8
HEAD_SIZE = 128
QBLK = 128

theta_base = 500000.0
neg_fill = -1e30
LOG2E = math.log2(math.e)
STAT_ROWS = 8
SUM_ROWS = 16
PACK_VMEM = 47 << 20


def rotary_tables(rows, first_row):
    half = HEAD_SIZE // 2
    lane = jnp.arange(HEAD_SIZE, dtype=jnp.int32)
    pair = (lane % half).astype(jnp.float32)
    frequency = theta_base ** (-(pair * (2.0 / HEAD_SIZE)))
    places = (first_row + jnp.arange(rows, dtype=jnp.int32)).astype(jnp.float32)
    angles = places[:, None] * frequency[None, :]
    sine = jnp.sin(angles)
    return jnp.cos(angles), jnp.where(lane[None, :] < half, -sine, sine)


def pack_queries_kernel(order, q_per_kv, group, cos_ref, sin_ref, q_ref, *out_refs):
    own = lax.rem(lax.axis_index("tok"), group)
    rows = q_ref.shape[0]
    cosine = cos_ref[...]
    sine = sin_ref[...]
    for offsets, out_ref in zip(order, out_refs):
        for at, offset in enumerate(offsets):
            head = own ^ offset
            for j in range(q_per_kv):
                start = pl.multiple_of((head * q_per_kv + j) * HEAD_SIZE, HEAD_SIZE)
                x = q_ref[:, pl.ds(start, HEAD_SIZE)].astype(jnp.float32)
                turned = pltpu.roll(x, HEAD_SIZE // 2, 1)
                row = (at * q_per_kv + j) * rows
                out_ref[row : row + rows, :] = (x * cosine + turned * sine).astype(jnp.bfloat16)


def pack_queries(queries, group, order):
    rows = queries.shape[0]
    q_per_kv = HEADS // KVH
    cosine, sine = rotary_tables(rows, lax.axis_index("tok") * rows)
    return pl.pallas_call(
        functools.partial(pack_queries_kernel, order, q_per_kv, group),
        out_shape=[
            jax.ShapeDtypeStruct((len(offsets) * q_per_kv * rows, HEAD_SIZE), jnp.bfloat16)
            for offsets in order
        ],
        name="pack_queries",
        cost_estimate=pl.CostEstimate(
            flops=6 * queries.size, bytes_accessed=4 * queries.size, transcendentals=0
        ),
        compiler_params=pltpu.CompilerParams(vmem_limit_bytes=PACK_VMEM),
    )(cosine, sine, queries)


def pack_cache_kernel(order, group, k_ref, v_ref, *out_refs):
    own = lax.rem(lax.axis_index("tok"), group)
    keys = k_ref.shape[0]
    for offsets, out_ref in zip(order, out_refs):
        for at, offset in enumerate(offsets):
            start = pl.multiple_of((own ^ offset) * HEAD_SIZE, HEAD_SIZE)
            row = 2 * at * keys
            out_ref[row : row + keys, :] = k_ref[:, pl.ds(start, HEAD_SIZE)]
            out_ref[row + keys : row + 2 * keys, :] = v_ref[:, pl.ds(start, HEAD_SIZE)]


def pack_cache(keys, values, group, order):
    return pl.pallas_call(
        functools.partial(pack_cache_kernel, order, group),
        out_shape=[
            jax.ShapeDtypeStruct((len(offsets) * 2 * keys.shape[0], HEAD_SIZE), jnp.bfloat16)
            for offsets in order
        ],
        name="pack_cache",
        cost_estimate=pl.CostEstimate(
            flops=0, bytes_accessed=8 * keys.size, transcendentals=0
        ),
        compiler_params=pltpu.CompilerParams(vmem_limit_bytes=PACK_VMEM),
    )(keys, values)


def mask_kernel(calls, rows, slot_hbm, count_hbm, mask_ref, slot_ref, count_ref, sems):
    server = lax.axis_index("tok")
    group = slot_ref.shape[0]
    own = lax.rem(server, group)
    copies = [
        pltpu.make_async_copy(slot_hbm, slot_ref, sems.at[0]),
        pltpu.make_async_copy(count_hbm, count_ref, sems.at[1]),
    ]
    for copy in copies:
        copy.start()
    for copy in copies:
        copy.wait()
    for call, displacements in enumerate(calls):
        mask = jnp.int32(0)
        for i, displacement in enumerate(displacements):
            block = ((server ^ displacement) * rows) // QBLK
            for k in range(group):
                key_block = server ^ k
                slot = slot_ref[own, block, key_block]
                active = (slot >= 0) & (slot < count_ref[own, key_block])
                mask = mask | (active.astype(jnp.int32) << (i * group + k))
        mask_ref[call] = jnp.full(mask_ref.shape[1:], mask, jnp.int32)


def active_masks(task_slot, task_count, calls, rows):
    hbm = pl.BlockSpec(memory_space=pltpu.HBM)
    return pl.pallas_call(
        functools.partial(mask_kernel, calls, rows),
        out_shape=jax.ShapeDtypeStruct((len(calls), 8, HEAD_SIZE), jnp.int32),
        in_specs=[hbm] * 2,
        scratch_shapes=[
            pltpu.SMEM(task_slot.shape, task_slot.dtype),
            pltpu.SMEM(task_count.shape, task_count.dtype),
            pltpu.SemaphoreType.DMA((2,)),
        ],
        name="masks",
        cost_estimate=pl.CostEstimate(
            flops=0, bytes_accessed=4 * task_slot.size, transcendentals=0
        ),
        compiler_params=pltpu.CompilerParams(vmem_limit_bytes=4 << 20),
    )(task_slot, task_count)


def lay_cache_kernel(laid, *refs):
    *in_refs, _, k_ref, v_ref = refs
    keys = k_ref.shape[1]
    if laid:
        k_ref[:laid] = in_refs[0][...]
        v_ref[:laid] = in_refs[1][...]
        in_refs = in_refs[2:]
    for at, ref in enumerate(in_refs, laid):
        k_ref[at] = ref[:keys, :]
        v_ref[at, :HEAD_SIZE, :] = jnp.transpose(ref[keys:, :].astype(jnp.float32)).astype(
            jnp.bfloat16
        )
        v_ref[at, HEAD_SIZE:, :] = jnp.ones((SUM_ROWS, keys), jnp.bfloat16)


def lay_cache(pieces, after, before=()):
    vmem = pl.BlockSpec(memory_space=pltpu.VMEM)
    laid = before[0].shape[0] if before else 0
    group = laid + len(pieces)
    keys = pieces[0].shape[0] // 2
    return pl.pallas_call(
        functools.partial(lay_cache_kernel, laid),
        out_shape=[
            jax.ShapeDtypeStruct((group, keys, HEAD_SIZE), jnp.bfloat16),
            jax.ShapeDtypeStruct((group, HEAD_SIZE + SUM_ROWS, keys), jnp.bfloat16),
        ],
        in_specs=[vmem] * (len(before) + len(pieces)) + [pl.BlockSpec(memory_space=pl.ANY)],
        name="lay_cache",
        cost_estimate=pl.CostEstimate(
            flops=0, bytes_accessed=8 * group * keys * HEAD_SIZE, transcendentals=0
        ),
        compiler_params=pltpu.CompilerParams(vmem_limit_bytes=8 << 20),
    )(*before, *pieces, after)


def split_stat(stat, width):
    high = stat.astype(jnp.bfloat16).astype(jnp.float32)
    rest = stat - high
    middle = rest.astype(jnp.bfloat16).astype(jnp.float32)
    low = rest - middle
    row = lax.broadcasted_iota(jnp.int32, (STAT_ROWS, width), 0)
    spread = jnp.where(row == 0, high, jnp.where(row == 1, middle, jnp.where(row == 2, low, 0.0)))
    return spread.astype(jnp.bfloat16)


def join_stat(ref):
    stat = ref[HEAD_SIZE : HEAD_SIZE + STAT_ROWS, :].astype(jnp.float32)
    return stat[0:1] + stat[1:2] + stat[2:3]


def attention_kernel(plan, mask_ref, *refs):
    which, offset, widths, slab, group, blocks, resumed, ended = plan
    n_chunks = sum(widths)
    n_in = len(widths)
    q_in_refs = refs[:n_in]
    k_ref, v_ref, _ = refs[n_in : n_in + 3]
    at = n_in + 3
    before_refs = refs[at : at + resumed]
    at += resumed
    n_out = n_chunks if ended else 2
    out_refs = refs[at : at + n_out]
    at += n_out
    if ended:
        m_ref, acc_ref = refs[at : at + 2]
        at += 2
    else:
        m_ref, acc_ref = out_refs
    list_ref, q_ref, *slots = refs[at:]
    width = q_ref.shape[1]
    scale = HEAD_SIZE ** (-0.5) * LOG2E

    mask = mask_ref[which, 0, 0]
    found = jnp.int32(0)
    for i in range(n_chunks):
        for k in blocks:
            entry = i * group + k
            list_ref[found] = entry
            found = found + ((mask >> (offset * group + entry)) & 1)

    at = 0
    for q_in_ref, n in zip(q_in_refs, widths):
        for i in range(n):
            q_ref[at + i] = q_in_ref[i * width : (i + 1) * width, :]
        at += n
    if resumed:
        at = 0
        for m_before, acc_before in zip(before_refs[::2], before_refs[1::2]):
            n = m_before.shape[0]
            m_ref[at : at + n] = m_before[...]
            acc_ref[at : at + n] = acc_before[...]
            at += n
    else:
        m_ref[...] = jnp.full_like(m_ref, neg_fill)
        acc_ref[...] = jnp.zeros_like(acc_ref)

    def pair(i):
        entry = list_ref[i]
        return entry // group, lax.rem(entry, group)

    def score(i, slot, slabs=range(0, width, slab)):
        chunk, k = pair(i)
        s_ref, top_ref, fade_ref = slot
        for c in slabs:
            scores = lax.dot_general(
                k_ref[k],
                q_ref[chunk, c : c + slab, :],
                (((1,), (1,)), ((), ())),
                preferred_element_type=jnp.float32,
            )
            s_ref[:, c : c + slab] = scores
            old = m_ref[chunk, :, c : c + slab]
            new = jnp.maximum(old, jnp.max(scores, axis=0, keepdims=True))
            m_ref[chunk, :, c : c + slab] = new
            top_ref[:, c : c + slab] = new
            fade_ref[:, c : c + slab] = jnp.exp2((old - new) * scale)

    def weigh(i, slot, slabs=range(0, width, slab)):
        chunk, k = pair(i)
        s_ref, top_ref, fade_ref = slot
        for c in slabs:
            p = jnp.exp2((s_ref[:, c : c + slab] - top_ref[0:1, c : c + slab]) * scale)
            product = jnp.dot(
                v_ref[k], p.astype(jnp.bfloat16), preferred_element_type=jnp.float32
            )
            acc_ref[chunk, :, c : c + slab] = (
                acc_ref[chunk, :, c : c + slab] * fade_ref[0:1, c : c + slab] + product
            )

    even, odd = slots[:3], slots[3:]

    @pl.when(found > 0)
    def _():
        score(0, even)

    def step(i, here, there):
        @pl.when(i + 1 < found)
        def _():
            for c in range(0, width, slab):
                score(i + 1, there, (c,))
                weigh(i, here, (c,))

        @pl.when(i + 1 == found)
        def _():
            weigh(i, here)

    def two(j, carry):
        step(2 * j, even, odd)
        step(2 * j + 1, odd, even)
        return carry

    lax.fori_loop(0, (found + 1) // 2, two, 0)

    if not ended:
        return
    for i in range(n_chunks):
        total = acc_ref[i, HEAD_SIZE : HEAD_SIZE + 1, :]
        seen = total > 0.0
        safe = jnp.where(seen, total, 1.0)
        stat = jnp.where(seen, m_ref[i, 0:1, :] * scale + jnp.log2(safe), neg_fill)
        out_refs[i][:HEAD_SIZE, :] = (acc_ref[i, :HEAD_SIZE, :] * (1.0 / safe)).astype(jnp.bfloat16)
        out_refs[i][HEAD_SIZE:, :] = split_stat(stat, width)


def attention(
    chunks, which, cache, masks, width, after, group, blocks, offset=0, before=(), ended=True
):
    k, v = cache
    keys = k.shape[1]
    widths = tuple(chunk.shape[0] // width for chunk in chunks)
    n = sum(widths)
    vmem = pl.BlockSpec(memory_space=pltpu.VMEM)
    state = [(n, 8, width), (n, HEAD_SIZE + SUM_ROWS, width)]
    slot = [
        pltpu.VMEM((keys, width), jnp.float32),
        pltpu.VMEM((8, width), jnp.float32),
        pltpu.VMEM((8, width), jnp.float32),
    ]
    if ended:
        out_shape = [jax.ShapeDtypeStruct((HEAD_SIZE + STAT_ROWS, width), jnp.bfloat16)] * n
        scratch = [pltpu.VMEM(shape, jnp.float32) for shape in state]
    else:
        out_shape = [jax.ShapeDtypeStruct(shape, jnp.float32) for shape in state]
        scratch = []
    pairs = n * len(blocks)
    plan = (which, offset, widths, min(256, width), group, tuple(blocks), len(before), ended)
    return pl.pallas_call(
        functools.partial(attention_kernel, plan),
        out_shape=out_shape,
        in_specs=[vmem] * (len(chunks) + 3)
        + [pl.BlockSpec(memory_space=pl.ANY)]
        + [vmem] * len(before),
        out_specs=[vmem] * len(out_shape),
        scratch_shapes=scratch
        + [
            pltpu.SMEM((pairs + 1,), jnp.int32),
            pltpu.VMEM((n, width, HEAD_SIZE), jnp.bfloat16),
        ]
        + slot
        + slot,
        name="attention",
        cost_estimate=pl.CostEstimate(
            flops=4 * pairs * keys * width * HEAD_SIZE,
            bytes_accessed=4 * n * width * HEAD_SIZE + 4 * len(blocks) * keys * HEAD_SIZE,
            transcendentals=pairs * keys * width,
        ),
        compiler_params=pltpu.CompilerParams(vmem_limit_bytes=20 << 20),
    )(masks, *chunks, k, v, after, *before)


def merge_kernel(n_in, keep_stat, *refs):
    in_refs, out_refs = refs[:n_in], refs[n_in + 1 :]
    stats = [join_stat(ref) for ref in in_refs]
    largest = functools.reduce(jnp.maximum, stats)
    weights = [jnp.exp2(stat - largest) for stat in stats]
    total = functools.reduce(jnp.add, weights)
    inverse = 1.0 / total
    value = functools.reduce(
        jnp.add,
        [
            (weight * inverse) * ref[:HEAD_SIZE, :].astype(jnp.float32)
            for weight, ref in zip(weights, in_refs)
        ],
    ).astype(jnp.bfloat16)
    stat = largest + jnp.log2(total)
    part = out_refs[0].shape[1]
    for i, out_ref in enumerate(out_refs):
        span = slice(i * part, (i + 1) * part)
        out_ref[:HEAD_SIZE, :] = value[:, span]
        if keep_stat:
            out_ref[HEAD_SIZE:, :] = split_stat(stat[:, span], part)


def merge(messages, parts, keep_stat=True, after=None):
    vmem = pl.BlockSpec(memory_space=pltpu.VMEM)
    after = messages[0] if after is None else after
    height, width = messages[0].shape
    height = height if keep_stat else HEAD_SIZE
    size = len(messages) * height * width
    return pl.pallas_call(
        functools.partial(merge_kernel, len(messages), keep_stat),
        out_shape=[jax.ShapeDtypeStruct((height, width // parts), jnp.bfloat16)] * parts,
        in_specs=[vmem] * len(messages) + [pl.BlockSpec(memory_space=pl.ANY)],
        name="merge" if keep_stat else "finish",
        cost_estimate=pl.CostEstimate(flops=4 * size, bytes_accessed=4 * size, transcendentals=0),
        compiler_params=pltpu.CompilerParams(vmem_limit_bytes=8 << 20),
    )(*messages, after)


def gather_kernel(rows, *refs):
    *piece_refs, out_ref = refs
    core = lax.rem(lax.axis_index("tok"), len(piece_refs))
    per = piece_refs[0].shape[1] // rows
    for offset, piece_ref in enumerate(piece_refs):
        for j in range(per):
            block = jnp.transpose(piece_ref[:, j * rows : (j + 1) * rows].astype(jnp.float32))
            start = pl.multiple_of(((core ^ offset) * per + j) * HEAD_SIZE, HEAD_SIZE)
            out_ref[:, pl.ds(start, HEAD_SIZE)] = block.astype(jnp.bfloat16)


def gather(pieces, rows):
    width = sum(piece.shape[1] for piece in pieces) // rows * HEAD_SIZE
    return pl.pallas_call(
        functools.partial(gather_kernel, rows),
        out_shape=jax.ShapeDtypeStruct((rows, width), jnp.bfloat16),
        name="gather",
        cost_estimate=pl.CostEstimate(
            flops=0, bytes_accessed=4 * rows * width, transcendentals=0
        ),
        compiler_params=pltpu.CompilerParams(vmem_limit_bytes=4 << 20),
    )(*pieces)


def project_kernel(plan, left_ref, w_ref, *refs):
    half, start, away = plan
    out_ref = refs[-1]
    columns = out_ref.shape[1]
    depth = left_ref.shape[1]
    base_start = start
    if half is not None:
        start = (lax.axis_index("head") ^ half) * (w_ref.shape[1] // 2) + start
    start = pl.multiple_of(start, HEAD_SIZE)
    row = 0
    if depth < w_ref.shape[0]:
        group = w_ref.shape[0] // depth * 2
        row = pl.multiple_of((lax.rem(lax.axis_index("tok"), group) // 2 ^ away) * depth, depth)
    total = jnp.dot(
        left_ref[...],
        w_ref[pl.ds(row, depth), pl.ds(start, columns)],
        preferred_element_type=jnp.float32,
    )
    if len(refs) == 2:
        total = total + refs[0][:, base_start : base_start + columns]
    out_ref[...] = total.astype(out_ref.dtype)


def project(left, out_weight, half, start, columns, kind, away=0, base=None):
    rows, depth = left.shape
    operands = (left, out_weight) if base is None else (left, out_weight, base)
    return pl.pallas_call(
        functools.partial(project_kernel, (half, start, away)),
        out_shape=jax.ShapeDtypeStruct((rows, columns), kind),
        in_specs=[pl.BlockSpec(memory_space=pltpu.VMEM)] * len(operands),
        out_specs=pl.BlockSpec(memory_space=pltpu.VMEM),
        name="project",
        cost_estimate=pl.CostEstimate(
            flops=2 * rows * depth * columns,
            bytes_accessed=2 * depth * columns,
            transcendentals=0,
        ),
        compiler_params=pltpu.CompilerParams(vmem_limit_bytes=24 << 20),
    )(*operands)


def swap(x, bits, servers):
    return lax.ppermute(x, "tok", [(i, i ^ bits) for i in range(servers)])


def attend_grouped(queries, keys, values, out_weight, task_slot, task_count, move):
    core, column, near, far = 1, 2, 4, 8
    rows = queries.shape[0]
    q_per_kv = HEADS // KVH
    part = q_per_kv * rows
    width = 2 * part

    keep, give = pack_queries(queries, 4, ((0, 2), (1, 3)))
    pieces = pack_cache(keys, values, 4, ((0,), (core,), (column,), (column | core,)))
    got = move(give, core)
    own = jnp.concatenate([keep[:part], got[:part]], axis=0)
    other = move(jnp.concatenate([keep[part:], got[part:]], axis=0), column)
    across = move(pieces[2], column)
    beyond = move(pieces[3], column | core)
    own_far = move(own, far)
    beside = move(pieces[1], core)
    other_far = move(other, far)
    own_near = move(own, near)
    other_near = move(other, near)
    own_last = move(own_far, near)
    other_last = move(other_far, near)

    calls = (
        (0, column, near, far, near | column, far | column),
        (far | near,),
        (far | near | column,),
    )
    masks = active_masks(task_slot, task_count, calls, rows)
    chip_cache = lay_cache([pieces[0], beside], masks)

    def first(chunks, offset, after):
        return attention(
            chunks, 0, chip_cache, masks, width, after, 4, (0, core), offset, ended=False
        )

    def call(chunks, which, after):
        return attention(chunks, which, cache, masks, width, after, 4, range(4))

    chunks = [own, other, own_near, own_far, other_near, other_far]
    own_state = first(chunks[:2], 0, masks)
    a_state = first(chunks[2:4], 2, own_state[0])
    b_state = first(chunks[4:], 4, a_state[0])
    cache = lay_cache([across, beyond], b_state[0], chip_cache)
    own_a, own_b, near_a, far_a, near_b, far_b = attention(
        chunks,
        0,
        cache,
        masks,
        width,
        b_state[0],
        4,
        (column, column | core),
        before=(*own_state, *a_state, *b_state),
    )
    (last_a,) = call([own_last], 1, far_b)
    (last_b,) = call([other_last], 2, last_a)

    far_b = move(far_b, far | column)
    last_a = move(last_a, near)
    last_b = move(last_b, far | near | column)
    near_b = move(near_b, near | column)
    near_a = move(near_a, near)
    own_b = move(own_b, column)
    (far_a,) = merge([far_a, last_a], 1)
    far_a = move(far_a, far)
    b_own, b_other = merge([own_b, near_b, far_b, last_b], 2, False)
    b_other = move(b_other, core)
    left_b = gather([b_own, b_other], rows)
    columns = out_weight.shape[1] // 2
    base = project(left_b, out_weight, 1, 0, columns, jnp.float32, away=1)
    a_own, a_other = merge([own_a, near_a, far_a], 2, False, after=base)
    a_other = move(a_other, core)
    left_a = gather([a_own, a_other], rows)

    piece = columns // 2
    arrived = []
    for i in range(2):
        part = project(left_a, out_weight, 1, i * piece, piece, jnp.bfloat16, base=base)
        arrived.append(lax.ppermute(part, "head", [(0, 1), (1, 0)]))
    here = project(left_b, out_weight, 0, 0, columns, jnp.float32, away=1)
    here = project(left_a, out_weight, 0, 0, columns, jnp.float32, base=here)
    return (here + jnp.concatenate(arrived, axis=1).astype(jnp.float32)).astype(jnp.bfloat16)


def attend_general(queries, keys, values, task_slot, task_count, move, servers):
    assert task_slot.shape[0] == 1
    rows = queries.shape[0]
    width = HEADS // KVH * rows
    step = min(4, servers)
    calls = tuple(tuple(range(i, i + step)) for i in range(0, servers, step))
    (own,) = pack_queries(queries, 1, ((0,),))
    masks = active_masks(task_slot, task_count, calls, rows)
    cache = lay_cache(pack_cache(keys, values, 1, ((0,),)), masks)
    held = {0: own}
    bit = servers // 2
    while bit:
        held.update({d ^ bit: move(chunk, bit) for d, chunk in held.items()})
        bit //= 2
    partial = {}
    for which, call in enumerate(calls):
        result = attention(
            [held[d] for d in call], which, cache, masks, width, masks, 1, range(1)
        )
        for j, d in enumerate(call):
            partial[d] = [result[j]]
    bit = 1
    while bit < servers:
        for d in sorted(partial, reverse=True):
            if d & bit:
                messages = partial.pop(d)
                message = messages[0] if len(messages) == 1 else merge(messages, 1)[0]
                partial[d ^ bit].append(move(message, bit))
        bit *= 2
    return merge(partial[0], 1, False)


def on_device(queries, keys, values, out_weight, task_slot, task_count):
    servers = lax.axis_size("tok")
    heads = lax.axis_size("head")
    rows = queries.shape[0]
    group = task_slot.shape[0]
    move = functools.partial(swap, servers=servers)
    if group == 4 and servers == 16 and heads == 2:
        return attend_grouped(
            queries, keys, values, out_weight, task_slot, task_count, move
        )
    attended = attend_general(queries, keys, values, task_slot, task_count, move, servers)
    left = gather(attended, rows)
    share = project(left, out_weight, None, 0, out_weight.shape[1], jnp.bfloat16)
    return lax.psum_scatter(share, "head", scatter_dimension=1, tiled=True)


def solution(mesh):
    placed = (
        P("tok", "head"),
        P("tok", "head"),
        P("tok", "head"),
        P("head", None),
        P("head", None, None),
        P("head", None),
    )
    return jax.shard_map(
        on_device, mesh=mesh, in_specs=placed, out_specs=P("tok", "head"), check_vma=False
    )
```
